32 devices in a mesh: batch: 8 (over z, x), mlp: 4 (over y, core).
Axes of the slice: x: 2, y: 2, z: 4, core: 2. Of those that a mesh axis runs over, the one named last changes fastest.
Arguments:
- patches: bfloat16 [128, 196, 768], P(('batch', 'mlp')), may hold values from -6 to 6
- mask: int32 [128, 196], P(('batch', 'mlp')), may hold values from 0 to 1, as said below
- student_square: float32 [3, 768, 768], P(None, 'batch')
- student_qkv: float32 [768, 2304], P('batch'), may hold values from -0.21875 to 0.21875
- student_expand: float32 [768, 3072], P('batch'), may hold values from -0.21875 to 0.21875
- student_contract: float32 [3072, 768], P('batch'), may hold values from -0.109375 to 0.109375
- student_vectors: float32 [17, 768], P(None, 'batch')
- first_square: float32 [3, 768, 768], P(None, 'batch')
- first_qkv: float32 [768, 2304], P('batch')
- first_expand: float32 [768, 3072], P('batch')
- first_contract: float32 [3072, 768], P('batch')
- first_vectors: float32 [17, 768], P(None, 'batch')
- second_square: float32 [3, 768, 768], P(None, 'batch'), as said below
- second_qkv: float32 [768, 2304], P('batch'), as said below
- second_expand: float32 [768, 3072], P('batch'), as said below
- second_contract: float32 [3072, 768], P('batch'), as said below
- second_vectors: float32 [17, 768], P(None, 'batch'), as said below
- teacher_square: bfloat16 [2, 768, 768], replicated
- teacher_qkv: bfloat16 [768, 2304], replicated, may hold values from -0.21875 to 0.21875
- teacher_expand: bfloat16 [768, 3072], P(None, 'mlp'), may hold values from -0.21875 to 0.21875
- teacher_contract: bfloat16 [3072, 768], P('mlp'), may hold values from -0.109375 to 0.109375
- teacher_vectors: float32 [13, 768], replicated
Outputs:
- loss_sum: float32 [], replicated
- masked_count: float32 [], replicated
- grad_norm: float32 [], replicated
- moment_square: float32 [3, 768, 768], P(None, 'batch')
- variance_square: float32 [3, 768, 768], P(None, 'batch')
- updated_square: float32 [3, 768, 768], P(None, 'batch')
- moment_qkv: float32 [768, 2304], P('batch')
- variance_qkv: float32 [768, 2304], P('batch')
- updated_qkv: float32 [768, 2304], P('batch')
- moment_expand: float32 [768, 3072], P('batch')
- variance_expand: float32 [768, 3072], P('batch')
- updated_expand: float32 [768, 3072], P('batch')
- moment_contract: float32 [3072, 768], P('batch')
- variance_contract: float32 [3072, 768], P('batch')
- updated_contract: float32 [3072, 768], P('batch')
- moment_vectors: float32 [17, 768], P(None, 'batch')
- variance_vectors: float32 [17, 768], P(None, 'batch')
- updated_vectors: float32 [17, 768], P(None, 'batch')
The draws below stay inside these ranges and needn't reach their ends.
Inputs may be any that keep to these rules, and one draw needn't show every extreme that they name: `mask`: each image has between 40 and 80 percent of its 196 patches masked. `second_square`: positive. `second_qkv`: positive. `second_expand`: positive. `second_contract`: positive. `second_vectors`: positive.
All inputs are finite; a program needn't handle non-finite values.
Results may differ from the reference program's by a relative error of at most 0.0019.
The reference program's roundings to bfloat16 on the way count: a program that leaves them out, or rounds other values in their place, can miss the bound.
Values may be sent and summed in bfloat16 or wider, within the bound.
No kernel may reach another device: no remote copies, remote signals or barrier semaphores. Data moves between devices by JAX's collectives and lax.ppermute only.
A program may use at most 192 MiB of HBM per device.

```python
import math
import jax
import jax.numpy as jnp
from jax import lax

D = 768
HEAD_DIM = 64
FF = 3072
ROWS = 196
NS = 17
NT = 13
STEP = 10
IMAGES = 128
NPARAM = 8270592


def draw_mask(key, part):
    key_count, key_order = jax.random.split(key)
    low_count = (2 * ROWS + 4) // 5
    high_count = 4 * ROWS // 5
    count_span = high_count - low_count
    image_index = jnp.arange(IMAGES, dtype=jnp.int32)
    base_count = low_count + count_span * image_index // max(IMAGES - 1, 1)
    jitter = jax.random.randint(key_count, (IMAGES,), -(count_span // 6), count_span // 6 + 1)
    counts = jnp.clip(base_count + jitter, low_count, high_count)
    scores = jax.random.randint(key_order, (IMAGES, ROWS), 0, 1 << 20) * ROWS + jnp.arange(ROWS, dtype=jnp.int32)
    row_order = jnp.argsort(scores, axis=1)
    row_ranks = jnp.argsort(row_order, axis=1)
    return (row_ranks < counts[:, None]).astype(jnp.int32)


def square_stack(key, factors):
    full_shape = (len(factors), D, D)
    scaled = jnp.array(factors, dtype=jnp.float32)[:, None, None] * D ** (-0.5)
    values = jax.random.truncated_normal(key, -4.0, 4.0, full_shape)
    return values * scaled


def vector_rows(key, row_count, gain_rows, mask_row):
    key_noise, key_gain = jax.random.split(key)
    column = jnp.arange(D, dtype=jnp.float32) / (D - 1)
    row_index = jnp.arange(row_count)[:, None]
    ramp = 0.6 * (1.0 + 2.0 * column)
    noise = jax.random.truncated_normal(key_noise, -4.0, 4.0, (row_count, D))
    wobble = jax.random.uniform(key_gain, (row_count, D), minval=0.8, maxval=1.2)
    is_gain = jnp.zeros((row_count, 1), dtype=bool)
    for gain_row in gain_rows:
        is_gain = is_gain | (row_index == gain_row)
    spread = jnp.where(row_index == mask_row, 1.0, 0.1)
    return jnp.where(is_gain, ramp * wobble, noise * spread)


def moment_values(key, full_shape, boost, second_kind):
    gradient_size = 0.001 / math.sqrt(NPARAM) * boost
    if second_kind:
        spread = jax.random.uniform(key, full_shape, minval=0.0, maxval=math.log(4.0))
        return 0.001 * gradient_size * gradient_size * jnp.exp(spread)
    return 0.111 * gradient_size * jax.random.truncated_normal(key, -4.0, 4.0, full_shape)


def draw_student_square(key, part):
    return square_stack(key, [1.0, 3.0, 1.0])


def draw_teacher_square(key, part):
    return square_stack(key, [1.0, 3.0]).astype(jnp.bfloat16)


def draw_student_vectors(key, part):
    return vector_rows(key, NS, (2, 7, 14), 1)


def draw_teacher_vectors(key, part):
    return vector_rows(key, NT, (1, 6), -1)


def draw_first_square(key, part):
    return moment_values(key, (3, D, D), 1.0, False)


def draw_first_qkv(key, part):
    return moment_values(key, (D, 3 * D), 1.0, False)


def draw_first_expand(key, part):
    return moment_values(key, (D, FF), 1.0, False)


def draw_first_contract(key, part):
    return moment_values(key, (FF, D), 1.0, False)


def draw_first_vectors(key, part):
    return moment_values(key, (NS, D), 4.0, False)


def draw_second_square(key, part):
    return moment_values(key, (3, D, D), 1.0, True)


def draw_second_qkv(key, part):
    return moment_values(key, (D, 3 * D), 1.0, True)


def draw_second_expand(key, part):
    return moment_values(key, (D, FF), 1.0, True)


def draw_second_contract(key, part):
    return moment_values(key, (FF, D), 1.0, True)


def draw_second_vectors(key, part):
    return moment_values(key, (NS, D), 4.0, True)


def block_levels(own_key, dims, cuts, low, largest):
    level = 1.0
    for dim, shards_of in cuts:
        heights = jax.random.uniform(jax.random.fold_in(jax.random.fold_in(own_key, 6), dim), (shards_of,), jnp.float32, low / len(cuts), largest / len(cuts))
        level = level * jnp.repeat(jnp.exp(heights), dims[dim] // shards_of).reshape((-1,) + (1,) * (len(dims) - 1 - dim))
    return level


def bell_draw(key, shape, scale, most, pieces=(), held_as=jnp.bfloat16):
    drawn = jax.random.normal(key, shape, jnp.float32) * scale
    if len(pieces) > 0:
        drawn = block_levels(key, shape, pieces, -0.22, 0.18) * drawn
    return jnp.clip(drawn, min=-most, max=most).astype(held_as)


def setup_inputs(seed: int = 0) -> dict:
    key_list = jax.random.split(jax.random.key(seed), 23)
    return {
        "patches": bell_draw(key_list[0], (IMAGES, ROWS, D), 1.0, 6.0, ((0, 32),)),
        "mask": draw_mask(jax.random.fold_in(key_list[22], 71), 0),
        "student_square": draw_student_square(jax.random.fold_in(key_list[22], 71), 0),
        "student_qkv": bell_draw(key_list[3], (D, 3 * D), D ** -0.5, 0.21875, ((0, 8),), jnp.float32),
        "student_expand": bell_draw(key_list[4], (D, FF), D ** -0.5, 0.21875, ((0, 8),), jnp.float32),
        "student_contract": bell_draw(key_list[5], (FF, D), FF ** -0.5, 0.109375, ((0, 8),), jnp.float32),
        "student_vectors": draw_student_vectors(jax.random.fold_in(key_list[22], 71), 0),
        "first_square": draw_first_square(jax.random.fold_in(key_list[22], 71), 0),
        "first_qkv": draw_first_qkv(jax.random.fold_in(key_list[22], 71), 0),
        "first_expand": draw_first_expand(jax.random.fold_in(key_list[22], 71), 0),
        "first_contract": draw_first_contract(jax.random.fold_in(key_list[22], 71), 0),
        "first_vectors": draw_first_vectors(jax.random.fold_in(key_list[22], 71), 0),
        "second_square": draw_second_square(jax.random.fold_in(key_list[22], 71), 0),
        "second_qkv": draw_second_qkv(jax.random.fold_in(key_list[22], 71), 0),
        "second_expand": draw_second_expand(jax.random.fold_in(key_list[22], 71), 0),
        "second_contract": draw_second_contract(jax.random.fold_in(key_list[22], 71), 0),
        "second_vectors": draw_second_vectors(jax.random.fold_in(key_list[22], 71), 0),
        "teacher_square": draw_teacher_square(jax.random.fold_in(key_list[22], 71), 0),
        "teacher_qkv": bell_draw(key_list[18], (D, 3 * D), D ** -0.5, 0.21875),
        "teacher_expand": bell_draw(key_list[19], (D, FF), D ** -0.5, 0.21875, ((1, 4),)),
        "teacher_contract": bell_draw(key_list[20], (FF, D), FF ** -0.5, 0.109375, ((0, 4),)),
        "teacher_vectors": draw_teacher_vectors(jax.random.fold_in(key_list[22], 71), 0),
    }


highest = lax.Precision.HIGHEST
norm_eps = 1e-06
inst_eps = 1e-05
clip_bound = 0.001
rate_matrix = 0.05
rate_vector = 0.5
decay_matrix = 0.05
beta_first = 0.9
beta_second = 0.999
adam_eps = 1e-08
group_images = 16

@jax.custom_vjp
def low(v):
    return lax.optimization_barrier(v.astype(jnp.bfloat16)).astype(jnp.float32)

@jax.custom_vjp
def low_back(v):
    return v

def low_keep(v):
    return (low(v), None)

def low_pass(kept, grad):
    return (grad,)

def back_keep(v):
    return (v, None)

def back_low(kept, grad):
    return (low(grad),)
low.defvjp(low_keep, low_pass)
low_back.defvjp(back_keep, back_low)

def product(left, right):
    return jnp.dot(left, right, precision=highest, preferred_element_type=jnp.float32)

def norm_rows(values, gain, shift):
    centred = values - lax.optimization_barrier(jnp.mean(values, axis=-1, keepdims=True))
    variance = lax.optimization_barrier(jnp.mean(centred * centred, axis=-1, keepdims=True))
    return centred * lax.rsqrt(variance + norm_eps) * gain + shift

def inst_norm(values):
    centred = values - lax.optimization_barrier(jnp.mean(values, axis=1, keepdims=True))
    variance = lax.optimization_barrier(jnp.mean(centred * centred, axis=1, keepdims=True))
    return centred * lax.rsqrt(variance + inst_eps)

def split_heads(values):
    return values.reshape(values.shape[0], values.shape[1], -1, HEAD_DIM)

def attend(queries, key_rows, value_rows):
    scores = jnp.einsum('gqhd,gkhd->ghqk', split_heads(queries), split_heads(key_rows), precision=highest) * HEAD_DIM ** (-0.5)
    scores = low_back(scores)
    probs = low(jax.nn.softmax(scores, axis=-1))
    mixed = jnp.einsum('ghqk,gkhd->gqhd', probs, split_heads(value_rows), precision=highest)
    return mixed.reshape(queries.shape)

def joint_bias(query_bias, value_bias):
    return jnp.concatenate([query_bias, jnp.zeros_like(query_bias), value_bias])

def gelu_exact(values):
    return jax.nn.gelu(values, approximate=False)

def teacher_group(pixels, teacher):
    square, joint, expand, contract, vectors = teacher
    embed = product(pixels, square[0]) + vectors[0]
    normed = low(norm_rows(embed, vectors[1], vectors[2]))
    mixed = product(normed, joint) + joint_bias(vectors[3], vectors[4])
    attended = low(attend(low(mixed[..., :D]), low(mixed[..., D:2 * D]), low(mixed[..., 2 * D:])))
    middle = embed + product(attended, square[1]) + vectors[5]
    normed_two = low(norm_rows(middle, vectors[6], vectors[7]))
    hidden = low(gelu_exact(product(normed_two, expand) + vectors[8:12].reshape(-1)))
    output = product(hidden, contract) + vectors[12]
    return 0.5 * (inst_norm(middle) + inst_norm(output))

def student_group(params, pixels, marks, targets):
    square, joint, expand, contract, vectors = [low(item) for item in params]
    embed = low_back(product(pixels, square[0]) + vectors[0])
    start = jnp.where(marks[..., None] > 0, vectors[1], embed)
    normed = low(norm_rows(start, vectors[2], vectors[3]))
    mixed = low_back(product(normed, joint) + joint_bias(vectors[4], vectors[5]))
    attended = low(low_back(attend(low(mixed[..., :D]), low(mixed[..., D:2 * D]), low(mixed[..., 2 * D:]))))
    middle = start + low_back(product(attended, square[1]) + vectors[6])
    normed_two = low(norm_rows(middle, vectors[7], vectors[8]))
    pre_act = low_back(product(normed_two, expand) + vectors[9:13].reshape(-1))
    hidden = low(gelu_exact(pre_act))
    final = middle + low_back(product(hidden, contract) + vectors[13])
    normed_three = low(norm_rows(final, vectors[14], vectors[15]))
    predicted = low_back(product(normed_three, square[2]) + vectors[16])
    error = predicted - targets
    return jnp.sum(marks[..., None] * error * error)

def adam_update(master, first, second, gradient, step_rate, weight_decay):
    moment = beta_first * first + (1.0 - beta_first) * gradient
    variance = beta_second * second + (1.0 - beta_second) * gradient * gradient
    corrected = moment / (1.0 - beta_first ** STEP)
    scaled = variance / (1.0 - beta_second ** STEP)
    updated = master - step_rate * (corrected / (jnp.sqrt(scaled) + adam_eps) + weight_decay * master)
    return (moment, variance, updated)

def reference(patches, mask, student_square, student_qkv, student_expand, student_contract, student_vectors, first_square, first_qkv, first_expand, first_contract, first_vectors, second_square, second_qkv, second_expand, second_contract, second_vectors, teacher_square, teacher_qkv, teacher_expand, teacher_contract, teacher_vectors):
    groups = IMAGES // group_images
    pixels = patches.astype(jnp.float32).reshape(groups, group_images, ROWS, D)
    marks = mask.astype(jnp.float32).reshape(groups, group_images, ROWS)
    teacher = (teacher_square.astype(jnp.float32), teacher_qkv.astype(jnp.float32), teacher_expand.astype(jnp.float32), teacher_contract.astype(jnp.float32), teacher_vectors)

    def one_group(block):
        return teacher_group(block, teacher)
    targets = lax.map(one_group, pixels)
    masked_count = jnp.sum(marks)
    masters = (student_square, student_qkv, student_expand, student_contract, student_vectors)
    student_step = jax.checkpoint(student_group)

    def total_loss(params):

        def accumulate(carry, item):
            return (carry + student_step(params, item[0], item[1], item[2]), None)
        loss_sum, _ = lax.scan(accumulate, jnp.zeros((), jnp.float32), (pixels, marks, targets))
        return (loss_sum / (masked_count * D), loss_sum)
    _, back_fn, loss_sum = jax.vjp(total_loss, masters, has_aux=True)
    grads = back_fn(jnp.ones((), jnp.float32))[0]
    squares = jnp.sum(grads[0] * grads[0]) + jnp.sum(grads[1] * grads[1]) + jnp.sum(grads[2] * grads[2])
    squares = squares + jnp.sum(grads[3] * grads[3]) + jnp.sum(grads[4] * grads[4])
    grad_norm = jnp.sqrt(squares)
    factor = clip_bound / jnp.maximum(grad_norm, clip_bound)
    moment_square, variance_square, updated_square = adam_update(student_square, first_square, second_square, grads[0] * factor, rate_matrix, decay_matrix)
    moment_qkv, variance_qkv, updated_qkv = adam_update(student_qkv, first_qkv, second_qkv, grads[1] * factor, rate_matrix, decay_matrix)
    moment_expand, variance_expand, updated_expand = adam_update(student_expand, first_expand, second_expand, grads[2] * factor, rate_matrix, decay_matrix)
    moment_contract, variance_contract, updated_contract = adam_update(student_contract, first_contract, second_contract, grads[3] * factor, rate_matrix, decay_matrix)
    moment_vectors, variance_vectors, updated_vectors = adam_update(student_vectors, first_vectors, second_vectors, grads[4] * factor, rate_vector, 0.0)
    return (loss_sum, masked_count, grad_norm, moment_square, variance_square, updated_square, moment_qkv, variance_qkv, updated_qkv, moment_expand, variance_expand, updated_expand, moment_contract, variance_contract, updated_contract, moment_vectors, variance_vectors, updated_vectors)
```

```python
import functools

import jax
import jax.numpy as jnp
from jax import lax
from jax.experimental import pallas as pl
from jax.experimental.pallas import tpu as pltpu
from jax.sharding import PartitionSpec as P

D = 768
HEAD_DIM = 64
PAIR = 2 * HEAD_DIM
STEP = 10


norm_eps = 1e-06
inst_eps = 1e-05
clip_bound = 0.001
rate_matrix = 0.05
rate_vector = 0.5
decay_matrix = 0.05
beta_first = 0.9
beta_second = 0.999
adam_eps = 1e-08
f32 = jnp.float32
bf16 = jnp.bfloat16


def mm(left, right):
    return lax.dot_general(left, right, (((1,), (0,)), ((), ())), preferred_element_type=f32)


def mm_nt(left, right):
    return lax.dot_general(left, right, (((1,), (1,)), ((), ())), preferred_element_type=f32)


def mm_tn(left, right):
    return lax.dot_general(left, right, (((0,), (0,)), ((), ())), preferred_element_type=f32)


def normed_rows(values):
    centred = values - jnp.mean(values, axis=-1, keepdims=True)
    variance = jnp.mean(centred * centred, axis=-1, keepdims=True)
    scale = lax.rsqrt(variance + norm_eps)
    return centred * scale, scale


def norm_back(xhat, scale, gain, grads):
    scaled = grads * gain
    mean_one = jnp.mean(scaled, axis=-1, keepdims=True)
    mean_two = jnp.mean(scaled * xhat, axis=-1, keepdims=True)
    back = scale * (scaled - mean_one - xhat * mean_two)
    return back, total_rows(grads * xhat), total_rows(grads)


def copy_all(copies):
    for copy in copies:
        copy.start()
    for copy in copies:
        copy.wait()


def piece_copies(table_ref, semaphores, pieces):
    core = table_ref[0]
    copies = []
    for ref, (unit, height, row, near), lanes, target in pieces:
        width = lanes[1] - lanes[0]
        column = pl.multiple_of((core if near else 1 - core) * width, 128)
        for block in range(ref.shape[0]):
            place = 0 if unit == 0 else pl.multiple_of(table_ref[row + block] * unit, 16)
            copies.append(
                pltpu.make_async_copy(
                    ref.at[block, :, pl.ds(lanes[0], width)],
                    target.at[pl.ds(place, height), pl.ds(column, width)],
                    semaphores.at[len(copies)],
                )
            )
    return copies


def total_rows(values):
    return jnp.sum(values, axis=0, keepdims=True)


def head_masks(rows):
    lane = lax.broadcasted_iota(jnp.int32, (rows, PAIR), 1)
    return lane < HEAD_DIM


def stacked(values, low):
    zero = jnp.zeros_like(values)
    return jnp.concatenate([jnp.where(low, values, zero), jnp.where(low, zero, values)], axis=0)


def pair_probs(stack, keys, real_rows):
    scores = mm_nt(stack, keys)
    column = lax.broadcasted_iota(jnp.int32, scores.shape, 1)
    scores = jnp.where(column < real_rows, scores, -1e30)
    shifted = jnp.exp(scores - jnp.max(scores, axis=-1, keepdims=True))
    return shifted / jnp.sum(shifted, axis=-1, keepdims=True)


def attend_block(is_student, real_rows, pad_rows, x_ref, marks_ref, weights, vec_ref, outs):
    w0_ref, wj_ref, w1_ref = weights
    start_ref, mid_ref, joint_ref, act_ref = outs
    at = (lambda student, teacher: student if is_student else teacher)
    vec = lambda row: vec_ref[row : row + 1, :]
    block = x_ref.shape[0]
    start = mm(x_ref[...], w0_ref[...]) + vec(0)
    if is_student:
        start = jnp.where(marks_ref[:, :1] > 0, vec(1), start)
    start_ref[...] = start
    xhat, _ = normed_rows(start)
    normed = (xhat * vec(at(2, 1)) + vec(at(3, 2))).astype(bf16)
    if is_student:
        act_ref[:, D : 2 * D] = normed
        act_ref[:, 2 * D :] = x_ref[...]
    biases = (vec(at(4, 3)), None, vec(at(5, 4)))
    for part in range(3):
        cols = slice(part * D, (part + 1) * D)
        mixed = mm(normed, wj_ref[:, cols])
        if biases[part] is not None:
            mixed = mixed + biases[part]
        joint_ref[:, cols] = mixed.astype(bf16)
    low = head_masks(pad_rows)

    def one_pair(step, carry):
        image = step // (D // PAIR)
        col = pl.multiple_of((step % (D // PAIR)) * PAIR, PAIR)
        rows = pl.ds(pl.multiple_of(image * pad_rows, 16), pad_rows)
        queries = joint_ref[rows, pl.ds(col, PAIR)] * HEAD_DIM ** (-0.5)
        keys = joint_ref[rows, pl.ds(col + D, PAIR)]
        values = joint_ref[rows, pl.ds(col + 2 * D, PAIR)]
        probs = pair_probs(stacked(queries.astype(bf16), low), keys, real_rows).astype(bf16)
        mixed = mm(probs, values)
        act_ref[rows, pl.ds(col, PAIR)] = jnp.where(
            low, mixed[:pad_rows], mixed[pad_rows:]
        ).astype(bf16)
        return carry

    lax.fori_loop(0, (block // pad_rows) * (D // PAIR), one_pair, 0)
    attended = act_ref[:, :D]
    mid_ref[...] = start_ref[...] + mm(attended, w1_ref[...]) + vec(at(6, 5))


def clear_at_first(*refs):
    @pl.when(pl.program_id(0) == 0)
    def _():
        for ref in refs:
            ref[...] = jnp.zeros_like(ref)


def place_at_first(table_ref, semaphores, pieces):
    @pl.when(pl.program_id(0) == 0)
    def _():
        copy_all(piece_copies(table_ref, semaphores, pieces))


def attend_teacher_kernel(real_rows, pad_rows, *refs):
    (x_ref, w0_ref, wj_ref, w1_ref, vec_ref, mid_ref, joint_ref, att_ref) = refs
    attend_block(
        False,
        real_rows,
        pad_rows,
        x_ref,
        None,
        (w0_ref, wj_ref, w1_ref),
        vec_ref,
        (mid_ref, mid_ref, joint_ref, att_ref),
    )


def attend_student_kernel(real_rows, pad_rows, metas, joint_metas, *refs):
    (table_ref, x_ref, marks_ref, vec_ref) = refs[:4]
    count = len(metas)
    piece_refs, joint_refs = refs[4 : 4 + count], refs[4 + count : 4 + 2 * count]
    (start_ref, mid_ref, joint_ref, act_ref) = refs[4 + 2 * count : 8 + 2 * count]
    (w0_ref, w1_ref, wj_ref, semaphores) = refs[8 + 2 * count :]
    pieces = section(piece_refs, metas, SQUARE_LANES[0], w0_ref)
    pieces += section(joint_refs, joint_metas, JOINT_LANES, wj_ref)
    pieces += section(piece_refs, metas, SQUARE_LANES[1], w1_ref)
    place_at_first(table_ref, semaphores, pieces)
    attend_block(
        True,
        real_rows,
        pad_rows,
        x_ref,
        marks_ref,
        (w0_ref, wj_ref, w1_ref),
        vec_ref,
        (start_ref, mid_ref, joint_ref, act_ref),
    )


def gelu_half(values):
    return 0.5 * (1.0 + lax.erf(values * 0.7071067811865476))


def teacher_ffn_kernel(real_rows, pad_rows, is_last, *refs):
    mid_ref, bias_ref, vec_ref = refs[:3]
    parts = bias_ref.shape[0]
    rest = refs[3 + parts :]
    mid = mid_ref[...]
    xhat, _ = normed_rows(mid)
    normed = (xhat * vec_ref[6:7, :] + vec_ref[7:8, :]).astype(bf16)
    total = rest[0][...] if is_last else None
    for part, both_ref in enumerate(refs[3 : 3 + parts]):
        pre = mm(normed, both_ref[:, :D]) + bias_ref[part : part + 1, :]
        hidden = (pre * gelu_half(pre)).astype(bf16)
        piece = mm(hidden, both_ref[:, D:])
        total = piece if total is None else total + piece
    out_ref = rest[-1]
    if not is_last:
        out_ref[...] = total
        return
    total = total + vec_ref[12:13, :]
    valid = lax.broadcasted_iota(jnp.int32, (pad_rows, D), 0) < real_rows
    for image in range(mid_ref.shape[0] // pad_rows):
        rows = slice(image * pad_rows, (image + 1) * pad_rows)
        result = None
        for values in (mid[rows], total[rows]):
            mean = total_rows(jnp.where(valid, values, 0.0)) / real_rows
            centred = values - mean
            variance = total_rows(jnp.where(valid, centred * centred, 0.0)) / real_rows
            normal = centred * lax.rsqrt(variance + inst_eps)
            result = normal if result is None else result + normal
        out_ref[rows, :] = 0.5 * result


def student_ffn_kernel(square_metas, expand_metas, contract_metas, *refs):
    (table_ref, scale_ref, mid_ref, target_ref, marks_ref, vec_ref) = refs[:6]
    counts = (len(square_metas), len(expand_metas), len(contract_metas))
    square_refs = refs[6 : 6 + counts[0]]
    expand_refs = refs[6 + counts[0] : 6 + counts[0] + counts[1]]
    contract_refs = refs[6 + counts[0] + counts[1] : 6 + sum(counts)]
    (keep_ref, one_ref, two_ref, dmid_ref, sum_ref) = refs[6 + sum(counts) : 11 + sum(counts)]
    (we_ref, wc_ref, wh_ref, slope_ref, half_ref, semaphores) = refs[11 + sum(counts) :]
    pieces = section(expand_refs, expand_metas, (0, 2 * D), we_ref)
    pieces += section(contract_refs, contract_metas, (0, D // 2), wc_ref)
    pieces += section(square_refs, square_metas, SQUARE_LANES[2], wh_ref)
    clear_at_first(sum_ref)
    place_at_first(table_ref, semaphores, pieces)
    core = table_ref[0]

    def add(row, values):
        sum_ref[pl.ds(row, 1), :] += values

    def add_grad(row, grads):
        add(row, total_rows(grads.astype(f32)))

    def halves(keep_cols, send_ref, send_cols, grads):
        half_ref[...] = grads
        width = D // 2
        keep_ref[:, keep_cols : keep_cols + width] = half_ref[
            :, pl.ds(pl.multiple_of(core * width, 128), width)
        ]
        send_ref[:, send_cols : send_cols + width] = half_ref[
            :, pl.ds(pl.multiple_of((1 - core) * width, 128), width)
        ]

    vec = lambda row: vec_ref[row : row + 1, :]
    mid = mid_ref[...]
    xhat2, scale2 = normed_rows(mid)
    n2 = (xhat2 * vec(7) + vec(8)).astype(bf16)
    one_ref[:, D : 2 * D] = n2
    total = None
    for part in range(4):
        cols = slice(part * D, (part + 1) * D)
        pre = mm(n2, we_ref[:, cols]) + vec(9 + part)
        half = gelu_half(pre)
        slope_ref[:, cols] = half + pre * (jnp.exp(-0.5 * pre * pre) * 0.3989422804014327)
        hidden = (pre * half).astype(bf16)
        two_ref[:, cols] = hidden
        piece = mm(hidden, wc_ref[cols, :])
        total = piece if total is None else total + piece
    final = mid + total + vec(13)
    xhat3, scale3 = normed_rows(final)
    n3 = (xhat3 * vec(14) + vec(15)).astype(bf16)
    one_ref[:, :D] = n3
    error = marks_ref[:, :1] * (mm(n3, wh_ref[...]) + vec(16) - target_ref[...])
    add(0, total_rows(error * error))
    dpred = (error * scale_ref[0]).astype(bf16)
    halves(2 * D, one_ref, 4 * D, dpred)
    add_grad(1, dpred)
    dfinal, gain3, shift3 = norm_back(xhat3, scale3, vec(14), mm_nt(dpred, wh_ref[...]))
    add(2, gain3)
    add(3, shift3)
    dbranch = dfinal.astype(bf16)
    halves(2 * D + D // 2, two_ref, 4 * D, dbranch)
    add_grad(4, dbranch)
    dn2 = None
    for side in range(2):
        for part in range(2):
            chunk = 2 * (core ^ side) + part
            cols = pl.ds(pl.multiple_of(chunk * D, 128), D)
            dpre = (mm_nt(dbranch, wc_ref[cols, :]) * slope_ref[:, cols]).astype(bf16)
            if side == 0:
                keep_ref[:, part * D : (part + 1) * D] = dpre
            else:
                one_ref[:, (2 + part) * D : (3 + part) * D] = dpre
            add_grad(5 + chunk, dpre)
            piece = mm_nt(dpre, we_ref[:, cols])
            dn2 = piece if dn2 is None else dn2 + piece
    dmid, gain2, shift2 = norm_back(xhat2, scale2, vec(7), dn2)
    add(9, gain2)
    add(10, shift2)
    dmid = dfinal + dmid
    dmid_ref[...] = dmid
    add(11, total_rows(dmid.astype(bf16).astype(f32)))


def attend_back_kernel(real_rows, pad_rows, metas, joint_metas, *refs):
    (table_ref, dmid_ref, joint_ref, start_ref, marks_ref, vec_ref) = refs[:6]
    count = len(metas)
    piece_refs, joint_refs = refs[6 : 6 + count], refs[6 + count : 6 + 2 * count]
    (keep_ref, send_ref, sum_ref) = refs[6 + 2 * count : 9 + 2 * count]
    (w1_ref, wj_ref, grad_ref, djoint_ref, half_ref, semaphores) = refs[9 + 2 * count :]
    pieces = section(piece_refs, metas, SQUARE_LANES[1], w1_ref)
    pieces += section(joint_refs, joint_metas, JOINT_LANES, wj_ref)
    clear_at_first(sum_ref)
    place_at_first(table_ref, semaphores, pieces)
    core = table_ref[0]

    def add(row, values):
        sum_ref[row : row + 1, :] += values

    def halves(column, source_ref, width):
        keep_ref[:, column : column + width] = source_ref[
            :, pl.ds(pl.multiple_of(core * width, 128), width)
        ]
        send_ref[:, column : column + width] = source_ref[
            :, pl.ds(pl.multiple_of((1 - core) * width, 128), width)
        ]

    vec = lambda row: vec_ref[row : row + 1, :]
    block = dmid_ref.shape[0]
    datt = dmid_ref[...].astype(bf16)
    half_ref[...] = datt
    halves(0, half_ref, D // 2)
    grad_ref[...] = mm_nt(datt, w1_ref[...]).astype(bf16)
    low = head_masks(pad_rows)

    def one_pair(step, carry):
        image = step // (D // PAIR)
        col = pl.multiple_of((step % (D // PAIR)) * PAIR, PAIR)
        rows = pl.ds(pl.multiple_of(image * pad_rows, 16), pad_rows)
        queries = joint_ref[rows, pl.ds(col, PAIR)] * HEAD_DIM ** (-0.5)
        keys = joint_ref[rows, pl.ds(col + D, PAIR)]
        values = joint_ref[rows, pl.ds(col + 2 * D, PAIR)]
        stack = stacked(queries.astype(bf16), low)
        dstack = stacked(grad_ref[rows, pl.ds(col, PAIR)], low)
        probs = pair_probs(stack, keys, real_rows)
        dprobs = mm_nt(dstack, values)
        dvalues = mm_tn(probs.astype(bf16), dstack)
        weighted = probs * dprobs
        dscores = (weighted - probs * jnp.sum(weighted, axis=-1, keepdims=True)).astype(bf16)
        both = mm(dscores, keys) * HEAD_DIM ** (-0.5)
        dqueries = jnp.where(low, both[:pad_rows], both[pad_rows:])
        dkeys = mm_tn(dscores, stack)
        djoint_ref[rows, pl.ds(col, PAIR)] = dqueries.astype(bf16)
        djoint_ref[rows, pl.ds(col + D, PAIR)] = dkeys.astype(bf16)
        djoint_ref[rows, pl.ds(col + 2 * D, PAIR)] = dvalues.astype(bf16)
        return carry

    lax.fori_loop(0, (block // pad_rows) * (D // PAIR), one_pair, 0)
    halves(D // 2, djoint_ref, 3 * D // 2)
    dnormed = None
    for part in range(3):
        cols = slice(part * D, (part + 1) * D)
        grads = djoint_ref[:, cols]
        if part != 1:
            add(part // 2, total_rows(grads.astype(f32)))
        piece = mm_nt(grads, wj_ref[:, cols])
        dnormed = piece if dnormed is None else dnormed + piece
    xhat, scale = normed_rows(start_ref[...])
    dstart, gain, shift = norm_back(xhat, scale, vec(2), dnormed)
    add(2, gain)
    add(3, shift)
    dstart = dstart + dmid_ref[...]
    masked = marks_ref[:, :1] > 0
    add(4, total_rows(jnp.where(masked, dstart, 0.0)))
    dembed = jnp.where(masked, 0.0, dstart).astype(bf16)
    half_ref[...] = dembed
    halves(2 * D, half_ref, D // 2)
    add(5, total_rows(dembed.astype(f32)))


def store_members(out_ref, table_ref, result, members, relative_y):
    rows = result.shape[0] // members
    for member in range(members):
        place = member ^ table_ref[2]
        for side in range(2):
            first = member * rows + side * (rows // 2)
            target = (side ^ table_ref[1]) if relative_y else side
            out_ref[place, target] = result[first : first + rows // 2]


def weight_grad_kernel(members, relative, relative_y, is_new, *refs):
    (table_ref, a_ref, a_peer_ref, b_ref, b_peer_ref, out_ref, top_ref, turned_ref) = refs

    @pl.when(is_new(pl.program_id(0)))
    def _():
        turned_ref[0] = a_ref[...].T
        turned_ref[1] = a_peer_ref[...].T

    result = mm(turned_ref[0], b_ref[...]) + mm(turned_ref[1], b_peer_ref[...])
    top_ref[...] = jnp.broadcast_to(jnp.max(jnp.abs(result), axis=0, keepdims=True), top_ref.shape)
    if relative:
        store_members(out_ref, table_ref, result, members, relative_y)
    else:
        out_ref[...] = result


def contract_grad_kernel(relative, *refs):
    (table_ref, d_ref, d_peer_ref, h_ref, h_peer_ref, out_ref, top_ref, turned_ref) = refs
    clear_at_first(top_ref)

    @pl.when(pl.program_id(0) == 0)
    def _():
        turned_ref[0] = d_ref[...].T
        turned_ref[1] = d_peer_ref[...].T

    result = (mm(turned_ref[0], h_ref[...]) + mm(turned_ref[1], h_peer_ref[...])).T
    top_ref[...] = jnp.maximum(top_ref[...], jnp.max(jnp.abs(result), axis=0, keepdims=True))
    if relative:
        rows = result.shape[0] // 2
        for side in range(2):
            out_ref[0, side ^ table_ref[1]] = result[side * rows : (side + 1) * rows]
    else:
        out_ref[...] = result


SQUARE_LANES = tuple((i * D // 2, (i + 1) * D // 2) for i in range(3))
JOINT_LANES = (0, 3 * D // 2)


def section(refs, metas, lanes, target):
    return [(ref, meta, lanes, target) for ref, meta in zip(refs, metas)]


def blocks_of(group):
    return sum(array.shape[0] for array in group[0])


def whole_spec(shape):
    return pl.BlockSpec(shape, lambda *_: (0,) * len(shape), pipeline_mode=pl.Buffered(1))


def row_spec(block, width):
    return pl.BlockSpec((block, width), lambda i, *_: (i, 0))


COSTS = {'attend_teacher': 13.0, 'attend_student': 29.0, 'teacher_ffn': 9.0, 'student_ffn': 35.0, 'attend_back': 36.0, 'grad_expand': 15.0, 'grad_contract': 13.0, 'grad_out_joint': 9.0, 'grad_joint_embed': 11.0}
smem_spec = pl.BlockSpec(memory_space=pltpu.SMEM)
any_spec = pl.BlockSpec(memory_space=pl.ANY)


def call(kernel, name, grid, ins, outs, scratch, flops, moved, prefetch=0):
    return pl.pallas_call(
        kernel,
        grid_spec=pltpu.PrefetchScalarGridSpec(
            num_scalar_prefetch=prefetch,
            grid=grid,
            in_specs=[spec for _, spec in ins[prefetch:]],
            out_specs=[spec for _, spec in outs],
            scratch_shapes=scratch,
        ),
        out_shape=[jax.ShapeDtypeStruct(*item) for item, _ in outs],
        compiler_params=pltpu.CompilerParams(vmem_limit_bytes=60 << 20),
        cost_estimate=pl.CostEstimate(
            flops=int(COSTS[name] * 1.15e9), transcendentals=0, bytes_accessed=1
        ),
        name=name,
    )(*[item for item, _ in ins])


def attend_teacher(real_rows, pad_rows, images, first, x, w0, wj, w1, vectors):
    rows = block = images * pad_rows
    wholes = [(item, whole_spec(item.shape)) for item in (w0, wj, w1, vectors)]
    return call(
        functools.partial(attend_teacher_kernel, real_rows, pad_rows),
        "attend_teacher",
        (rows // block,),
        [(x, pl.BlockSpec((block, D), lambda i, *_: (first, 0)))] + wholes,
        [(((rows, D), f32), row_spec(block, D))],
        [pltpu.VMEM((block, 3 * D), bf16), pltpu.VMEM((block, D), bf16)],
        14 * rows * D * D,
        20e6,
    )[0]


def attend_student(real_rows, pad_rows, images, table, x, marks, vectors, square, joint):
    rows, block = x.shape[0], images * pad_rows
    arrays, metas = square[0] + joint[0], (square[1], joint[1])
    outs = [(D, f32), (D, f32), (3 * D, bf16), (3 * D, bf16)]
    return call(
        functools.partial(attend_student_kernel, real_rows, pad_rows, *metas),
        "attend_student",
        (rows // block,),
        [
            (table, smem_spec),
            (x, row_spec(block, D)),
            (marks, row_spec(block, 128)),
            (vectors, whole_spec(vectors.shape)),
        ]
        + [(array, any_spec) for array in arrays],
        [(((rows, width), kind), row_spec(block, width)) for width, kind in outs],
        [
            pltpu.VMEM((D, D), bf16),
            pltpu.VMEM((D, D), bf16),
            pltpu.VMEM((D, 3 * D), bf16),
            pltpu.SemaphoreType.DMA((2 * blocks_of(square) + blocks_of(joint),)),
        ],
        14 * rows * D * D,
        25e6,
    )


def teacher_ffn(real_rows, pad_rows, images, mid, weights, biases, vectors, sums):
    rows, block = mid.shape[0], images * pad_rows
    items = [biases, vectors, *weights]
    wholes = [(item, whole_spec(item.shape)) for item in items]
    last = [] if sums is None else [(sums, row_spec(block, D))]
    return call(
        functools.partial(teacher_ffn_kernel, real_rows, pad_rows, sums is not None),
        "teacher_ffn",
        (rows // block,),
        [(mid, row_spec(block, D))] + wholes + last,
        [(((rows, D), f32), row_spec(block, D))],
        [],
        16 * rows * D * D,
        15e6,
    )[0]


def student_ffn(pad_rows, images, table, scale, mid, targets, marks, vectors, square, expand, contract):
    rows, block = mid.shape[0], images * pad_rows
    outs = [(3 * D, bf16), (9 * D // 2, bf16), (9 * D // 2, bf16), (D, f32)]
    return call(
        functools.partial(student_ffn_kernel, square[1], expand[1], contract[1]),
        "student_ffn",
        (rows // block,),
        [
            (table, smem_spec),
            (scale, smem_spec),
            (mid, row_spec(block, D)),
            (targets, row_spec(block, D)),
            (marks, row_spec(block, 128)),
            (vectors, whole_spec(vectors.shape)),
        ]
        + [(array, any_spec) for array in (*square[0], *expand[0], *contract[0])],
        [(((rows, width), kind), row_spec(block, width)) for width, kind in outs]
        + [(((16, D), f32), whole_spec((16, D)))],
        [
            pltpu.VMEM((D, 4 * D), bf16),
            pltpu.VMEM((4 * D, D), bf16),
            pltpu.VMEM((D, D), bf16),
            pltpu.VMEM((block, 4 * D), f32),
            pltpu.VMEM((block, D), bf16),
            pltpu.SemaphoreType.DMA((blocks_of(square) + blocks_of(expand) + blocks_of(contract),)),
        ],
        36 * rows * D * D,
        40e6,
    )


def attend_back(
    real_rows, pad_rows, images, table, dmid, joint, start, marks, vectors, square, qkv
):
    rows, block = dmid.shape[0], images * pad_rows
    arrays, metas = square[0] + qkv[0], (square[1], qkv[1])
    return call(
        functools.partial(attend_back_kernel, real_rows, pad_rows, *metas),
        "attend_back",
        (rows // block,),
        [
            (table, smem_spec),
            (dmid, row_spec(block, D)),
            (joint, row_spec(block, 3 * D)),
            (start, row_spec(block, D)),
            (marks, row_spec(block, 128)),
            (vectors, whole_spec(vectors.shape)),
        ]
        + [(array, any_spec) for array in arrays],
        [(((rows, 5 * D // 2), bf16), row_spec(block, 5 * D // 2))] * 2
        + [(((16, D), f32), whole_spec((16, D)))],
        [
            pltpu.VMEM((D, D), bf16),
            pltpu.VMEM((D, 3 * D), bf16),
            pltpu.VMEM((block, D), bf16),
            pltpu.VMEM((block, 3 * D), bf16),
            pltpu.VMEM((block, D), bf16),
            pltpu.SemaphoreType.DMA((blocks_of(square) + blocks_of(qkv),)),
        ],
        20 * rows * D * D,
        25e6,
    )


def relative_rows(grads, members, relative_y, place, own_y):
    grads = grads.reshape(members, 2, -1, grads.shape[1])
    grads = jnp.take(grads, jnp.arange(members) ^ place, axis=0)
    if relative_y:
        grads = jnp.take(grads, jnp.arange(2) ^ own_y, axis=1)
    return grads


def weight_grad(name, table, members, relative_y, steps, own_a, peer_a, own_b, peer_b, is_new):
    rows = own_a[0].shape[0]
    wide = D // 2
    relative = (D // members) % 16 == 0

    def spec(item):
        return (item[0], pl.BlockSpec((rows, item[1]), lambda j, _: (0, item[2](j))))

    if relative:
        shape = (members, 2, D // members // 2)
        out = ((shape + (steps * wide,), f32), pl.BlockSpec(shape + (wide,), lambda j, _: (0, 0, 0, j)))
    else:
        out = (((D, steps * wide), f32), pl.BlockSpec((D, wide), lambda j, _: (0, j)))
    grads, top = call(
        functools.partial(weight_grad_kernel, members, relative, relative_y, is_new),
        name,
        (steps,),
        [(table, None), spec(own_a), spec(peer_a), spec(own_b), spec(peer_b)],
        [out, (((8, steps * wide), f32), pl.BlockSpec((8, wide), lambda j, _: (0, j)))],
        [pltpu.VMEM((2, D, rows), bf16)],
        4 * rows * D * wide * steps,
        4 * D * wide * steps + 4 * rows * (D + wide * steps),
        prefetch=1,
    )
    if not relative:
        grads = relative_rows(grads, members, relative_y, table[2], table[1])
    return grads, top[:1]


def contract_grad(table, members, keep, own, peer):
    rows = own.shape[0]
    wide = D // 2
    height = 4 * D // members
    relative = height == wide
    column = lambda index: pl.BlockSpec((rows, wide), lambda i, _: (0, index))
    moving = pl.BlockSpec((rows, wide), lambda i, _: (0, i))
    if relative:
        out = (
            ((members, 2, height // 2, wide), f32),
            pl.BlockSpec((1, 2, height // 2, wide), lambda i, t: (i ^ t[2], 0, 0, 0)),
        )
    else:
        out = (((4 * D, wide), f32), pl.BlockSpec((wide, wide), lambda i, _: (i, 0)))
    grads, top = call(
        functools.partial(contract_grad_kernel, relative),
        "grad_contract",
        (4 * D // wide,),
        [(table, None), (keep, column(5)), (peer, column(8)), (own, moving), (peer, moving)],
        [out, (((8, wide), f32), whole_spec((8, wide)))],
        [pltpu.VMEM((2, wide, rows), bf16)],
        16 * rows * D * wide,
        16 * D * wide + 16 * rows * D,
        prefetch=1,
    )
    if not relative:
        grads = relative_rows(grads, members, True, table[2], table[1])
    return grads, top[:1]


def after(value, *others):
    return lax.optimization_barrier((value, *others))[0]


def swap(values, bit):
    total = lax.axis_size("batch") * lax.axis_size("mlp")
    return lax.ppermute(values, ("batch", "mlp"), [(i, i ^ bit) for i in range(total)])


def batch_swap(values, bit):
    return swap(values, lax.axis_size("mlp") << bit)


def bit_of(axis, bit):
    return (lax.axis_index(axis) >> bit) & 1


def all_sum(values, bits):
    for bit in bits:
        values = values + swap(values, 1 << bit)
    return values


def half_of(values, which, axis):
    width = values.shape[axis] // 2
    return lax.dynamic_slice_in_dim(values, which * width, width, axis)


def in_order(first, second, bit_value, axis):
    return jnp.where(
        bit_value == 0,
        jnp.concatenate([first, second], axis),
        jnp.concatenate([second, first], axis),
    )


def natural_rows(blocks, order):
    count = len(order)
    full = blocks.reshape((2,) * count + blocks.shape[1:])
    for place in range(count):
        flip = bit_of("batch", order[count - 1 - place])
        full = jnp.where(flip == 0, full, jnp.flip(full, place))
    source = [count - 1 - order.index(bit) for bit in reversed(range(count))]
    full = full.transpose(source + [count, count + 1])
    return full.reshape(1, -1, full.shape[-1])


def blocks_group(held, last, order, row):
    members = 1 << len(order)
    height = held.shape[1]
    if height % 16 != 0:
        return whole_group(natural_rows(jnp.concatenate([held, last], 0), order), row)
    entries = [
        lax.axis_index("batch") ^ sum(((p >> j) & 1) << bit for j, bit in enumerate(order))
        for p in range(members)
    ]
    arrays = [held, last, swap(held, 1), swap(last, 1)]
    metas = [
        (height, height, row + part * (members // 2), near)
        for near in (True, False)
        for part in (0, 1)
    ]
    return (arrays, tuple(metas)), entries


def whole_group(near, row):
    metas = tuple((0, near.shape[1], row, side) for side in (True, False))
    return ([near, swap(near, 1)], metas), []


def power_of_two(exponent):
    size = jnp.abs(exponent).astype(jnp.int32)
    result = jnp.ones_like(exponent)
    for bit in range(7):
        factor = jnp.where(exponent > 0, 2.0 ** (1 << bit) if bit < 7 else 1.0, 2.0 ** -(1 << bit))
        result = jnp.where((size >> bit) & 1 == 1, result * factor, result)
    return result


def packed(values, bound):
    exponent = jnp.floor(14.0 - jnp.log2(jnp.clip(bound, 1e-30, 1e30)))
    scaled = lax.reduce_precision(values * power_of_two(exponent), 5, 10).astype(jnp.float16)
    tail = jnp.broadcast_to(exponent.astype(jnp.float16), (16, exponent.shape[1]))
    return jnp.concatenate([scaled.reshape(-1, scaled.shape[-1]), tail], 0)


def unpacked(rows, shape):
    exponent = rows[-1:].astype(f32)
    values = rows[:-16].astype(f32) * power_of_two(-exponent)
    return values.reshape(shape), power_of_two(15.0 - exponent)


def first_axis_half(sums, place):
    return lax.index_in_dim(sums, 0, place, keepdims=False), lax.index_in_dim(
        sums, 1, place, keepdims=False
    )


class Reduction:
    def __init__(self, blocks, top, order, y_first):
        count = len(order)
        self.sums = blocks.reshape((2,) * count + blocks.shape[1:])
        self.bound = top
        self.left = list(reversed(range(count))) + ["y"]
        self.hops = (["y"] if y_first else []) + list(order)
        self.y_first = y_first
        self.sent = None

    def send(self, *gates):
        if self.hops:
            place = self.left.index(self.hops[0])
            self.left.remove(self.hops[0])
            self.sums, sent = first_axis_half(self.sums, place)
            self.sent = packed(after(sent, *gates), self.bound)
        else:
            self.sent = packed(after(self.sums, *gates), self.bound)
        return self.sent

    def receive(self):
        if not self.hops:
            other = swap(self.sent, 2)
            own, _ = unpacked(self.sent, self.sums.shape)
            other, _ = unpacked(other, self.sums.shape)
            if self.y_first:
                self.sums = in_order(own, other, bit_of("mlp", 1), 0)
            else:
                self.sums = (own + other).reshape(-1, own.shape[-1])
            return self
        bit = self.hops.pop(0)
        other = swap(self.sent, 2) if bit == "y" else batch_swap(self.sent, bit)
        other, bound = unpacked(other, self.sums.shape)
        self.sums = self.sums + other
        self.bound = self.bound + bound
        return self

    def hop(self, *gates):
        self.send(*gates)
        return self.receive()

    def finish(self):
        while self.hops:
            self.hop()
        return self.hop().sums


def adam_update(master, first, second, gradient, step_rate, weight_decay):
    moment = beta_first * first + (1.0 - beta_first) * gradient
    variance = beta_second * second + (1.0 - beta_second) * gradient * gradient
    corrected = moment / (1.0 - beta_first**STEP)
    scaled = variance / (1.0 - beta_second**STEP)
    updated = master - step_rate * (
        corrected / (jnp.sqrt(scaled) + adam_eps) + weight_decay * master
    )
    return (moment, variance, updated)


def on_device(
    patches,
    mask,
    student_square,
    student_qkv,
    student_expand,
    student_contract,
    student_vectors,
    first_square,
    first_qkv,
    first_expand,
    first_contract,
    first_vectors,
    second_square,
    second_qkv,
    second_expand,
    second_contract,
    second_vectors,
    teacher_square,
    teacher_qkv,
    teacher_expand,
    teacher_contract,
    teacher_vectors,
):
    members = lax.axis_size("batch")
    count = members.bit_length() - 1
    mlp_bits = lax.axis_size("mlp").bit_length() - 1
    near = list(range(count))
    far = near[::-1]
    batch_bits = range(mlp_bits, mlp_bits + count)
    shard_rows = D // members
    core, own_y = bit_of("mlp", 0), bit_of("mlp", 1)
    place = lax.axis_index("batch")
    group, real_rows = mask.shape
    pad_rows = -(-real_rows // 16) * 16
    half = D // 2

    pad = ((0, 0), (0, pad_rows - real_rows))
    x = jnp.pad(patches, pad + ((0, 0),)).reshape(-1, D)
    marks = jnp.pad(mask.astype(f32), pad).reshape(-1)
    wide_marks = jnp.broadcast_to(marks[:, None], (marks.shape[0], 128))

    square_half = jnp.concatenate([half_of(student_square[i], core, 1) for i in range(3)], 1)
    square_held = square_half.astype(bf16)[None]
    qkv_held = half_of(student_qkv, core, 1).astype(bf16)[None]
    expand_near = lax.all_gather(
        half_of(student_expand, core, 1).astype(bf16), "batch", axis=0, tiled=True
    )
    contract_near = lax.all_gather(
        half_of(student_contract, core, 1).astype(bf16), "batch", axis=0, tiled=True
    )
    teacher_own = jnp.concatenate([teacher_expand, teacher_contract], 1)
    teacher_y = swap(teacher_own, 2)
    teacher_core = swap(teacher_own, 1)
    low_vectors = lax.reduce_precision(student_vectors, 8, 7)
    small = lax.dynamic_update_slice(
        jnp.zeros((low_vectors.shape[0], D), f32), low_vectors, (0, place * shard_rows)
    )
    small = jnp.concatenate([small, jnp.full((1, D), jnp.sum(marks))], 0)

    images = min(group, 2)
    sizes = (real_rows, pad_rows, images)
    teacher_weights = (teacher_square[0], teacher_qkv, teacher_square[1], teacher_vectors)
    own = lax.axis_index("mlp")
    biases = jnp.concatenate(
        [lax.dynamic_slice_in_dim(teacher_vectors, 8 + (own ^ part), 1, 0) for part in range(4)]
    )
    tmids, tsum, done = [], None, ()
    square_order, qkv_order = far, near[:1] + far[:-1]
    for hop in range(count):
        sends = lax.optimization_barrier((square_held, qkv_held, small, *done))[:3]
        square_held, qkv_held, small = sends
        square_last = batch_swap(square_held, square_order[hop])
        qkv_last = batch_swap(qkv_held, qkv_order[hop])
        small_last = batch_swap(small, near[hop])
        if len(tmids) < group // images:
            item = attend_teacher(*sizes, len(tmids), after(x, *sends), *teacher_weights)
            tmids.append(item)
            done = (item,)
        elif tsum is None:
            tmid = jnp.concatenate(tmids, 0)
            tsum = teacher_ffn(
                *sizes,
                after(tmid, *sends),
                (teacher_own, teacher_core),
                biases[:2],
                teacher_vectors,
                None,
            )
            done = (tsum,)
        if hop + 1 < count:
            square_held = jnp.concatenate([square_held, square_last], 0)
            qkv_held = jnp.concatenate([qkv_held, qkv_last], 0)
        small = small + small_last
    vectors = small[:-1]
    square_held, qkv_held, square_last, qkv_last = lax.optimization_barrier(
        (square_held, qkv_held, square_last, qkv_last, *done)
    )[:4]
    square, square_rows = blocks_group(square_held, square_last, square_order, 3)
    qkv, qkv_rows = blocks_group(qkv_held, qkv_last, qkv_order, 3 + len(square_rows))
    entries = [core, own_y, place] + square_rows + qkv_rows
    table = jnp.stack([jnp.asarray(entry, jnp.int32) for entry in entries])

    masked_count = all_sum(small[-1:, :128], range(mlp_bits))[0, 0]
    teacher_far = swap(after(teacher_y, small), 1)
    start, mid, joint, act = attend_student(
        *sizes, table, after(x, tsum), wide_marks, vectors, square, qkv
    )
    act_peer = swap(act, 1)
    expand, _ = whole_group(after(expand_near, mid)[None], 0)
    contract, _ = whole_group(after(contract_near, mid)[None], 0)
    targets = teacher_ffn(
        *sizes,
        after(tmid, mid),
        (teacher_y, teacher_far),
        biases[2:],
        teacher_vectors,
        tsum,
    )
    scale = (2.0 / (masked_count * D)).reshape(1)
    keep, one, two, dmid, ffn_sums = student_ffn(
        pad_rows, images, table, scale, mid, targets, wide_marks, vectors, square, expand, contract
    )
    one_peer, two_peer = swap(one, 1), swap(two, 1)

    blocks, top = weight_grad(
        "grad_expand",
        table,
        members,
        False,
        5,
        (one, D, lambda j: 1 - j // 4),
        (one_peer, D, lambda j: 1 - j // 4),
        (keep, half, lambda j: j),
        (one_peer, half, lambda j: j + 4),
        lambda j: (j == 0) | (j == 4),
    )
    to_expand = Reduction(blocks, top, near, False)
    sent = to_expand.send()
    blocks, top = contract_grad(table, members, keep, two, after(two_peer, sent))
    to_contract = Reduction(blocks, top, near, True)
    sent = to_contract.send()
    keep3, send3, att_sums = attend_back(
        *sizes, table, after(dmid, sent), joint, start, wide_marks, vectors, square, qkv
    )
    total = jnp.concatenate([ffn_sums[:12], att_sums[:6]], 0)
    total_bits = list(range(mlp_bits + count))
    send3_peer = swap(send3, 1)
    moving = [to_expand, to_contract]

    def receive_all():
        for item in moving:
            item.receive()

    def send_all(*gates):
        return [item.send(*gates) for item in moving]

    def total_hop(*gates):
        nonlocal total
        if total_bits:
            total = after(total, *gates)
            total = total + swap(total, 1 << total_bits.pop(0))

    receive_all()
    sent = send_all(keep3)
    blocks, top = weight_grad(
        "grad_out_joint",
        table,
        members,
        False,
        2,
        (act, D, lambda j: j),
        (act_peer, D, lambda j: j),
        (keep3, half, lambda j: j),
        (after(send3_peer, *sent), half, lambda j: j),
        lambda j: j >= 0,
    )
    total_hop(*sent)
    receive_all()
    to_first = Reduction(blocks, top, near, False)
    moving.append(to_first)
    sent = send_all(blocks)
    blocks, top = weight_grad(
        "grad_joint_embed",
        table,
        members,
        True,
        3,
        (act, D, lambda j: 1 + j // 2),
        (act_peer, D, lambda j: 1 + j // 2),
        (keep3, half, lambda j: j + 2),
        (after(send3_peer, total, *sent), half, lambda j: j + 2),
        lambda j: (j == 0) | (j == 2),
    )
    total_hop(*sent)
    receive_all()
    to_second = Reduction(blocks, top, near, True)
    moving.append(to_second)
    gates = (blocks,)
    while moving:
        total_hop(*send_all(*gates))
        for item in list(moving):
            is_last = not item.hops
            item.receive()
            if is_last:
                moving.remove(item)
        gates = ()
    while total_bits:
        total_hop()
    sum_expand, sum_contract = to_expand.sums, to_contract.sums
    sum_first, sum_second = to_first.sums, to_second.sums
    ffn_total, att_total = total[:12], total[12:]

    own_sums = (sum_expand, sum_contract, sum_first, sum_second)
    vector_total = jnp.concatenate(
        [
            att_total[5:6],
            att_total[4:5],
            att_total[2:4],
            att_total[0:2],
            ffn_total[11:12],
            ffn_total[9:11],
            ffn_total[5:9],
            ffn_total[4:5],
            ffn_total[2:4],
            ffn_total[1:2],
        ]
    )
    loss_sum = jnp.sum(ffn_total[0])
    vector_grad = lax.dynamic_slice_in_dim(vector_total, place * shard_rows, shard_rows, 1)
    squares = 0.5 * jnp.sum(vector_grad * vector_grad)
    for member in own_sums:
        squares = squares + jnp.sum(member * member)
    squares = all_sum(jnp.full((1, 128), squares), [0, *batch_bits])
    grad_norm = jnp.sqrt(squares[0, 0])
    factor = clip_bound / jnp.maximum(grad_norm, clip_bound)

    pairs = [(item, swap(item, 1)) for item in own_sums]

    def columns(index, first, last):
        return [item[:, first:last] for item in pairs[index]]

    joint_pair = [
        jnp.concatenate([left, right], 1)
        for left, right in zip(columns(2, half, 2 * half), columns(3, 0, 2 * half))
    ]
    whole = lambda pair: in_order(pair[0], pair[1], core, 1)
    grads = (
        jnp.stack(
            [
                whole(columns(3, 2 * half, 3 * half)),
                whole(columns(2, 0, half)),
                whole(columns(0, 4 * half, 5 * half)),
            ]
        ),
        whole(joint_pair),
        whole(columns(0, 0, 4 * half)),
        whole(columns(1, 0, half)),
        vector_grad,
    )
    masters = (student_square, student_qkv, student_expand, student_contract, student_vectors)
    firsts = (first_square, first_qkv, first_expand, first_contract, first_vectors)
    seconds = (second_square, second_qkv, second_expand, second_contract, second_vectors)
    results = [loss_sum, masked_count, grad_norm]
    for index, (master, first, second, grad) in enumerate(zip(masters, firsts, seconds, grads)):
        rate, decay = (rate_vector, 0.0) if index == 4 else (rate_matrix, decay_matrix)
        results += adam_update(master, first, second, grad * factor, rate, decay)
    return tuple(results)


def solution(mesh):
    return jax.shard_map(
        on_device,
        mesh=mesh,
        in_specs=(
            P(("batch", "mlp"), None, None),
            P(("batch", "mlp"), None),
            P(None, "batch", None),
            P("batch", None),
            P("batch", None),
            P("batch", None),
            P(None, "batch"),
            P(None, "batch", None),
            P("batch", None),
            P("batch", None),
            P("batch", None),
            P(None, "batch"),
            P(None, "batch", None),
            P("batch", None),
            P("batch", None),
            P("batch", None),
            P(None, "batch"),
            P(),
            P(),
            P(None, "mlp"),
            P("mlp", None),
            P(),
        ),
        out_specs=(
            P(),
            P(),
            P(),
            P(None, "batch", None),
            P(None, "batch", None),
            P(None, "batch", None),
            P("batch", None),
            P("batch", None),
            P("batch", None),
            P("batch", None),
            P("batch", None),
            P("batch", None),
            P("batch", None),
            P("batch", None),
            P("batch", None),
            P(None, "batch"),
            P(None, "batch"),
            P(None, "batch"),
        ),
        check_vma=False,
    )
```

```python
import functools

import jax
import jax.numpy as jnp
from jax import lax
from jax.experimental import pallas as pl
from jax.experimental.pallas import tpu as pltpu
from jax.sharding import PartitionSpec as P

D = 768
HEAD_DIM = 64
PAIR = 2 * HEAD_DIM
UNROLL = 3
STEP = 10


norm_eps = 1e-06
inst_eps = 1e-05
clip_bound = 0.001
rate_matrix = 0.05
rate_vector = 0.5
decay_matrix = 0.05
beta_first = 0.9
beta_second = 0.999
adam_eps = 1e-08
f32 = jnp.float32
bf16 = jnp.bfloat16


def mm(left, right):
    return lax.dot_general(left, right, (((1,), (0,)), ((), ())), preferred_element_type=f32)


def mm_nt(left, right):
    return lax.dot_general(left, right, (((1,), (1,)), ((), ())), preferred_element_type=f32)


def mm_tn(left, right):
    return lax.dot_general(left, right, (((0,), (0,)), ((), ())), preferred_element_type=f32)


def normed_rows(values):
    centred = values - jnp.mean(values, axis=-1, keepdims=True)
    variance = jnp.mean(centred * centred, axis=-1, keepdims=True)
    scale = lax.rsqrt(variance + norm_eps)
    return centred * scale, scale


def norm_back(xhat, scale, gain, grads):
    scaled = grads * gain
    mean_one = jnp.mean(scaled, axis=-1, keepdims=True)
    mean_two = jnp.mean(scaled * xhat, axis=-1, keepdims=True)
    back = scale * (scaled - mean_one - xhat * mean_two)
    return back, total_rows(grads * xhat), total_rows(grads)


def copy_all(copies):
    for copy in copies:
        copy.start()
    for copy in copies:
        copy.wait()


def piece_copies(table_ref, semaphores, pieces):
    core, own_y = table_ref[0], table_ref[1]
    copies = []
    for ref, (side, unit, height, row, near), lanes, target, offset in pieces:
        width = lanes[1] - lanes[0]
        column = (core if near else 1 - core) * (target.shape[1] // 2) + offset
        column = pl.multiple_of(column, 128)
        base = (0, own_y * height, (1 - own_y) * height)[side]
        for block in range(ref.shape[0]):
            place = 0 if unit == 0 else pl.multiple_of(table_ref[row + block] * unit + base, 16)
            copies.append(
                pltpu.make_async_copy(
                    ref.at[block, :, pl.ds(lanes[0], width)],
                    target.at[pl.ds(place, height), pl.ds(column, width)],
                    semaphores.at[len(copies)],
                )
            )
    return copies


def total_rows(values):
    return jnp.sum(values, axis=0, keepdims=True)


def head_masks(rows):
    lane = lax.broadcasted_iota(jnp.int32, (rows, PAIR), 1)
    return lane < HEAD_DIM


def stacked(values, low):
    zero = jnp.zeros_like(values)
    return jnp.concatenate([jnp.where(low, values, zero), jnp.where(low, zero, values)], axis=0)


def pair_probs(stack, keys, real_rows):
    scores = mm_nt(stack, keys)
    column = lax.broadcasted_iota(jnp.int32, scores.shape, 1)
    scores = jnp.where(column < real_rows, scores, -1e30)
    shifted = jnp.exp(scores - jnp.max(scores, axis=-1, keepdims=True))
    return shifted * (1.0 / jnp.sum(shifted, axis=-1, keepdims=True))


def attend_block(is_student, real_rows, pad_rows, x_ref, marks_ref, weights, vec_ref, outs):
    w0_ref, wj_ref, w1_ref = weights
    start_ref, mid_ref, joint_ref, act_ref = outs
    at = (lambda student, teacher: student if is_student else teacher)
    vec = lambda row: vec_ref[row : row + 1, :]
    block = x_ref.shape[0]
    start = mm(x_ref[...], w0_ref[...]) + vec(0)
    if is_student:
        start = jnp.where(marks_ref[:, :1] > 0, vec(1), start)
    start_ref[...] = start
    xhat, _ = normed_rows(start)
    normed = (xhat * vec(at(2, 1)) + vec(at(3, 2))).astype(bf16)
    if is_student:
        act_ref[:, D : 2 * D] = normed
        act_ref[:, 2 * D :] = x_ref[...]
    biases = (vec(at(4, 3)), None, vec(at(5, 4)))
    for part in range(3):
        cols = slice(part * D, (part + 1) * D)
        mixed = mm(normed, wj_ref[:, cols])
        if biases[part] is not None:
            mixed = mixed + biases[part]
        joint_ref[:, cols] = mixed.astype(bf16)
    low = head_masks(pad_rows)

    def one_pair(step, carry):
        image = step // (D // PAIR)
        col = pl.multiple_of((step % (D // PAIR)) * PAIR, PAIR)
        rows = pl.ds(pl.multiple_of(image * pad_rows, 16), pad_rows)
        queries = joint_ref[rows, pl.ds(col, PAIR)] * HEAD_DIM ** (-0.5)
        keys = joint_ref[rows, pl.ds(col + D, PAIR)]
        values = joint_ref[rows, pl.ds(col + 2 * D, PAIR)]
        probs = pair_probs(stacked(queries.astype(bf16), low), keys, real_rows).astype(bf16)
        mixed = mm(probs, values)
        act_ref[rows, pl.ds(col, PAIR)] = jnp.where(
            low, mixed[:pad_rows], mixed[pad_rows:]
        ).astype(bf16)
        return carry

    lax.fori_loop(0, (block // pad_rows) * (D // PAIR), one_pair, 0, unroll=UNROLL)
    attended = act_ref[:, :D]
    mid_ref[...] = start_ref[...] + mm(attended, w1_ref[...]) + vec(at(6, 5))


def clear_at_first(*refs):
    @pl.when(pl.program_id(0) == 0)
    def _():
        for ref in refs:
            ref[...] = jnp.zeros_like(ref)


def place_at_first(table_ref, semaphores, pieces):
    @pl.when(pl.program_id(0) == 0)
    def _():
        copy_all(piece_copies(table_ref, semaphores, pieces))


def attend_teacher_kernel(real_rows, pad_rows, *refs):
    x_ref, w0_ref, wj_ref, w1_ref, vec_ref = refs[:5]
    mid_ref, joint_ref, att_ref = refs[-3:]
    attend_block(
        False,
        real_rows,
        pad_rows,
        x_ref,
        None,
        (w0_ref, wj_ref, w1_ref),
        vec_ref,
        (mid_ref, mid_ref, joint_ref, att_ref),
    )


def attend_student_kernel(real_rows, pad_rows, metas, joint_metas, *refs):
    (table_ref, x_ref, marks_ref, vec_ref) = refs[:4]
    count = len(metas)
    piece_refs, joint_refs = refs[4 : 4 + count], refs[4 + count : 4 + 2 * count]
    (start_ref, mid_ref, joint_ref, act_ref) = refs[4 + 2 * count : 8 + 2 * count]
    (w0_ref, w1_ref, wj_ref, semaphores) = refs[8 + 2 * count :]
    pieces = section(piece_refs, metas, SQUARE_LANES[0], w0_ref)
    pieces += section(piece_refs, metas, SQUARE_LANES[2], wj_ref)
    pieces += section(joint_refs, joint_metas, (0, D), wj_ref, D // 2)
    pieces += section(piece_refs, metas, SQUARE_LANES[1], w1_ref)
    place_at_first(table_ref, semaphores, pieces)
    attend_block(
        True,
        real_rows,
        pad_rows,
        x_ref,
        marks_ref,
        (w0_ref, wj_ref, w1_ref),
        vec_ref,
        (start_ref, mid_ref, joint_ref, act_ref),
    )


def gelu_half(values):
    return 0.5 * (1.0 + lax.erf(values * 0.7071067811865476))


def teacher_ffn_kernel(real_rows, pad_rows, is_last, *refs):
    mid_ref, bias_ref, vec_ref = refs[:3]
    parts = bias_ref.shape[0]
    rest = refs[3 + parts :]
    mid = mid_ref[...]
    xhat, _ = normed_rows(mid)
    normed = (xhat * vec_ref[6:7, :] + vec_ref[7:8, :]).astype(bf16)
    total = rest[0][...] if is_last else None
    for part, both_ref in enumerate(refs[3 : 3 + parts]):
        pre = mm(normed, both_ref[:, :D]) + bias_ref[part : part + 1, :]
        hidden = (pre * gelu_half(pre)).astype(bf16)
        piece = mm(hidden, both_ref[:, D:])
        total = piece if total is None else total + piece
    out_ref = rest[-1]
    if not is_last:
        out_ref[...] = total
        return
    total = total + vec_ref[12:13, :]
    valid = lax.broadcasted_iota(jnp.int32, (pad_rows, D), 0) < real_rows
    for image in range(mid_ref.shape[0] // pad_rows):
        rows = slice(image * pad_rows, (image + 1) * pad_rows)
        result = None
        for values in (mid[rows], total[rows]):
            mean = total_rows(jnp.where(valid, values, 0.0)) / real_rows
            centred = values - mean
            variance = total_rows(jnp.where(valid, centred * centred, 0.0)) / real_rows
            normal = centred * lax.rsqrt(variance + inst_eps)
            result = normal if result is None else result + normal
        out_ref[rows, :] = 0.5 * result


def student_ffn_kernel(expand_metas, contract_metas, *refs):
    (table_ref, scale_ref, mid_ref, target_ref, marks_ref, vec_ref) = refs[:6]
    counts = (len(expand_metas), len(contract_metas))
    expand_refs, contract_refs = refs[6 : 6 + counts[0]], refs[6 + counts[0] : 6 + sum(counts)]
    (keep_ref, one_ref, two_ref, dmid_ref, sum_ref) = refs[6 + sum(counts) : 11 + sum(counts)]
    (we_ref, wc_ref, wh_ref, slope_ref, half_ref, semaphores) = refs[11 + sum(counts) :]
    pieces = section(expand_refs, expand_metas, (0, 2 * D), we_ref)
    pieces += section(contract_refs, contract_metas, (0, D // 2), wc_ref)
    pieces += section(expand_refs, expand_metas, (2 * D, 5 * D // 2), wh_ref)
    clear_at_first(sum_ref)
    place_at_first(table_ref, semaphores, pieces)
    core = table_ref[0]

    def add(row, values):
        sum_ref[pl.ds(row, 1), :] += values

    def add_grad(row, grads):
        add(row, total_rows(grads.astype(f32)))

    def halves(keep_cols, send_ref, send_cols, grads):
        half_ref[...] = grads
        width = D // 2
        keep_ref[:, keep_cols : keep_cols + width] = half_ref[
            :, pl.ds(pl.multiple_of(core * width, 128), width)
        ]
        send_ref[:, send_cols : send_cols + width] = half_ref[
            :, pl.ds(pl.multiple_of((1 - core) * width, 128), width)
        ]

    vec = lambda row: vec_ref[row : row + 1, :]
    mid = mid_ref[...]
    xhat2, scale2 = normed_rows(mid)
    n2 = (xhat2 * vec(7) + vec(8)).astype(bf16)
    one_ref[:, :D] = n2
    total = None
    for part in range(4):
        cols = slice(part * D, (part + 1) * D)
        pre = mm(n2, we_ref[:, cols]) + vec(9 + part)
        half = gelu_half(pre)
        slope_ref[:, cols] = half + pre * (jnp.exp(-0.5 * pre * pre) * 0.3989422804014327)
        hidden = (pre * half).astype(bf16)
        two_ref[:, (part + 1) * D : (part + 2) * D] = hidden
        piece = mm(hidden, wc_ref[cols, :])
        total = piece if total is None else total + piece
    final = mid + total + vec(13)
    xhat3, scale3 = normed_rows(final)
    n3 = (xhat3 * vec(14) + vec(15)).astype(bf16)
    two_ref[:, :D] = n3
    error = marks_ref[:, :1] * (mm(n3, wh_ref[...]) + vec(16) - target_ref[...])
    add(0, total_rows(error * error))
    dpred = (error * scale_ref[0]).astype(bf16)
    halves(2 * D, two_ref, 11 * D // 2, dpred)
    add_grad(1, dpred)
    dfinal, gain3, shift3 = norm_back(xhat3, scale3, vec(14), mm_nt(dpred, wh_ref[...]))
    add(2, gain3)
    add(3, shift3)
    dbranch = dfinal.astype(bf16)
    halves(2 * D + D // 2, two_ref, 5 * D, dbranch)
    add_grad(4, dbranch)
    dn2 = None
    for side in range(2):
        for part in range(2):
            chunk = 2 * (core ^ side) + part
            cols = pl.ds(pl.multiple_of(chunk * D, 128), D)
            dpre = (mm_nt(dbranch, wc_ref[cols, :]) * slope_ref[:, cols]).astype(bf16)
            if side == 0:
                keep_ref[:, part * D : (part + 1) * D] = dpre
            else:
                one_ref[:, (1 + part) * D : (2 + part) * D] = dpre
            add_grad(5 + chunk, dpre)
            piece = mm_nt(dpre, we_ref[:, cols])
            dn2 = piece if dn2 is None else dn2 + piece
    dmid, gain2, shift2 = norm_back(xhat2, scale2, vec(7), dn2)
    add(9, gain2)
    add(10, shift2)
    dmid = dfinal + dmid
    dmid_ref[...] = dmid
    datt = dmid.astype(bf16)
    halves(3 * D, one_ref, 3 * D, datt)
    add(11, total_rows(datt.astype(f32)))


def attend_back_kernel(real_rows, pad_rows, metas, joint_metas, *refs):
    (table_ref, dmid_ref, joint_ref, start_ref, marks_ref, vec_ref) = refs[:6]
    count = len(metas)
    piece_refs, joint_refs = refs[6 : 6 + count], refs[6 + count : 6 + 2 * count]
    (keep_ref, send_ref, sum_ref) = refs[6 + 2 * count : 9 + 2 * count]
    (w1_ref, wj_ref, grad_ref, djoint_ref, half_ref, semaphores) = refs[9 + 2 * count :]
    pieces = section(piece_refs, metas, SQUARE_LANES[1], w1_ref)
    pieces += section(piece_refs, metas, SQUARE_LANES[2], wj_ref)
    pieces += section(joint_refs, joint_metas, (0, D), wj_ref, D // 2)
    clear_at_first(sum_ref)
    place_at_first(table_ref, semaphores, pieces)
    core = table_ref[0]

    def add(row, values):
        sum_ref[row : row + 1, :] += values

    def halves(column, source_ref, width):
        keep_ref[:, column : column + width] = source_ref[
            :, pl.ds(pl.multiple_of(core * width, 128), width)
        ]
        send_ref[:, column : column + width] = source_ref[
            :, pl.ds(pl.multiple_of((1 - core) * width, 128), width)
        ]

    vec = lambda row: vec_ref[row : row + 1, :]
    block = dmid_ref.shape[0]
    datt = dmid_ref[...].astype(bf16)
    grad_ref[...] = mm_nt(datt, w1_ref[...]).astype(bf16)
    low = head_masks(pad_rows)

    def one_pair(step, carry):
        image = step // (D // PAIR)
        col = pl.multiple_of((step % (D // PAIR)) * PAIR, PAIR)
        rows = pl.ds(pl.multiple_of(image * pad_rows, 16), pad_rows)
        queries = joint_ref[rows, pl.ds(col, PAIR)] * HEAD_DIM ** (-0.5)
        keys = joint_ref[rows, pl.ds(col + D, PAIR)]
        values = joint_ref[rows, pl.ds(col + 2 * D, PAIR)]
        stack = stacked(queries.astype(bf16), low)
        dstack = stacked(grad_ref[rows, pl.ds(col, PAIR)], low)
        probs = pair_probs(stack, keys, real_rows)
        dprobs = mm_nt(dstack, values)
        dvalues = mm_tn(probs.astype(bf16), dstack)
        weighted = probs * dprobs
        dscores = (weighted - probs * jnp.sum(weighted, axis=-1, keepdims=True)).astype(bf16)
        both = mm(dscores, keys) * HEAD_DIM ** (-0.5)
        dqueries = jnp.where(low, both[:pad_rows], both[pad_rows:])
        dkeys = mm_tn(dscores, stack)
        djoint_ref[rows, pl.ds(col, PAIR)] = dqueries.astype(bf16)
        djoint_ref[rows, pl.ds(col + D, PAIR)] = dkeys.astype(bf16)
        djoint_ref[rows, pl.ds(col + 2 * D, PAIR)] = dvalues.astype(bf16)
        return carry

    lax.fori_loop(0, (block // pad_rows) * (D // PAIR), one_pair, 0, unroll=UNROLL)
    halves(0, djoint_ref, 3 * D // 2)
    dnormed = None
    for part in range(3):
        cols = slice(part * D, (part + 1) * D)
        grads = djoint_ref[:, cols]
        if part != 1:
            add(part // 2, total_rows(grads.astype(f32)))
        piece = mm_nt(grads, wj_ref[:, cols])
        dnormed = piece if dnormed is None else dnormed + piece
    xhat, scale = normed_rows(start_ref[...])
    dstart, gain, shift = norm_back(xhat, scale, vec(2), dnormed)
    add(2, gain)
    add(3, shift)
    dstart = dstart + dmid_ref[...]
    masked = marks_ref[:, :1] > 0
    add(4, total_rows(jnp.where(masked, dstart, 0.0)))
    dembed = jnp.where(masked, 0.0, dstart).astype(bf16)
    half_ref[...] = dembed
    halves(3 * D // 2, half_ref, D // 2)
    add(5, total_rows(dembed.astype(f32)))


def relative_places(members, y_first):
    count = members.bit_length() - 1
    rels = [sum(((p >> (count - 1 - bit)) & 1) << bit for bit in range(count)) for p in range(members)]
    if y_first:
        return [(rel, side) for side in range(2) for rel in rels]
    return [(rel, None) for rel in rels]


def column_exponents(top):
    return jnp.floor(14.0 - jnp.log(jnp.clip(top, 1e-30, 1e30)) * 1.4426950408889634)


def store_halves(keep_ref, sent_ref, top_ref, table_ref, plain_ref, members, y_first):
    top = jnp.max(jnp.abs(plain_ref[...]), axis=0, keepdims=True)
    top_ref[...] = jnp.broadcast_to(top, top_ref.shape)
    exponent = column_exponents(top)
    factor = jnp.exp2(exponent)
    places = relative_places(members, y_first)
    rows = plain_ref.shape[0] // members
    height = rows // 2 if y_first else rows
    for index, (rel, side) in enumerate(places):
        first = (table_ref[2] ^ rel) * rows
        if y_first:
            first = first + (table_ref[1] ^ side) * height
        block = plain_ref[pl.ds(pl.multiple_of(first, 16), height), :]
        if index < len(places) // 2:
            keep_ref[index * height : (index + 1) * height, :] = block
        else:
            here = (index - len(places) // 2) * height
            sent_ref[here : here + height, :] = block * factor
    half_rows = keep_ref.shape[0]
    sent_ref[half_rows:, :] = jnp.broadcast_to(exponent, (16, exponent.shape[1]))


def weight_grad_kernel(members, y_first, relative, new_at, *refs):
    table_ref = refs[0]
    sides = refs[1 : 1 + 2 * len(new_at)]
    b_ref, b_peer_ref = refs[1 + 2 * len(new_at) : 3 + 2 * len(new_at)]
    outs, (turned_ref, plain_ref) = refs[3 + 2 * len(new_at) : -2], refs[-2:]
    step = pl.program_id(0)
    for index, steps in enumerate(new_at):
        is_new = step == steps[0]
        for other in steps[1:]:
            is_new = is_new | (step == other)

        @pl.when(is_new)
        def _(index=index):
            turned_ref[0] = sides[2 * index][...].T
            turned_ref[1] = sides[2 * index + 1][...].T

    plain_ref[...] = mm(turned_ref[0], b_ref[...]) + mm(turned_ref[1], b_peer_ref[...])
    if relative:
        store_halves(*outs, table_ref, plain_ref, members, y_first)
    else:
        outs[0][...] = plain_ref[...]


def contract_grad_kernel(members, relative, *refs):
    (table_ref, d_ref, d_peer_ref, h_ref, h_peer_ref) = refs[:5]
    (n_ref, n_peer_ref, b_ref, b_peer_ref) = refs[5:9]
    outs, (turned_ref, plain_ref) = refs[9:-2], refs[-2:]
    step = pl.program_id(0)
    half = D // 2

    @pl.when(step == 0)
    def _():
        turned_ref[0, :half] = d_ref[...].T
        turned_ref[1, :half] = d_peer_ref[...].T

    @pl.when(step < pl.num_programs(0) - 1)
    def _():
        result = mm(turned_ref[0, :half], h_ref[...]) + mm(turned_ref[1, :half], h_peer_ref[...])
        if relative:
            rows = D // members
            here = pl.ds(pl.multiple_of(step * rows, 16), rows)
            for part in range(half // rows):
                plain_ref[here, part * half : (part + 1) * half] = result[
                    part * rows : (part + 1) * rows
                ]
        else:
            outs[0][...] = result

    @pl.when(step == pl.num_programs(0) - 1)
    def _():
        turned_ref[0] = n_ref[...].T
        turned_ref[1] = n_peer_ref[...].T
        result = mm(turned_ref[0], b_ref[...]) + mm(turned_ref[1], b_peer_ref[...])
        if relative:
            plain_ref[:, 2 * D :] = result
            store_halves(*outs, table_ref, plain_ref, members, True)
        else:
            outs[1][...] = result


def adam_kernel(pick, *refs):
    table_ref, numbers_ref = refs[:2]
    master_ref, first_ref, second_ref = refs[2:5]
    sums, outs = refs[5:-3], refs[-3:]
    grads = pick(pl.program_id(0), table_ref[0], numbers_ref, sums)
    results = adam_update(
        master_ref[...], first_ref[...], second_ref[...], grads, rate_matrix, decay_matrix
    )
    for out_ref, result in zip(outs, results):
        out_ref[...] = result


SQUARE_LANES = tuple((i * D // 2, (i + 1) * D // 2) for i in range(3))


def section(refs, metas, lanes, target, offset=0):
    return [(ref, meta, lanes, target, offset) for ref, meta in zip(refs, metas)]


def blocks_of(group):
    return sum(array.shape[0] for array in group[0])


def whole_spec(shape):
    return pl.BlockSpec(shape, lambda *_: (0,) * len(shape), pipeline_mode=pl.Buffered(1))


def row_spec(block, width):
    return pl.BlockSpec((block, width), lambda i, *_: (i, 0))


COSTS = {"adam_square": 3, "adam_qkv": 3, "adam_expand": 3, "adam_contract": 3, 'attend_teacher': 13, 'attend_student': 29, 'teacher_ffn': 9, 'student_ffn': 35, 'attend_back': 36, 'grad_expand': 15, 'grad_contract': 13, 'grad_joint': 7, 'grad_embed': 7}
smem_spec = pl.BlockSpec(memory_space=pltpu.SMEM)
any_spec = pl.BlockSpec(memory_space=pl.ANY)


def call(kernel, name, grid, ins, outs, scratch, flops, moved, prefetch=0, aliases={}):
    return pl.pallas_call(
        kernel,
        grid_spec=pltpu.PrefetchScalarGridSpec(
            num_scalar_prefetch=prefetch,
            grid=grid,
            in_specs=[spec for _, spec in ins[prefetch:]],
            out_specs=[spec for _, spec in outs],
            scratch_shapes=scratch,
        ),
        out_shape=[jax.ShapeDtypeStruct(*item) for item, _ in outs],
        input_output_aliases=aliases,
        compiler_params=pltpu.CompilerParams(vmem_limit_bytes=60 << 20),
        cost_estimate=pl.CostEstimate(
            flops=int(COSTS[name] * 1.15e9), transcendentals=0, bytes_accessed=1
        ),
        name=name,
    )(*[item for item, _ in ins])


def attend_teacher(real_rows, pad_rows, images, first, before, x, square, wj, vectors):
    rows, block = x.shape[0], images * pad_rows
    wj, vectors = ((item, whole_spec(item.shape)) for item in (wj, vectors))
    w0, w1 = ((square, pl.BlockSpec((None, D, D), lambda i, *_, at=at: (at, 0, 0))) for at in range(2))
    here = pl.BlockSpec((block, D), lambda i, *_: (first, 0))
    return call(
        functools.partial(attend_teacher_kernel, real_rows, pad_rows),
        "attend_teacher",
        (1,),
        [(x, here), w0, wj, w1, vectors] + ([] if before is None else [(before, any_spec)]),
        [(((rows, D), f32), here)],
        [pltpu.VMEM((block, 3 * D), bf16), pltpu.VMEM((block, D), bf16)],
        14 * rows * D * D,
        20e6,
        aliases={} if before is None else {5: 0},
    )[0]


def attend_student(real_rows, pad_rows, images, table, x, marks, vectors, square, joint):
    rows, block = x.shape[0], images * pad_rows
    arrays, metas = square[0] + joint[0], (square[1], joint[1])
    outs = [(D, f32), (D, f32), (3 * D, bf16), (3 * D, bf16)]
    return call(
        functools.partial(attend_student_kernel, real_rows, pad_rows, *metas),
        "attend_student",
        (rows // block,),
        [
            (table, smem_spec),
            (x, row_spec(block, D)),
            (marks, row_spec(block, 128)),
            (vectors, whole_spec(vectors.shape)),
        ]
        + [(array, any_spec) for array in arrays],
        [(((rows, width), kind), row_spec(block, width)) for width, kind in outs],
        [
            pltpu.VMEM((D, D), bf16),
            pltpu.VMEM((D, D), bf16),
            pltpu.VMEM((D, 3 * D), bf16),
            pltpu.SemaphoreType.DMA((3 * blocks_of(square) + blocks_of(joint),)),
        ],
        14 * rows * D * D,
        25e6,
    )


def teacher_ffn(real_rows, pad_rows, images, mid, weights, biases, vectors, sums):
    rows, block = mid.shape[0], images * pad_rows
    items = [biases, vectors, *weights]
    wholes = [(item, whole_spec(item.shape)) for item in items]
    last = [] if sums is None else [(sums, row_spec(block, D))]
    return call(
        functools.partial(teacher_ffn_kernel, real_rows, pad_rows, sums is not None),
        "teacher_ffn",
        (rows // block,),
        [(mid, row_spec(block, D))] + wholes + last,
        [(((rows, D), f32), row_spec(block, D))],
        [],
        16 * rows * D * D,
        15e6,
    )[0]


def student_ffn(pad_rows, images, table, scale, mid, targets, marks, vectors, expand, contract):
    rows, block = mid.shape[0], images * pad_rows
    outs = [(7 * D // 2, bf16), (7 * D // 2, bf16), (6 * D, bf16), (D, f32)]
    return call(
        functools.partial(student_ffn_kernel, expand[1], contract[1]),
        "student_ffn",
        (rows // block,),
        [
            (table, smem_spec),
            (scale, smem_spec),
            (mid, row_spec(block, D)),
            (targets, row_spec(block, D)),
            (marks, row_spec(block, 128)),
            (vectors, whole_spec(vectors.shape)),
        ]
        + [(array, any_spec) for array in (*expand[0], *contract[0])],
        [(((rows, width), kind), row_spec(block, width)) for width, kind in outs]
        + [(((16, D), f32), whole_spec((16, D)))],
        [
            pltpu.VMEM((D, 4 * D), bf16),
            pltpu.VMEM((4 * D, D), bf16),
            pltpu.VMEM((D, D), bf16),
            pltpu.VMEM((block, 4 * D), f32),
            pltpu.VMEM((block, D), bf16),
            pltpu.SemaphoreType.DMA((2 * blocks_of(expand) + blocks_of(contract),)),
        ],
        36 * rows * D * D,
        40e6,
    )


def attend_back(
    real_rows, pad_rows, images, table, dmid, joint, start, marks, vectors, square, qkv
):
    rows, block = dmid.shape[0], images * pad_rows
    arrays, metas = square[0] + qkv[0], (square[1], qkv[1])
    return call(
        functools.partial(attend_back_kernel, real_rows, pad_rows, *metas),
        "attend_back",
        (rows // block,),
        [
            (table, smem_spec),
            (dmid, row_spec(block, D)),
            (joint, row_spec(block, 3 * D)),
            (start, row_spec(block, D)),
            (marks, row_spec(block, 128)),
            (vectors, whole_spec(vectors.shape)),
        ]
        + [(array, any_spec) for array in arrays],
        [(((rows, 2 * D), bf16), row_spec(block, 2 * D))] * 2
        + [(((16, D), f32), whole_spec((16, D)))],
        [
            pltpu.VMEM((D, D), bf16),
            pltpu.VMEM((D, 3 * D), bf16),
            pltpu.VMEM((block, D), bf16),
            pltpu.VMEM((block, 3 * D), bf16),
            pltpu.VMEM((block, D), bf16),
            pltpu.SemaphoreType.DMA((2 * blocks_of(square) + blocks_of(qkv),)),
        ],
        20 * rows * D * D,
        25e6,
    )


def split_blocks(grads, members, y_first, place, own_y):
    top = jnp.max(jnp.abs(grads), axis=0, keepdims=True)
    rows = grads.shape[0] // members
    rels = jnp.array([rel for rel, _ in relative_places(members, False)])
    blocks = jnp.take(grads.reshape(members, rows, -1), rels ^ place, axis=0)
    if y_first:
        blocks = blocks.reshape(members, 2, rows // 2, -1)
        blocks = jnp.take(blocks, jnp.arange(2) ^ own_y, axis=1).swapaxes(0, 1)
    blocks = blocks.reshape(grads.shape)
    keep, sent = jnp.split(blocks, 2)
    exponent = column_exponents(top)
    tail = jnp.broadcast_to(exponent, (16, exponent.shape[1]))
    return keep, jnp.concatenate([sent * power_of_two(exponent), tail], 0), top


def half_outs(width, columns, index):
    heights = (D // 2, D // 2 + 16, 8)
    return [(((height, columns), f32), pl.BlockSpec((height, width), index)) for height in heights]


def weight_grad(name, table, members, y_first, steps, sides, own_b, peer_b):
    rows = own_b[0].shape[0]
    wide = D // 2
    relative = (D // members) % 32 == 0
    ins = [(table, None)]
    for own, peer, index, _ in sides:
        spec = pl.BlockSpec((rows, D), lambda j, _, index=index: (0, index(j)))
        ins += [(own, spec), (peer, spec)]
    for item, index in (own_b, peer_b):
        ins.append((item, pl.BlockSpec((rows, wide), lambda j, _, index=index: (0, index(j)))))
    if relative:
        outs = half_outs(wide, steps * wide, lambda j, _: (0, j))
    else:
        outs = [(((D, steps * wide), f32), pl.BlockSpec((D, wide), lambda j, _: (0, j)))]
    results = call(
        functools.partial(
            weight_grad_kernel, members, y_first, relative, tuple(side[3] for side in sides)
        ),
        name,
        (steps,),
        ins,
        outs,
        [pltpu.VMEM((2, D, rows), bf16), pltpu.VMEM((D, wide), f32)],
        4 * rows * D * wide * steps,
        4 * D * wide * steps + 4 * rows * (D + wide * steps),
        prefetch=1,
    )
    if relative:
        return results
    return split_blocks(results[0], members, y_first, table[2], table[1])


def contract_grad(table, members, keep, two, two_peer):
    rows = two.shape[0]
    wide = D // 2
    shard = D // members
    relative = shard % 32 == 0
    steps = 4 * D // wide
    column = lambda item, index: (item, pl.BlockSpec((rows, wide), lambda i, _: (0, index)))
    moving = lambda item: (
        item,
        pl.BlockSpec((rows, wide), lambda i, _: (0, 2 + jnp.minimum(i, steps - 1))),
    )
    left = pl.BlockSpec((rows, D), lambda i, _: (0, 0))
    if relative:
        assert 4 * shard == wide
        outs = half_outs(5 * wide, 5 * wide, lambda i, _: (0, 0))
        plain = (D, 5 * wide)
    else:
        outs = [
            (((wide, 4 * D), f32), pl.BlockSpec((wide, wide), lambda i, _: (0, jnp.minimum(i, steps - 1)))),
            (((D, wide), f32), pl.BlockSpec((D, wide), lambda i, _: (0, 0))),
        ]
        plain = (8, 128)
    results = call(
        functools.partial(contract_grad_kernel, members, relative),
        "grad_contract",
        (steps + 1,),
        [(table, None), column(keep, 5), column(two_peer, 10), moving(two), moving(two_peer)]
        + [(two, left), (two_peer, left), column(keep, 4), column(two_peer, 11)],
        outs,
        [pltpu.VMEM((2, D, rows), bf16), pltpu.VMEM(plain, f32)],
        16 * rows * D * wide,
        16 * D * wide + 16 * rows * D,
        prefetch=1,
    )
    if relative:
        return results
    blocks = results[0].reshape(wide // shard, shard, members, 4 * shard)
    blocks = blocks.transpose(2, 1, 0, 3).reshape(D, -1)
    whole = jnp.concatenate([blocks, results[1]], 1)
    return split_blocks(whole, members, True, table[2], table[1])


def adam(name, pick, table, numbers, masters, block, index, steps, sums):
    spec = pl.BlockSpec(block, lambda j, *_: index(j))
    ins = [(table, smem_spec), (numbers, smem_spec)] + [(item, spec) for item in masters]
    ins += [(item, pl.BlockSpec(shape, lambda j, *_, at=at: at(j))) for item, shape, at in sums]
    size = masters[0].size
    return call(
        functools.partial(adam_kernel, pick),
        name,
        (steps,),
        ins,
        [((masters[0].shape, f32), spec)] * 3,
        [],
        10 * size,
        32 * size,
    )


def after(value, *others):
    return lax.optimization_barrier((value, *others))[0]


def swap(values, bit):
    total = lax.axis_size("batch") * lax.axis_size("mlp")
    return lax.ppermute(values, ("batch", "mlp"), [(i, i ^ bit) for i in range(total)])


def batch_swap(values, bit):
    return swap(values, lax.axis_size("mlp") << bit)


def bit_of(axis, bit):
    return (lax.axis_index(axis) >> bit) & 1


def all_sum(values, bits):
    for bit in bits:
        values = values + swap(values, 1 << bit)
    return values


def half_of(values, which, axis):
    width = values.shape[axis] // 2
    return lax.dynamic_slice_in_dim(values, which * width, width, axis)


def in_order(first, second, bit_value, axis):
    return jnp.where(
        bit_value == 0,
        jnp.concatenate([first, second], axis),
        jnp.concatenate([second, first], axis),
    )


def natural_rows(blocks, order):
    count = len(order)
    full = blocks.reshape((2,) * count + blocks.shape[1:])
    for place in range(count):
        flip = bit_of("batch", order[count - 1 - place])
        full = jnp.where(flip == 0, full, jnp.flip(full, place))
    source = [count - 1 - order.index(bit) for bit in reversed(range(count))]
    full = full.transpose(source + [count, count + 1])
    return full.reshape(1, -1, full.shape[-1])


def blocks_group(held, last, order, row):
    members = 1 << len(order)
    height = held.shape[1]
    if height % 16 != 0:
        return whole_group(natural_rows(jnp.concatenate([held, last], 0), order), row)
    entries = [
        lax.axis_index("batch") ^ sum(((p >> j) & 1) << bit for j, bit in enumerate(order))
        for p in range(members)
    ]
    arrays = [held, last, swap(held, 1), swap(last, 1)]
    metas = [
        (0, height, height, row + part * (members // 2), near)
        for near in (True, False)
        for part in (0, 1)
    ]
    return (arrays, tuple(metas)), entries


def sides_group(own, other, members, row):
    height = own.shape[0] // members
    own, other = (item.reshape(members, height, -1) for item in (own, other))
    if height % 16 != 0:
        both = in_order(own[:, None], other[:, None], bit_of("mlp", 1), 1)
        return whole_group(both.reshape(1, 2 * members * height, -1), row)[0]
    arrays = [own, other, swap(own, 1), swap(other, 1)]
    metas = [(side, 2 * height, height, row, near) for near in (True, False) for side in (1, 2)]
    return arrays, tuple(metas)


def whole_group(near, row):
    metas = tuple((0, 0, near.shape[1], row, side) for side in (True, False))
    return ([near, swap(near, 1)], metas), []


def power_of_two(exponent):
    size = jnp.abs(exponent).astype(jnp.int32)
    result = jnp.ones_like(exponent)
    for bit in range(7):
        factor = jnp.where(exponent > 0, 2.0 ** (1 << bit) if bit < 7 else 1.0, 2.0 ** -(1 << bit))
        result = jnp.where((size >> bit) & 1 == 1, result * factor, result)
    return result


def low_half(values):
    return lax.reduce_precision(values, 5, 10).astype(jnp.float16)


def low_half(values):
    return lax.reduce_precision(values, 5, 10).astype(jnp.float16)


def packed(values, exponent):
    tail = jnp.broadcast_to(exponent, (16, exponent.shape[1]))
    return low_half(jnp.concatenate([values * power_of_two(exponent), tail], 0))


class Reduction:
    def __init__(self, blocks, order, y_first):
        self.keep, sent, top = blocks
        self.bound = top[:1]
        self.hops = (["y"] if y_first else []) + list(order) + ["last"]
        self.y_first = y_first
        self.sent = low_half(sent)

    def receive(self, *gates):
        bit = self.hops.pop(0)
        other = swap(self.sent, 2) if bit in ("y", "last") else batch_swap(self.sent, bit)
        other = after(other, *gates)
        rows = other.shape[0] - 16
        exponent = other[-1:].astype(f32)
        factor = power_of_two(-exponent)
        if bit == "last":
            own = self.sent[:rows].astype(f32) * power_of_two(-self.sent[-1:].astype(f32))
            other = other[:rows].astype(f32) * factor
            if self.y_first:
                self.sums = in_order(own, other, bit_of("mlp", 1), 0)
            else:
                self.sums = own + other
            return self
        self.bound = self.bound + power_of_two(15.0 - exponent)
        half = rows // 2 if len(self.hops) > 1 else 0
        sums = self.keep[half:] + other[half:rows].astype(f32) * factor
        self.sent = packed(sums, column_exponents(self.bound))
        if half:
            self.keep = self.keep[:half] + other[:half].astype(f32) * factor
        return self


def adam_update(master, first, second, gradient, step_rate, weight_decay):
    moment = beta_first * first + (1.0 - beta_first) * gradient
    variance = beta_second * second + (1.0 - beta_second) * gradient * gradient
    corrected = moment / (1.0 - beta_first**STEP)
    scaled = variance / (1.0 - beta_second**STEP)
    updated = master - step_rate * (
        corrected / (jnp.sqrt(scaled) + adam_eps) + weight_decay * master
    )
    return (moment, variance, updated)


def on_device(
    patches,
    mask,
    student_square,
    student_qkv,
    student_expand,
    student_contract,
    student_vectors,
    first_square,
    first_qkv,
    first_expand,
    first_contract,
    first_vectors,
    second_square,
    second_qkv,
    second_expand,
    second_contract,
    second_vectors,
    teacher_square,
    teacher_qkv,
    teacher_expand,
    teacher_contract,
    teacher_vectors,
):
    members = lax.axis_size("batch")
    count = members.bit_length() - 1
    mlp_bits = lax.axis_size("mlp").bit_length() - 1
    near = list(range(count))
    far = near[::-1]
    batch_bits = range(mlp_bits, mlp_bits + count)
    shard_rows = D // members
    core, own_y = bit_of("mlp", 0), bit_of("mlp", 1)
    place = lax.axis_index("batch")
    group, real_rows = mask.shape
    pad_rows = -(-real_rows // 16) * 16
    half = D // 2

    pad = ((0, 0), (0, pad_rows - real_rows))
    x = jnp.pad(patches, pad + ((0, 0),)).reshape(-1, D)
    marks = jnp.pad(mask.astype(f32), pad).reshape(-1)
    wide_marks = jnp.broadcast_to(marks[:, None], (marks.shape[0], 128))

    square_held = jnp.concatenate(
        [half_of(student_square[i], core, 1) for i in range(2)]
        + [lax.dynamic_slice_in_dim(student_qkv, core * 3 * half, half, 1)],
        1,
    ).astype(bf16)[None]
    qkv_held = lax.dynamic_slice_in_dim(student_qkv, core * 3 * half + half, D, 1)
    qkv_held = qkv_held.astype(bf16)[None]
    expand_held = jnp.concatenate(
        [half_of(half_of(item, core, 1), own_y, 0) for item in (student_expand, student_square[2])],
        1,
    )
    expand_own = lax.all_gather(expand_held.astype(bf16), "batch", axis=0, tiled=True)
    contract_near = lax.all_gather(
        half_of(student_contract, core, 1).astype(bf16), "batch", axis=0, tiled=True
    )
    teacher_own = jnp.concatenate([after(teacher_expand, square_held, qkv_held), teacher_contract], 1)
    teacher_y = swap(teacher_own, 2)
    teacher_core = swap(teacher_own, 1)
    low_vectors = lax.reduce_precision(student_vectors, 8, 7)
    small = lax.dynamic_update_slice(
        jnp.zeros((low_vectors.shape[0], D), f32), low_vectors, (0, place * shard_rows)
    )
    small = jnp.concatenate([small, jnp.full((1, D), jnp.sum(marks))], 0)

    images = min(group, 2)
    sizes = (real_rows, pad_rows, images)
    teacher_weights = (teacher_square, teacher_qkv, teacher_vectors)
    own = lax.axis_index("mlp")
    biases = jnp.concatenate(
        [lax.dynamic_slice_in_dim(teacher_vectors, 8 + (own ^ part), 1, 0) for part in range(4)]
    )
    tmid, runs, tsum, done = None, 0, None, ()
    square_order, qkv_order = far, near[:1] + far[:-1]
    for hop in range(count):
        sends = lax.optimization_barrier((square_held, qkv_held, small, *done))[:3]
        square_held, qkv_held, small = sends
        square_last = batch_swap(square_held, square_order[hop])
        qkv_last = batch_swap(qkv_held, qkv_order[hop])
        small_last = batch_swap(small, near[hop])
        if runs < group // images:
            tmid = attend_teacher(*sizes, runs, tmid, after(x, *sends), *teacher_weights)
            runs += 1
            done = (tmid,)
        elif tsum is None:
            tsum = teacher_ffn(
                *sizes,
                after(tmid, *sends),
                (teacher_own, teacher_core),
                biases[:2],
                teacher_vectors,
                None,
            )
            done = (tsum,)
        if hop + 1 < count:
            square_held = jnp.concatenate([square_held, square_last], 0)
            qkv_held = jnp.concatenate([qkv_held, qkv_last], 0)
        small = small + small_last
    vectors = small[:-1]
    square_held, qkv_held, square_last, qkv_last = lax.optimization_barrier(
        (square_held, qkv_held, square_last, qkv_last, *done, teacher_y)
    )[:4]
    square, square_rows = blocks_group(square_held, square_last, square_order, 3)
    qkv, qkv_rows = blocks_group(qkv_held, qkv_last, qkv_order, 3 + len(square_rows))
    entries = [core, own_y, place] + square_rows + qkv_rows + list(range(members))
    table = jnp.stack([jnp.asarray(entry, jnp.int32) for entry in entries])

    masked_count = all_sum(after(small, *done)[-1:, :128], range(mlp_bits))
    expand_y = swap(after(expand_own, masked_count), 2)
    start, mid, joint, act = attend_student(
        *sizes, table, after(x, tsum, masked_count, expand_own), wide_marks, vectors, square, qkv
    )
    masked_count = masked_count[0, 0]
    mid, expand_y = lax.optimization_barrier((mid, expand_y))
    teacher_far = swap(after(teacher_y, mid), 1)
    expand = sides_group(after(expand_own, mid), expand_y, members, 3 + len(square_rows + qkv_rows))
    contract, _ = whole_group(after(contract_near, mid)[None], 0)
    act_peer = swap(after(act, mid), 1)
    targets = teacher_ffn(
        *sizes,
        after(tmid, mid, expand_y),
        (teacher_y, teacher_far),
        biases[2:],
        teacher_vectors,
        tsum,
    )
    scale = (2.0 / (masked_count * D)).reshape(1)
    keep, one, two, dmid, ffn_sums = student_ffn(
        pad_rows, images, table, scale, after(mid, act_peer), targets, wide_marks, vectors, expand, contract
    )
    one_peer = swap(one, 1)
    two_peer = swap(after(two, one_peer), 1)

    blocks = weight_grad(
        "grad_expand",
        table,
        members,
        False,
        5,
        [
            (one, one_peer, lambda j: 0, (0,)),
            (act, act_peer, lambda j: 0, (4,)),
        ],
        (keep, lambda j: jnp.where(j == 4, 6, j)),
        (one_peer, lambda j: jnp.where(j == 4, 6, j + 2)),
    )
    to_expand = Reduction(blocks, near, False)
    blocks = contract_grad(table, members, keep, two, after(two_peer, to_expand.sent))
    to_contract = Reduction(blocks, near, True)
    keep3, send3, att_sums = attend_back(
        *sizes,
        table,
        after(dmid, to_contract.sent),
        joint,
        start,
        wide_marks,
        vectors,
        square,
        qkv,
    )
    send3_peer = swap(send3, 1)
    to_expand.receive(att_sums)
    to_contract.receive()

    total = jnp.concatenate([ffn_sums[:12], att_sums[:6]], 0)
    total_bits = list(range(mlp_bits + count))

    def total_hop(*gates):
        nonlocal total
        if total_bits:
            total = after(total, *gates)
            total = total + swap(total, 1 << total_bits.pop(0))

    total_hop(to_expand.sent, to_contract.sent)
    blocks = weight_grad(
        "grad_joint",
        table,
        members,
        False,
        2,
        [(act, act_peer, lambda j: 1, (0,))],
        (keep3, lambda j: j),
        (after(send3_peer, to_expand.sent, to_contract.sent), lambda j: j),
    )
    to_first = Reduction(blocks, near, False)
    to_expand.receive(to_first.sent)
    to_contract.receive(to_first.sent)
    total_hop(to_first.sent)
    blocks = weight_grad(
        "grad_embed",
        table,
        members,
        True,
        2,
        [(act, act_peer, lambda j: 1 + j, (0, 1))],
        (keep3, lambda j: j + 2),
        (after(send3_peer, to_first.sent, to_expand.sent, to_contract.sent), lambda j: j + 2),
    )
    to_second = Reduction(blocks, near, True)
    to_first.receive(to_second.sent)
    gates = (to_first.sent,)
    to_expand.receive(*gates)
    to_contract.receive(*gates)
    total_hop(*gates)
    to_second.receive()
    gates = (to_second.sent,)
    moving = [to_second, to_first, to_contract, to_expand]
    while moving:
        total_hop(*gates)
        for item in list(moving):
            item.receive(*gates)
            if not item.hops:
                moving.remove(item)
        gates = (moving[0].sent,) if moving else ()
    while total_bits:
        total_hop()
    ffn_total, att_total = total[:12], total[12:]

    own_sums = [item.sums for item in (to_expand, to_contract, to_first, to_second)]
    vector_total = jnp.concatenate(
        [
            att_total[5:6],
            att_total[4:5],
            att_total[2:4],
            att_total[0:2],
            ffn_total[11:12],
            ffn_total[9:11],
            ffn_total[5:9],
            ffn_total[4:5],
            ffn_total[2:4],
            ffn_total[1:2],
        ]
    )
    loss_sum = jnp.sum(ffn_total[0])
    vector_grad = lax.dynamic_slice_in_dim(vector_total, place * shard_rows, shard_rows, 1)
    squares = 0.5 * jnp.sum(vector_grad * vector_grad)
    for member in own_sums:
        squares = squares + jnp.sum(member * member)
    squares = all_sum(jnp.full((1, 128), squares), [0, *batch_bits])
    grad_norm = jnp.sqrt(squares[0, 0])
    factor = clip_bound / jnp.maximum(grad_norm, clip_bound)

    pairs = [(item, swap(item, 1)) for item in own_sums]
    numbers = factor.reshape(1)

    def picked(is_own, own_ref, peer_ref):
        return jnp.where(is_own, own_ref[...], peer_ref[...])

    def pick_square(step, core_of, numbers_ref, refs):
        sides = []
        for near in (True, False):
            parts = [refs[2 * i + (0 if near else 1)][...] for i in range(3)]
            side = jnp.where(step == 0, parts[0], jnp.where(step == 1, parts[1], parts[2]))
            sides.append(side)
        left = jnp.where(core_of == 0, sides[0], sides[1])
        right = jnp.where(core_of == 0, sides[1], sides[0])
        return (jnp.concatenate([left, right], 1) * numbers_ref[0])[None]

    def pick_joint(step, core_of, numbers_ref, refs):
        parts = [picked(step == core_of, *refs[2 * i : 2 * i + 2]) for i in range(2)]
        return jnp.concatenate(parts, 1) * numbers_ref[0]

    def pick_expand(step, core_of, numbers_ref, refs):
        return picked(step == core_of, *refs) * numbers_ref[0]

    def pick_contract(step, core_of, numbers_ref, refs):
        grads = picked(step == core_of, *refs)
        if grads.shape[0] != 4 * shard_rows:
            parts = half // shard_rows
            grads = [grads[:, i * 4 * shard_rows : (i + 1) * 4 * shard_rows] for i in range(parts)]
            grads = jnp.concatenate(grads, 0).T
        return grads * numbers_ref[0]

    def pieces(index, at, width=half):
        return [(item, (shard_rows, width), at) for item in pairs[index]]

    square_results = adam(
        "adam_square",
        pick_square,
        table,
        numbers,
        (student_square, first_square, second_square),
        (1, shard_rows, D),
        lambda j: (j, 0, 0),
        3,
        pieces(3, lambda j: (0, 1)) + pieces(0, lambda j: (0, 4)) + pieces(1, lambda j: (0, 4)),
    )
    qkv_results = adam(
        "adam_qkv",
        pick_joint,
        table,
        numbers,
        (student_qkv, first_qkv, second_qkv),
        (shard_rows, 3 * half),
        lambda j: (0, j),
        2,
        pieces(2, lambda j: (0, 0), 2 * half) + pieces(3, lambda j: (0, 0)),
    )
    expand_results = adam(
        "adam_expand",
        pick_expand,
        table,
        numbers,
        (student_expand, first_expand, second_expand),
        (shard_rows, 4 * half),
        lambda j: (0, j),
        2,
        pieces(0, lambda j: (0, 0), 4 * half),
    )
    if 4 * shard_rows == half:
        contract_pieces = pieces(1, lambda j: (0, 0), 4 * half)
    else:
        contract_pieces = []
        for item in pairs[1]:
            item = item[:, : 4 * half].reshape(shard_rows, half // shard_rows, 4 * shard_rows)
            item = item.swapaxes(0, 1).reshape(half, 4 * shard_rows).T
            contract_pieces.append((item, item.shape, lambda j: (0, 0)))
    contract_results = adam(
        "adam_contract",
        pick_contract,
        table,
        numbers,
        (student_contract, first_contract, second_contract),
        (4 * shard_rows, half),
        lambda j: (0, j),
        2,
        contract_pieces,
    )
    vector_results = adam_update(
        student_vectors, first_vectors, second_vectors, vector_grad * factor, rate_vector, 0.0
    )
    return (
        loss_sum,
        masked_count,
        grad_norm,
        *square_results,
        *qkv_results,
        *expand_results,
        *contract_results,
        *vector_results,
    )


def solution(mesh):
    return jax.shard_map(
        on_device,
        mesh=mesh,
        in_specs=(
            P(("batch", "mlp"), None, None),
            P(("batch", "mlp"), None),
            P(None, "batch", None),
            P("batch", None),
            P("batch", None),
            P("batch", None),
            P(None, "batch"),
            P(None, "batch", None),
            P("batch", None),
            P("batch", None),
            P("batch", None),
            P(None, "batch"),
            P(None, "batch", None),
            P("batch", None),
            P("batch", None),
            P("batch", None),
            P(None, "batch"),
            P(),
            P(),
            P(None, "mlp"),
            P("mlp", None),
            P(),
        ),
        out_specs=(
            P(),
            P(),
            P(),
            P(None, "batch", None),
            P(None, "batch", None),
            P(None, "batch", None),
            P("batch", None),
            P("batch", None),
            P("batch", None),
            P("batch", None),
            P("batch", None),
            P("batch", None),
            P("batch", None),
            P("batch", None),
            P("batch", None),
            P(None, "batch"),
            P(None, "batch"),
            P(None, "batch"),
        ),
        check_vma=False,
    )
```

```python
import functools

import jax
import jax.numpy as jnp
from jax import lax
from jax.experimental import pallas as pl
from jax.experimental.pallas import tpu as pltpu
from jax.sharding import PartitionSpec as P

D = 768
HEAD_DIM = 64
PAIR = 2 * HEAD_DIM
UNROLL = 3
STEP = 10


norm_eps = 1e-06
inst_eps = 1e-05
clip_bound = 0.001
rate_matrix = 0.05
rate_vector = 0.5
decay_matrix = 0.05
beta_first = 0.9
beta_second = 0.999
adam_eps = 1e-08
f32 = jnp.float32
bf16 = jnp.bfloat16


def mm(left, right):
    return lax.dot_general(left, right, (((1,), (0,)), ((), ())), preferred_element_type=f32)


def mm_nt(left, right):
    return lax.dot_general(left, right, (((1,), (1,)), ((), ())), preferred_element_type=f32)


def mm_tn(left, right):
    return lax.dot_general(left, right, (((0,), (0,)), ((), ())), preferred_element_type=f32)


def normed_rows(values):
    centred = values - jnp.mean(values, axis=-1, keepdims=True)
    variance = jnp.mean(centred * centred, axis=-1, keepdims=True)
    scale = lax.rsqrt(variance + norm_eps)
    return centred * scale, scale


def norm_back(xhat, scale, gain, grads):
    scaled = grads * gain
    mean_one = jnp.mean(scaled, axis=-1, keepdims=True)
    mean_two = jnp.mean(scaled * xhat, axis=-1, keepdims=True)
    back = scale * (scaled - mean_one - xhat * mean_two)
    return back, total_rows(grads * xhat), total_rows(grads)


def piece_copies(table_ref, semaphores, first, pieces):
    core, own_y = table_ref[0], table_ref[1]
    copies = []
    for ref, (side, unit, height, row, near), lanes, target, offset in pieces:
        width = lanes[1] - lanes[0]
        column = (core if near else 1 - core) * (target.shape[1] // 2) + offset
        column = pl.multiple_of(column, 128)
        base = (0, own_y * height, (1 - own_y) * height)[side]
        for block in range(ref.shape[0]):
            place = 0 if unit == 0 else pl.multiple_of(table_ref[row + block] * unit + base, 16)
            copies.append(
                pltpu.make_async_copy(
                    ref.at[block, :, pl.ds(lanes[0], width)],
                    target.at[pl.ds(place, height), pl.ds(column, width)],
                    semaphores.at[first + len(copies)],
                )
            )
    return copies


def total_rows(values):
    return jnp.sum(values, axis=0, keepdims=True)


def head_masks(rows):
    lane = lax.broadcasted_iota(jnp.int32, (rows, PAIR), 1)
    return lane < HEAD_DIM


def stacked(values, low):
    zero = jnp.zeros_like(values)
    return jnp.concatenate([jnp.where(low, values, zero), jnp.where(low, zero, values)], axis=0)


def pair_probs(stack, keys, real_rows):
    scores = mm_nt(stack, keys)
    column = lax.broadcasted_iota(jnp.int32, scores.shape, 1)
    scores = jnp.where(column < real_rows, scores, -1e30)
    shifted = jnp.exp(scores - jnp.max(scores, axis=-1, keepdims=True))
    return shifted * (1.0 / jnp.sum(shifted, axis=-1, keepdims=True))


def attend_block(is_student, real_rows, pad_rows, x_ref, marks_ref, weights, vec_ref, outs, waits):
    w0_ref, wj_ref, w1_ref = weights
    start_ref, mid_ref, joint_ref, act_ref = outs
    at = (lambda student, teacher: student if is_student else teacher)
    vec = lambda row: vec_ref[row : row + 1, :]
    block = x_ref.shape[0]
    if is_student:
        waits[0]()
    start = mm(x_ref[...], w0_ref[...]) + vec(0)
    if is_student:
        start = jnp.where(marks_ref[:, :1] > 0, vec(1), start)
    start_ref[...] = start
    xhat, _ = normed_rows(start)
    normed = (xhat * vec(at(2, 1)) + vec(at(3, 2))).astype(bf16)
    if is_student:
        act_ref[:, D : 2 * D] = normed
        act_ref[:, 2 * D :] = x_ref[...]
    biases = (vec(at(4, 3)), None, vec(at(5, 4)))
    if is_student:
        waits[1]()
    for part in range(3):
        cols = slice(part * D, (part + 1) * D)
        mixed = mm(normed, wj_ref[:, cols])
        if biases[part] is not None:
            mixed = mixed + biases[part]
        joint_ref[:, cols] = mixed.astype(bf16)
    low = head_masks(pad_rows)

    def one_pair(step, carry):
        image = step // (D // PAIR)
        col = pl.multiple_of((step % (D // PAIR)) * PAIR, PAIR)
        rows = pl.ds(pl.multiple_of(image * pad_rows, 16), pad_rows)
        queries = joint_ref[rows, pl.ds(col, PAIR)] * HEAD_DIM ** (-0.5)
        keys = joint_ref[rows, pl.ds(col + D, PAIR)]
        values = joint_ref[rows, pl.ds(col + 2 * D, PAIR)]
        probs = pair_probs(stacked(queries.astype(bf16), low), keys, real_rows).astype(bf16)
        mixed = mm(probs, values)
        act_ref[rows, pl.ds(col, PAIR)] = jnp.where(
            low, mixed[:pad_rows], mixed[pad_rows:]
        ).astype(bf16)
        return carry

    lax.fori_loop(0, (block // pad_rows) * (D // PAIR), one_pair, 0, unroll=2 * UNROLL)
    attended = act_ref[:, :D]
    if is_student:
        waits[2]()
    mid_ref[...] = start_ref[...] + mm(attended, w1_ref[...]) + vec(at(6, 5))


def clear_at_first(*refs):
    @pl.when(pl.program_id(0) == 0)
    def _():
        for ref in refs:
            ref[...] = jnp.zeros_like(ref)


def place_at_first(table_ref, semaphores, *groups):
    all_copies, count = [], 0
    for pieces in groups:
        all_copies.append(piece_copies(table_ref, semaphores, count, pieces))
        count += len(all_copies[-1])

    @pl.when(pl.program_id(0) == 0)
    def _():
        for copies in all_copies:
            for copy in copies:
                copy.start()

    def wait_for(copies):
        @pl.when(pl.program_id(0) == 0)
        def _():
            for copy in copies:
                copy.wait()

    return [functools.partial(wait_for, copies) for copies in all_copies]


def attend_teacher_kernel(real_rows, pad_rows, *refs):
    x_ref, w0_ref, wj_ref, w1_ref, vec_ref = refs[:5]
    mid_ref, joint_ref, att_ref = refs[-3:]
    attend_block(
        False,
        real_rows,
        pad_rows,
        x_ref,
        None,
        (w0_ref, wj_ref, w1_ref),
        vec_ref,
        (mid_ref, mid_ref, joint_ref, att_ref),
        None,
    )


def attend_student_kernel(real_rows, pad_rows, metas, joint_metas, *refs):
    (table_ref, x_ref, marks_ref, vec_ref) = refs[:4]
    count = len(metas)
    piece_refs, joint_refs = refs[4 : 4 + count], refs[4 + count : 4 + 2 * count]
    (start_ref, mid_ref, joint_ref, act_ref) = refs[4 + 2 * count : 8 + 2 * count]
    (w0_ref, w1_ref, wj_ref, semaphores) = refs[8 + 2 * count :]
    joint_pieces = section(piece_refs, metas, SQUARE_LANES[2], wj_ref)
    joint_pieces += section(joint_refs, joint_metas, (0, D), wj_ref, D // 2)
    waits = place_at_first(
        table_ref,
        semaphores,
        section(piece_refs, metas, SQUARE_LANES[0], w0_ref),
        joint_pieces,
        section(piece_refs, metas, SQUARE_LANES[1], w1_ref),
    )
    attend_block(
        True,
        real_rows,
        pad_rows,
        x_ref,
        marks_ref,
        (w0_ref, wj_ref, w1_ref),
        vec_ref,
        (start_ref, mid_ref, joint_ref, act_ref),
        waits,
    )


def gelu_half(values):
    return 0.5 * (1.0 + lax.erf(values * 0.7071067811865476))


def teacher_ffn_kernel(real_rows, pad_rows, is_last, *refs):
    mid_ref, bias_ref, vec_ref = refs[:3]
    parts = bias_ref.shape[0]
    rest = refs[3 + parts :]
    mid = mid_ref[...]
    xhat, _ = normed_rows(mid)
    normed = (xhat * vec_ref[6:7, :] + vec_ref[7:8, :]).astype(bf16)
    total = rest[0][...] if is_last else None
    for part, both_ref in enumerate(refs[3 : 3 + parts]):
        pre = mm(normed, both_ref[:, :D]) + bias_ref[part : part + 1, :]
        hidden = (pre * gelu_half(pre)).astype(bf16)
        piece = mm(hidden, both_ref[:, D:])
        total = piece if total is None else total + piece
    out_ref = rest[-1]
    if not is_last:
        out_ref[...] = total
        return
    total = total + vec_ref[12:13, :]
    valid = lax.broadcasted_iota(jnp.int32, (pad_rows, D), 0) < real_rows
    for image in range(mid_ref.shape[0] // pad_rows):
        rows = slice(image * pad_rows, (image + 1) * pad_rows)
        result = None
        for values in (mid[rows], total[rows]):
            mean = total_rows(jnp.where(valid, values, 0.0)) / real_rows
            centred = values - mean
            variance = total_rows(jnp.where(valid, centred * centred, 0.0)) / real_rows
            normal = centred * lax.rsqrt(variance + inst_eps)
            result = normal if result is None else result + normal
        out_ref[rows, :] = 0.5 * result


def student_ffn_kernel(expand_metas, contract_metas, *refs):
    (table_ref, scale_ref, mid_ref, target_ref, marks_ref, vec_ref) = refs[:6]
    counts = (len(expand_metas), len(contract_metas))
    expand_refs, contract_refs = refs[6 : 6 + counts[0]], refs[6 + counts[0] : 6 + sum(counts)]
    (keep_ref, one_ref, two_ref, dmid_ref, sum_ref) = refs[6 + sum(counts) : 11 + sum(counts)]
    (we_ref, wc_ref, wh_ref, slope_ref, half_ref, semaphores) = refs[11 + sum(counts) :]
    clear_at_first(sum_ref)
    expand_wait, contract_wait, head_wait = place_at_first(
        table_ref,
        semaphores,
        section(expand_refs, expand_metas, (0, 2 * D), we_ref),
        section(contract_refs, contract_metas, (0, D // 2), wc_ref),
        section(expand_refs, expand_metas, (2 * D, 5 * D // 2), wh_ref),
    )
    core = table_ref[0]

    def add(row, values):
        sum_ref[pl.ds(row, 1), :] += values

    def add_grad(row, grads):
        add(row, total_rows(grads.astype(f32)))

    def halves(keep_cols, send_ref, send_cols, grads):
        half_ref[...] = grads
        width = D // 2
        keep_ref[:, keep_cols : keep_cols + width] = half_ref[
            :, pl.ds(pl.multiple_of(core * width, 128), width)
        ]
        send_ref[:, send_cols : send_cols + width] = half_ref[
            :, pl.ds(pl.multiple_of((1 - core) * width, 128), width)
        ]

    vec = lambda row: vec_ref[row : row + 1, :]
    mid = mid_ref[...]
    xhat2, scale2 = normed_rows(mid)
    n2 = (xhat2 * vec(7) + vec(8)).astype(bf16)
    one_ref[:, :D] = n2
    total = None
    expand_wait()
    for part in range(4):
        cols = slice(part * D, (part + 1) * D)
        pre = mm(n2, we_ref[:, cols]) + vec(9 + part)
        half = gelu_half(pre)
        slope_ref[:, cols] = half + pre * (jnp.exp(-0.5 * pre * pre) * 0.3989422804014327)
        hidden = (pre * half).astype(bf16)
        two_ref[:, (part + 1) * D : (part + 2) * D] = hidden
        if part == 0:
            contract_wait()
        piece = mm(hidden, wc_ref[cols, :])
        total = piece if total is None else total + piece
    final = mid + total + vec(13)
    xhat3, scale3 = normed_rows(final)
    n3 = (xhat3 * vec(14) + vec(15)).astype(bf16)
    two_ref[:, :D] = n3
    head_wait()
    error = marks_ref[:, :1] * (mm(n3, wh_ref[...]) + vec(16) - target_ref[...])
    add(0, total_rows(error * error))
    dpred = (error * scale_ref[0]).astype(bf16)
    halves(2 * D, two_ref, 11 * D // 2, dpred)
    add_grad(1, dpred)
    dfinal, gain3, shift3 = norm_back(xhat3, scale3, vec(14), mm_nt(dpred, wh_ref[...]))
    add(2, gain3)
    add(3, shift3)
    dbranch = dfinal.astype(bf16)
    halves(2 * D + D // 2, two_ref, 5 * D, dbranch)
    add_grad(4, dbranch)
    dn2 = None
    for side in range(2):
        for part in range(2):
            chunk = 2 * (core ^ side) + part
            cols = pl.ds(pl.multiple_of(chunk * D, 128), D)
            dpre = (mm_nt(dbranch, wc_ref[cols, :]) * slope_ref[:, cols]).astype(bf16)
            if side == 0:
                keep_ref[:, part * D : (part + 1) * D] = dpre
            else:
                one_ref[:, (1 + part) * D : (2 + part) * D] = dpre
            add_grad(5 + chunk, dpre)
            piece = mm_nt(dpre, we_ref[:, cols])
            dn2 = piece if dn2 is None else dn2 + piece
    dmid, gain2, shift2 = norm_back(xhat2, scale2, vec(7), dn2)
    add(9, gain2)
    add(10, shift2)
    dmid = dfinal + dmid
    dmid_ref[...] = dmid
    datt = dmid.astype(bf16)
    halves(3 * D, one_ref, 3 * D, datt)
    add(11, total_rows(datt.astype(f32)))


def attend_back_kernel(real_rows, pad_rows, metas, joint_metas, *refs):
    (table_ref, dmid_ref, joint_ref, start_ref, marks_ref, vec_ref) = refs[:6]
    count = len(metas)
    piece_refs, joint_refs = refs[6 : 6 + count], refs[6 + count : 6 + 2 * count]
    (keep_ref, send_ref, sum_ref) = refs[6 + 2 * count : 9 + 2 * count]
    (w1_ref, wj_ref, grad_ref, djoint_ref, half_ref, semaphores) = refs[9 + 2 * count :]
    clear_at_first(sum_ref)
    joint_pieces = section(piece_refs, metas, SQUARE_LANES[2], wj_ref)
    joint_pieces += section(joint_refs, joint_metas, (0, D), wj_ref, D // 2)
    out_wait, joint_wait = place_at_first(
        table_ref, semaphores, section(piece_refs, metas, SQUARE_LANES[1], w1_ref), joint_pieces
    )
    out_wait()
    core = table_ref[0]

    def add(row, values):
        sum_ref[row : row + 1, :] += values

    def halves(column, source_ref, width):
        keep_ref[:, column : column + width] = source_ref[
            :, pl.ds(pl.multiple_of(core * width, 128), width)
        ]
        send_ref[:, column : column + width] = source_ref[
            :, pl.ds(pl.multiple_of((1 - core) * width, 128), width)
        ]

    vec = lambda row: vec_ref[row : row + 1, :]
    block = dmid_ref.shape[0]
    datt = dmid_ref[...].astype(bf16)
    grad_ref[...] = mm_nt(datt, w1_ref[...]).astype(bf16)
    low = head_masks(pad_rows)

    def one_pair(step, carry):
        image = step // (D // PAIR)
        col = pl.multiple_of((step % (D // PAIR)) * PAIR, PAIR)
        rows = pl.ds(pl.multiple_of(image * pad_rows, 16), pad_rows)
        queries = joint_ref[rows, pl.ds(col, PAIR)] * HEAD_DIM ** (-0.5)
        keys = joint_ref[rows, pl.ds(col + D, PAIR)]
        values = joint_ref[rows, pl.ds(col + 2 * D, PAIR)]
        stack = stacked(queries.astype(bf16), low)
        dstack = stacked(grad_ref[rows, pl.ds(col, PAIR)], low)
        probs = pair_probs(stack, keys, real_rows)
        dprobs = mm_nt(dstack, values)
        dvalues = mm_tn(probs.astype(bf16), dstack)
        weighted = probs * dprobs
        dscores = (weighted - probs * jnp.sum(weighted, axis=-1, keepdims=True)).astype(bf16)
        both = mm(dscores, keys) * HEAD_DIM ** (-0.5)
        dqueries = jnp.where(low, both[:pad_rows], both[pad_rows:])
        dkeys = mm_tn(dscores, stack)
        djoint_ref[rows, pl.ds(col, PAIR)] = dqueries.astype(bf16)
        djoint_ref[rows, pl.ds(col + D, PAIR)] = dkeys.astype(bf16)
        djoint_ref[rows, pl.ds(col + 2 * D, PAIR)] = dvalues.astype(bf16)
        return carry

    lax.fori_loop(0, (block // pad_rows) * (D // PAIR), one_pair, 0, unroll=UNROLL)
    halves(0, djoint_ref, 3 * D // 2)
    joint_wait()
    dnormed = None
    for part in range(3):
        cols = slice(part * D, (part + 1) * D)
        grads = djoint_ref[:, cols]
        if part != 1:
            add(part // 2, total_rows(grads.astype(f32)))
        piece = mm_nt(grads, wj_ref[:, cols])
        dnormed = piece if dnormed is None else dnormed + piece
    xhat, scale = normed_rows(start_ref[...])
    dstart, gain, shift = norm_back(xhat, scale, vec(2), dnormed)
    add(2, gain)
    add(3, shift)
    dstart = dstart + dmid_ref[...]
    masked = marks_ref[:, :1] > 0
    add(4, total_rows(jnp.where(masked, dstart, 0.0)))
    dembed = jnp.where(masked, 0.0, dstart).astype(bf16)
    half_ref[...] = dembed
    halves(3 * D // 2, half_ref, D // 2)
    add(5, total_rows(dembed.astype(f32)))


def relative_places(members, y_first):
    count = members.bit_length() - 1
    rels = [sum(((p >> (count - 1 - bit)) & 1) << bit for bit in range(count)) for p in range(members)]
    if y_first:
        return [(rel, side) for side in range(2) for rel in rels]
    return [(rel, None) for rel in rels]


def column_exponents(top):
    return jnp.floor(14.0 - jnp.log(jnp.clip(top, 1e-30, 1e30)) * 1.4426950408889634)


def store_halves(keep_ref, sent_ref, top_ref, table_ref, plain_ref, members, y_first):
    top = jnp.max(jnp.abs(plain_ref[...]), axis=0, keepdims=True)
    top_ref[...] = jnp.broadcast_to(top, top_ref.shape)
    exponent = column_exponents(top)
    factor = jnp.exp2(exponent)
    places = relative_places(members, y_first)
    rows = plain_ref.shape[0] // members
    height = rows // 2 if y_first else rows
    for index, (rel, side) in enumerate(places):
        first = (table_ref[2] ^ rel) * rows
        if y_first:
            first = first + (table_ref[1] ^ side) * height
        block = plain_ref[pl.ds(pl.multiple_of(first, 16), height), :]
        if index < len(places) // 2:
            keep_ref[index * height : (index + 1) * height, :] = block
        else:
            here = (index - len(places) // 2) * height
            sent_ref[here : here + height, :] = block * factor
    half_rows = keep_ref.shape[0]
    sent_ref[half_rows:, :] = jnp.broadcast_to(exponent, (16, exponent.shape[1]))


def weight_grad_kernel(members, y_first, relative, steps_of, *refs):
    table_ref = refs[0]
    sides = refs[1 : 1 + 2 * len(steps_of)]
    b_ref, b_peer_ref = refs[1 + 2 * len(steps_of) : 3 + 2 * len(steps_of)]
    outs, plain_ref = refs[3 + 2 * len(steps_of) : -1], refs[-1]
    step = pl.program_id(0)
    for index, steps in enumerate(steps_of):
        is_side = step == steps[0]
        for other in steps[1:]:
            is_side = is_side | (step == other)

        @pl.when(is_side)
        def _(index=index):
            plain_ref[...] = mm_tn(sides[2 * index][...], b_ref[...]) + mm_tn(
                sides[2 * index + 1][...], b_peer_ref[...]
            )

    if relative:
        store_halves(*outs, table_ref, plain_ref, members, y_first)
    else:
        outs[0][...] = plain_ref[...]


def contract_grad_kernel(members, relative, *refs):
    (table_ref, d_ref, d_peer_ref, h_ref, h_peer_ref) = refs[:5]
    (n_ref, n_peer_ref, b_ref, b_peer_ref) = refs[5:9]
    outs, plain_ref = refs[9:-1], refs[-1]
    step = pl.program_id(0)
    half = D // 2
    shard = D // members

    @pl.when(step < pl.num_programs(0) - 1)
    def _():
        result = mm_tn(d_ref[...], h_ref[...]) + mm_tn(d_peer_ref[...], h_peer_ref[...])
        if relative:
            count = result.shape[1] // (4 * shard)
            for member in range(count):
                here = pl.ds(pl.multiple_of((step * count + member) * shard, 16), shard)
                for part in range(half // shard):
                    plain_ref[here, part * half : (part + 1) * half] = result[
                        part * shard : (part + 1) * shard, member * half : (member + 1) * half
                    ]
        else:
            outs[0][...] = result

    @pl.when(step == pl.num_programs(0) - 1)
    def _():
        result = mm_tn(n_ref[...], b_ref[...]) + mm_tn(n_peer_ref[...], b_peer_ref[...])
        if relative:
            plain_ref[:, 2 * D :] = result
            store_halves(*outs, table_ref, plain_ref, members, True)
        else:
            outs[1][...] = result


def adam_kernel(pick, *refs):
    table_ref, numbers_ref = refs[:2]
    master_ref, first_ref, second_ref = refs[2:5]
    sums, outs = refs[5:-3], refs[-3:]
    grads = pick(pl.program_id(0), table_ref[0], numbers_ref, sums)
    results = adam_update(
        master_ref[...], first_ref[...], second_ref[...], grads, rate_matrix, decay_matrix
    )
    for out_ref, result in zip(outs, results):
        out_ref[...] = result


SQUARE_LANES = tuple((i * D // 2, (i + 1) * D // 2) for i in range(3))


def section(refs, metas, lanes, target, offset=0):
    return [(ref, meta, lanes, target, offset) for ref, meta in zip(refs, metas)]


def blocks_of(group):
    return sum(array.shape[0] for array in group[0])


def whole_spec(shape):
    return pl.BlockSpec(shape, lambda *_: (0,) * len(shape), pipeline_mode=pl.Buffered(1))


def row_spec(block, width):
    return pl.BlockSpec((block, width), lambda i, *_: (i, 0))


COSTS = {'adam_square': 3, 'adam_qkv': 3, 'adam_expand': 3, 'adam_contract': 3, 'attend_teacher': 13, 'attend_student': 0.01, 'teacher_ffn': 0.01, 'student_ffn': 35, 'attend_back': 36, 'grad_expand': 15, 'grad_contract': 13, 'grad_joint': 7, 'grad_embed': 7}
smem_spec = pl.BlockSpec(memory_space=pltpu.SMEM)
any_spec = pl.BlockSpec(memory_space=pl.ANY)


def call(kernel, name, grid, ins, outs, scratch, flops, moved, prefetch=0, aliases={}):
    return pl.pallas_call(
        kernel,
        grid_spec=pltpu.PrefetchScalarGridSpec(
            num_scalar_prefetch=prefetch,
            grid=grid,
            in_specs=[spec for _, spec in ins[prefetch:]],
            out_specs=[spec for _, spec in outs],
            scratch_shapes=scratch,
        ),
        out_shape=[jax.ShapeDtypeStruct(*item) for item, _ in outs],
        input_output_aliases=aliases,
        compiler_params=pltpu.CompilerParams(vmem_limit_bytes=60 << 20),
        cost_estimate=pl.CostEstimate(
            flops=int(COSTS[name] * 1.15e9), transcendentals=0, bytes_accessed=1
        ),
        name=name,
    )(*[item for item, _ in ins])


def attend_teacher(real_rows, pad_rows, images, first, before, x, square, wj, vectors):
    rows, block = x.shape[0], images * pad_rows
    wj, vectors = ((item, whole_spec(item.shape)) for item in (wj, vectors))
    w0, w1 = ((square, pl.BlockSpec((None, D, D), lambda i, *_, at=at: (at, 0, 0))) for at in range(2))
    here = pl.BlockSpec((block, D), lambda i, *_: (first, 0))
    return call(
        functools.partial(attend_teacher_kernel, real_rows, pad_rows),
        "attend_teacher",
        (1,),
        [(x, here), w0, wj, w1, vectors] + ([] if before is None else [(before, any_spec)]),
        [(((rows, D), f32), here)],
        [pltpu.VMEM((block, 3 * D), bf16), pltpu.VMEM((block, D), bf16)],
        14 * rows * D * D,
        20e6,
        aliases={} if before is None else {5: 0},
    )[0]


def attend_student(real_rows, pad_rows, images, table, x, marks, vectors, square, joint):
    rows, block = x.shape[0], images * pad_rows
    arrays, metas = square[0] + joint[0], (square[1], joint[1])
    outs = [(D, f32), (D, f32), (3 * D, bf16), (3 * D, bf16)]
    return call(
        functools.partial(attend_student_kernel, real_rows, pad_rows, *metas),
        "attend_student",
        (rows // block,),
        [
            (table, smem_spec),
            (x, row_spec(block, D)),
            (marks, row_spec(block, 128)),
            (vectors, whole_spec(vectors.shape)),
        ]
        + [(array, any_spec) for array in arrays],
        [(((rows, width), kind), row_spec(block, width)) for width, kind in outs],
        [
            pltpu.VMEM((D, D), bf16),
            pltpu.VMEM((D, D), bf16),
            pltpu.VMEM((D, 3 * D), bf16),
            pltpu.SemaphoreType.DMA((3 * blocks_of(square) + blocks_of(joint),)),
        ],
        14 * rows * D * D,
        25e6,
    )


def teacher_ffn(real_rows, pad_rows, images, mid, weights, biases, vectors, sums):
    rows, block = mid.shape[0], images * pad_rows
    items = [biases, vectors, *weights]
    wholes = [(item, whole_spec(item.shape)) for item in items]
    last = [] if sums is None else [(sums, row_spec(block, D))]
    return call(
        functools.partial(teacher_ffn_kernel, real_rows, pad_rows, sums is not None),
        "teacher_ffn",
        (rows // block,),
        [(mid, row_spec(block, D))] + wholes + last,
        [(((rows, D), f32), row_spec(block, D))],
        [],
        16 * rows * D * D,
        15e6,
    )[0]


def student_ffn(pad_rows, images, table, scale, mid, targets, marks, vectors, expand, contract):
    rows, block = mid.shape[0], images * pad_rows
    outs = [(7 * D // 2, bf16), (7 * D // 2, bf16), (6 * D, bf16), (D, f32)]
    return call(
        functools.partial(student_ffn_kernel, expand[1], contract[1]),
        "student_ffn",
        (rows // block,),
        [
            (table, smem_spec),
            (scale, smem_spec),
            (mid, row_spec(block, D)),
            (targets, row_spec(block, D)),
            (marks, row_spec(block, 128)),
            (vectors, whole_spec(vectors.shape)),
        ]
        + [(array, any_spec) for array in (*expand[0], *contract[0])],
        [(((rows, width), kind), row_spec(block, width)) for width, kind in outs]
        + [(((16, D), f32), whole_spec((16, D)))],
        [
            pltpu.VMEM((D, 4 * D), bf16),
            pltpu.VMEM((4 * D, D), bf16),
            pltpu.VMEM((D, D), bf16),
            pltpu.VMEM((block, 4 * D), f32),
            pltpu.VMEM((block, D), bf16),
            pltpu.SemaphoreType.DMA((2 * blocks_of(expand) + blocks_of(contract),)),
        ],
        36 * rows * D * D,
        40e6,
    )


def attend_back(
    real_rows, pad_rows, images, table, dmid, joint, start, marks, vectors, square, qkv
):
    rows, block = dmid.shape[0], images * pad_rows
    arrays, metas = square[0] + qkv[0], (square[1], qkv[1])
    return call(
        functools.partial(attend_back_kernel, real_rows, pad_rows, *metas),
        "attend_back",
        (rows // block,),
        [
            (table, smem_spec),
            (dmid, row_spec(block, D)),
            (joint, row_spec(block, 3 * D)),
            (start, row_spec(block, D)),
            (marks, row_spec(block, 128)),
            (vectors, whole_spec(vectors.shape)),
        ]
        + [(array, any_spec) for array in arrays],
        [(((rows, 2 * D), bf16), row_spec(block, 2 * D))] * 2
        + [(((16, D), f32), whole_spec((16, D)))],
        [
            pltpu.VMEM((D, D), bf16),
            pltpu.VMEM((D, 3 * D), bf16),
            pltpu.VMEM((block, D), bf16),
            pltpu.VMEM((block, 3 * D), bf16),
            pltpu.VMEM((block, D), bf16),
            pltpu.SemaphoreType.DMA((2 * blocks_of(square) + blocks_of(qkv),)),
        ],
        20 * rows * D * D,
        25e6,
    )


def split_blocks(grads, members, y_first, place, own_y):
    top = jnp.max(jnp.abs(grads), axis=0, keepdims=True)
    rows = grads.shape[0] // members
    rels = jnp.array([rel for rel, _ in relative_places(members, False)])
    blocks = jnp.take(grads.reshape(members, rows, -1), rels ^ place, axis=0)
    if y_first:
        blocks = blocks.reshape(members, 2, rows // 2, -1)
        blocks = jnp.take(blocks, jnp.arange(2) ^ own_y, axis=1).swapaxes(0, 1)
    blocks = blocks.reshape(grads.shape)
    keep, sent = jnp.split(blocks, 2)
    exponent = column_exponents(top)
    tail = jnp.broadcast_to(exponent, (16, exponent.shape[1]))
    return keep, jnp.concatenate([sent * power_of_two(exponent), tail], 0), top


def half_outs(width, columns, index):
    heights = (D // 2, D // 2 + 16, 8)
    return [(((height, columns), f32), pl.BlockSpec((height, width), index)) for height in heights]


def weight_grad(name, table, members, y_first, steps, sides, own_b, peer_b):
    rows = own_b[0].shape[0]
    wide = D // 2
    relative = (D // members) % 32 == 0
    ins = [(table, None)]
    for own, peer, index, _ in sides:
        spec = pl.BlockSpec((rows, D), lambda j, _, index=index: (0, index(j)))
        ins += [(own, spec), (peer, spec)]
    for item, index in (own_b, peer_b):
        ins.append((item, pl.BlockSpec((rows, wide), lambda j, _, index=index: (0, index(j)))))
    if relative:
        outs = half_outs(wide, steps * wide, lambda j, _: (0, j))
    else:
        outs = [(((D, steps * wide), f32), pl.BlockSpec((D, wide), lambda j, _: (0, j)))]
    results = call(
        functools.partial(
            weight_grad_kernel, members, y_first, relative, tuple(side[3] for side in sides)
        ),
        name,
        (steps,),
        ins,
        outs,
        [pltpu.VMEM((D, wide), f32)],
        4 * rows * D * wide * steps,
        4 * D * wide * steps + 4 * rows * (D + wide * steps),
        prefetch=1,
    )
    if relative:
        return results
    return split_blocks(results[0], members, y_first, table[2], table[1])


def contract_grad(table, members, keep, two, two_peer):
    rows = two.shape[0]
    wide = D // 2
    shard = D // members
    relative = shard % 32 == 0
    steps = 4
    column = lambda item, index: (item, pl.BlockSpec((rows, wide), lambda i, _: (0, index)))
    moving = lambda item: (
        item,
        pl.BlockSpec((rows, D), lambda i, _: (0, 1 + jnp.minimum(i, steps - 1))),
    )
    left = pl.BlockSpec((rows, D), lambda i, _: (0, 0))
    if relative:
        assert 4 * shard == wide
        outs = half_outs(5 * wide, 5 * wide, lambda i, _: (0, 0))
        plain = (D, 5 * wide)
    else:
        outs = [
            (((wide, 4 * D), f32), pl.BlockSpec((wide, D), lambda i, _: (0, jnp.minimum(i, steps - 1)))),
            (((D, wide), f32), pl.BlockSpec((D, wide), lambda i, _: (0, 0))),
        ]
        plain = (8, 128)
    results = call(
        functools.partial(contract_grad_kernel, members, relative),
        "grad_contract",
        (steps + 1,),
        [(table, None), column(keep, 5), column(two_peer, 10), moving(two), moving(two_peer)]
        + [(two, left), (two_peer, left), column(keep, 4), column(two_peer, 11)],
        outs,
        [pltpu.VMEM(plain, f32)],
        16 * rows * D * wide,
        16 * D * wide + 16 * rows * D,
        prefetch=1,
    )
    if relative:
        return results
    blocks = results[0].reshape(wide // shard, shard, members, 4 * shard)
    blocks = blocks.transpose(2, 1, 0, 3).reshape(D, -1)
    whole = jnp.concatenate([blocks, results[1]], 1)
    return split_blocks(whole, members, True, table[2], table[1])


def adam(name, pick, table, numbers, masters, block, index, steps, sums):
    spec = pl.BlockSpec(block, lambda j, *_: index(j))
    ins = [(table, smem_spec), (numbers, smem_spec)] + [(item, spec) for item in masters]
    ins += [(item, pl.BlockSpec(shape, lambda j, *_, at=at: at(j))) for item, shape, at in sums]
    size = masters[0].size
    return call(
        functools.partial(adam_kernel, pick),
        name,
        (steps,),
        ins,
        [((masters[0].shape, f32), spec)] * 3,
        [],
        10 * size,
        32 * size,
    )


def after(value, *others):
    return lax.optimization_barrier((value, *others))[0]


def swap(values, bit):
    total = lax.axis_size("batch") * lax.axis_size("mlp")
    return lax.ppermute(values, ("batch", "mlp"), [(i, i ^ bit) for i in range(total)])


def batch_swap(values, bit):
    return swap(values, lax.axis_size("mlp") << bit)


def bit_of(axis, bit):
    return (lax.axis_index(axis) >> bit) & 1


def all_sum(values, bits):
    for bit in bits:
        values = values + swap(values, 1 << bit)
    return values


def pairs_sum(values, bits):
    while bits:
        one, bits = 1 << bits[0], bits[1:]
        if not bits:
            return values + swap(values, one)
        two, bits = 1 << bits[0], bits[1:]
        values = (values + swap(values, one)) + (swap(values, two) + swap(values, one | two))
    return values


def half_of(values, which, axis):
    width = values.shape[axis] // 2
    return lax.dynamic_slice_in_dim(values, which * width, width, axis)


def in_order(first, second, bit_value, axis):
    return jnp.where(
        bit_value == 0,
        jnp.concatenate([first, second], axis),
        jnp.concatenate([second, first], axis),
    )


def natural_rows(blocks, order):
    count = len(order)
    full = blocks.reshape((2,) * count + blocks.shape[1:])
    for place in range(count):
        flip = bit_of("batch", order[count - 1 - place])
        full = jnp.where(flip == 0, full, jnp.flip(full, place))
    source = [count - 1 - order.index(bit) for bit in reversed(range(count))]
    full = full.transpose(source + [count, count + 1])
    return full.reshape(1, -1, full.shape[-1])


def blocks_group(held, last, order, row):
    members = 1 << len(order)
    height = held.shape[1]
    if height % 16 != 0:
        return whole_group(natural_rows(jnp.concatenate([held, last], 0), order), row)
    entries = [
        lax.axis_index("batch") ^ sum(((p >> j) & 1) << bit for j, bit in enumerate(order))
        for p in range(members)
    ]
    arrays = [held, last, swap(held, 1), swap(last, 1)]
    metas = [
        (0, height, height, row + part * (members // 2), near)
        for near in (True, False)
        for part in (0, 1)
    ]
    return (arrays, tuple(metas)), entries


def sides_group(own, other, members, row):
    height = own.shape[0] // members
    own, other = (item.reshape(members, height, -1) for item in (own, other))
    if height % 16 != 0:
        both = in_order(own[:, None], other[:, None], bit_of("mlp", 1), 1)
        return whole_group(both.reshape(1, 2 * members * height, -1), row)[0]
    arrays = [own, other, swap(own, 1), swap(other, 1)]
    metas = [(side, 2 * height, height, row, near) for near in (True, False) for side in (1, 2)]
    return arrays, tuple(metas)


def whole_group(near, row):
    metas = tuple((0, 0, near.shape[1], row, side) for side in (True, False))
    return ([near, swap(near, 1)], metas), []


def power_of_two(exponent):
    size = jnp.abs(exponent).astype(jnp.int32)
    result = jnp.ones_like(exponent)
    for bit in range(7):
        factor = jnp.where(exponent > 0, 2.0 ** (1 << bit) if bit < 7 else 1.0, 2.0 ** -(1 << bit))
        result = jnp.where((size >> bit) & 1 == 1, result * factor, result)
    return result


def low_half(values):
    return lax.reduce_precision(values, 5, 10).astype(jnp.float16)


def low_half(values):
    return lax.reduce_precision(values, 5, 10).astype(jnp.float16)


def packed(values, exponent):
    tail = jnp.broadcast_to(exponent, (16, exponent.shape[1]))
    return low_half(jnp.concatenate([values * jnp.exp2(exponent), tail], 0))


class Reduction:
    def __init__(self, blocks, order, y_first):
        self.keep, sent, _ = blocks
        self.exponent = sent[-1:]
        self.hops = (["y"] if y_first else []) + list(order) + ["last"]
        self.y_first = y_first
        self.sent = low_half(sent)
        self.other = None

    def fetch(self):
        if self.other is None:
            at_y = self.hops[0] in ("y", "last")
            self.other = swap(self.sent, 2) if at_y else batch_swap(self.sent, self.hops[0])
        return self.other

    def receive(self, *gates):
        other = after(self.fetch(), *gates)
        self.other = None
        bit = self.hops.pop(0)
        rows = other.shape[0] - 16
        exponent = other[-1:].astype(f32)
        if bit == "last":
            own = self.sent[:rows].astype(f32) * power_of_two(-self.sent[-1:].astype(f32))
            other = other[:rows].astype(f32) * power_of_two(-exponent)
            if self.y_first:
                self.sums = in_order(own, other, bit_of("mlp", 1), 0)
            else:
                self.sums = own + other
            return self
        factor = jnp.exp2(-exponent)
        self.exponent = jnp.minimum(self.exponent, exponent) - 1.0
        half = rows // 2 if len(self.hops) > 1 else 0
        sums = self.keep[half:] + other[half:rows].astype(f32) * factor
        self.sent = packed(sums, self.exponent)
        if half:
            self.keep = self.keep[:half] + other[:half].astype(f32) * factor
        return self


def adam_update(master, first, second, gradient, step_rate, weight_decay):
    moment = beta_first * first + (1.0 - beta_first) * gradient
    variance = beta_second * second + (1.0 - beta_second) * gradient * gradient
    corrected = moment / (1.0 - beta_first**STEP)
    scaled = variance / (1.0 - beta_second**STEP)
    updated = master - step_rate * (
        corrected / (jnp.sqrt(scaled) + adam_eps) + weight_decay * master
    )
    return (moment, variance, updated)


def on_device(
    patches,
    mask,
    student_square,
    student_qkv,
    student_expand,
    student_contract,
    student_vectors,
    first_square,
    first_qkv,
    first_expand,
    first_contract,
    first_vectors,
    second_square,
    second_qkv,
    second_expand,
    second_contract,
    second_vectors,
    teacher_square,
    teacher_qkv,
    teacher_expand,
    teacher_contract,
    teacher_vectors,
):
    members = lax.axis_size("batch")
    count = members.bit_length() - 1
    mlp_bits = lax.axis_size("mlp").bit_length() - 1
    near = list(range(count))
    far = near[::-1]
    batch_bits = range(mlp_bits, mlp_bits + count)
    shard_rows = D // members
    core, own_y = bit_of("mlp", 0), bit_of("mlp", 1)
    place = lax.axis_index("batch")
    group, real_rows = mask.shape
    pad_rows = -(-real_rows // 16) * 16
    half = D // 2

    pad = ((0, 0), (0, pad_rows - real_rows))
    x = jnp.pad(patches, pad + ((0, 0),)).reshape(-1, D)
    marks = jnp.pad(mask.astype(f32), pad).reshape(-1)
    wide_marks = jnp.broadcast_to(marks[:, None], (marks.shape[0], 128))

    square_held = jnp.concatenate(
        [half_of(student_square[i], core, 1) for i in range(2)]
        + [lax.dynamic_slice_in_dim(student_qkv, core * 3 * half, half, 1)],
        1,
    ).astype(bf16)[None]
    qkv_held = lax.dynamic_slice_in_dim(student_qkv, core * 3 * half + half, D, 1)
    qkv_held = qkv_held.astype(bf16)[None]
    expand_held = jnp.concatenate(
        [half_of(half_of(item, core, 1), own_y, 0) for item in (student_expand, student_square[2])],
        1,
    )
    expand_own = lax.all_gather(expand_held.astype(bf16), "batch", axis=0, tiled=True)
    contract_near = lax.all_gather(
        half_of(student_contract, core, 1).astype(bf16), "batch", axis=0, tiled=True
    )
    low_vectors = lax.reduce_precision(student_vectors, 8, 7)
    small = lax.dynamic_update_slice(
        jnp.zeros((low_vectors.shape[0], D), f32), low_vectors, (0, place * shard_rows)
    )
    small = jnp.concatenate([small, jnp.full((1, D), jnp.sum(marks))], 0)

    images = min(group, 2)
    sizes = (real_rows, pad_rows, images)
    teacher_weights = (teacher_square, teacher_qkv, teacher_vectors)
    own = lax.axis_index("mlp")
    biases = jnp.concatenate(
        [lax.dynamic_slice_in_dim(teacher_vectors, 8 + (own ^ part), 1, 0) for part in range(4)]
    )
    tmid, runs, tsum, done = None, 0, None, ()
    square_order, qkv_order = far, near[:1] + far[:-1]
    for hop in range(count):
        sends = lax.optimization_barrier((square_held, qkv_held, small, *done))[:3]
        square_held, qkv_held, small = sends
        square_last = batch_swap(square_held, square_order[hop])
        qkv_last = batch_swap(qkv_held, qkv_order[hop])
        small_last = batch_swap(small, near[hop])
        if runs < group // images:
            tmid = attend_teacher(*sizes, runs, tmid, after(x, *sends), *teacher_weights)
            runs += 1
            done = (tmid,)
            if runs == 1:
                teacher_own = jnp.concatenate([after(teacher_expand, tmid), teacher_contract], 1)
                teacher_y = swap(teacher_own, 2)
                teacher_core = swap(teacher_own, 1)
        elif tsum is None:
            tsum = teacher_ffn(
                *sizes,
                after(tmid, *sends, expand_own),
                (teacher_own, teacher_core),
                biases[:2],
                teacher_vectors,
                None,
            )
            done = (tsum,)
        if hop + 1 < count:
            square_held = jnp.concatenate([square_held, square_last], 0)
            qkv_held = jnp.concatenate([qkv_held, qkv_last], 0)
        small = small + after(small_last, *done)
    vectors = small[:-1]
    square_held, qkv_held, square_last, qkv_last = lax.optimization_barrier(
        (square_held, qkv_held, square_last, qkv_last, *done, teacher_y)
    )[:4]
    square, square_rows = blocks_group(square_held, square_last, square_order, 3)
    qkv, qkv_rows = blocks_group(qkv_held, qkv_last, qkv_order, 3 + len(square_rows))
    entries = [core, own_y, place] + square_rows + qkv_rows + list(range(members))
    table = jnp.stack([jnp.asarray(entry, jnp.int32) for entry in entries])

    masked_count = all_sum(after(small, square_last, qkv_last)[-1:, :128], range(mlp_bits))
    expand_y = swap(after(expand_own, masked_count), 2)
    teacher_far = swap(after(teacher_y, masked_count), 1)
    targets = teacher_ffn(
        *sizes,
        after(tmid, masked_count, expand_own),
        (teacher_y, teacher_far),
        biases[2:],
        teacher_vectors,
        tsum,
    )
    start, mid, joint, act = attend_student(
        *sizes, table, after(x, targets), wide_marks, vectors, square, qkv
    )
    masked_count = masked_count[0, 0]
    mid, expand_y = lax.optimization_barrier((mid, expand_y))
    expand = sides_group(after(expand_own, mid), expand_y, members, 3 + len(square_rows + qkv_rows))
    contract, _ = whole_group(after(contract_near, mid)[None], 0)
    act_peer = swap(after(act, mid), 1)
    scale = (2.0 / (masked_count * D)).reshape(1)
    keep, one, two, dmid, ffn_sums = student_ffn(
        pad_rows, images, table, scale, mid, targets, wide_marks, vectors, expand, contract
    )
    one_peer = swap(after(one, act_peer), 1)
    two_peer = swap(after(two, one_peer), 1)

    blocks = weight_grad(
        "grad_expand",
        table,
        members,
        False,
        5,
        [
            (one, one_peer, lambda j: 0, (0, 1, 2, 3)),
            (act, act_peer, lambda j: 0, (4,)),
        ],
        (keep, lambda j: jnp.where(j == 4, 6, j)),
        (one_peer, lambda j: jnp.where(j == 4, 6, j + 2)),
    )
    to_expand = Reduction(blocks, near, False)
    blocks = contract_grad(table, members, keep, two, after(two_peer, to_expand.sent))
    to_contract = Reduction(blocks, near, True)
    keep3, send3, att_sums = attend_back(
        *sizes,
        table,
        after(dmid, to_contract.sent),
        joint,
        start,
        wide_marks,
        vectors,
        square,
        qkv,
    )
    send3_peer = swap(send3, 1)
    to_expand.receive(att_sums)
    to_contract.receive()

    total = jnp.concatenate([ffn_sums[:12], att_sums[:6]], 0)
    total_bits = list(range(mlp_bits + count))

    def total_hop(*gates):
        nonlocal total
        if total_bits:
            total = after(total, *gates)
            total = total + swap(total, 1 << total_bits.pop(0))

    total_hop(to_expand.sent, to_contract.sent)
    blocks = weight_grad(
        "grad_joint",
        table,
        members,
        False,
        3,
        [(act, act_peer, lambda j: 1, (0, 1, 2))],
        (keep3, lambda j: j),
        (after(send3_peer, to_expand.sent, to_contract.sent), lambda j: j),
    )
    to_first = Reduction(blocks, near, False)
    to_expand.receive(to_first.sent)
    to_contract.receive(to_first.sent)
    total_hop(to_first.sent)
    blocks = weight_grad(
        "grad_embed",
        table,
        members,
        True,
        1,
        [(act, act_peer, lambda j: 2, (0,))],
        (keep3, lambda j: j + 3),
        (after(send3_peer, to_first.sent, to_expand.sent, to_contract.sent), lambda j: j + 3),
    )
    keep_rows, sent_rows, top = blocks
    sent_rows = after(sent_rows, to_first.fetch())
    to_second = Reduction((keep_rows, sent_rows, top), near, True)
    others = to_expand.fetch(), to_contract.fetch()
    to_first.receive(to_second.sent)
    to_second.receive(*others)
    gates = (to_second.sent, to_first.sent)
    to_expand.receive(*gates)
    to_contract.receive(*gates)
    moving = [to_first, to_second, to_contract, to_expand]
    while moving:
        total_hop(*gates)
        for item in list(moving):
            item.receive(*gates)
            if not item.hops:
                moving.remove(item)
        gates = (moving[0].sent,) if moving else ()
    while total_bits:
        total_hop()
    ffn_total, att_total = total[:12], total[12:]

    own_sums = [item.sums for item in (to_expand, to_contract, to_first, to_second)]
    vector_total = jnp.concatenate(
        [
            att_total[5:6],
            att_total[4:5],
            att_total[2:4],
            att_total[0:2],
            ffn_total[11:12],
            ffn_total[9:11],
            ffn_total[5:9],
            ffn_total[4:5],
            ffn_total[2:4],
            ffn_total[1:2],
        ]
    )
    loss_sum = jnp.sum(ffn_total[0])
    vector_grad = lax.dynamic_slice_in_dim(vector_total, place * shard_rows, shard_rows, 1)
    squares = 0.5 * jnp.sum(vector_grad * vector_grad)
    for member in own_sums:
        squares = squares + jnp.sum(member * member)
    squares = pairs_sum(jnp.full((1, 128), squares), [0, *batch_bits])
    grad_norm = jnp.sqrt(squares[0, 0])
    factor = clip_bound / jnp.maximum(grad_norm, clip_bound)

    pairs = [(item, swap(item, 1)) for item in own_sums]
    numbers = factor.reshape(1)

    def picked(is_own, own_ref, peer_ref):
        return jnp.where(is_own, own_ref[...], peer_ref[...])

    def pick_square(step, core_of, numbers_ref, refs):
        sides = []
        for near in (True, False):
            parts = [refs[2 * i + (0 if near else 1)][...] for i in range(3)]
            side = jnp.where(step == 0, parts[0], jnp.where(step == 1, parts[1], parts[2]))
            sides.append(side)
        left = jnp.where(core_of == 0, sides[0], sides[1])
        right = jnp.where(core_of == 0, sides[1], sides[0])
        return (jnp.concatenate([left, right], 1) * numbers_ref[0])[None]

    def pick_joint(step, core_of, numbers_ref, refs):
        return picked(step == core_of, *refs) * numbers_ref[0]

    def pick_expand(step, core_of, numbers_ref, refs):
        return picked(step == core_of, *refs) * numbers_ref[0]

    def pick_contract(step, core_of, numbers_ref, refs):
        grads = picked(step == core_of, *refs)
        if grads.shape[0] != 4 * shard_rows:
            parts = half // shard_rows
            grads = [grads[:, i * 4 * shard_rows : (i + 1) * 4 * shard_rows] for i in range(parts)]
            grads = jnp.concatenate(grads, 0).T
        return grads * numbers_ref[0]

    def pieces(index, at, width=half):
        return [(item, (shard_rows, width), at) for item in pairs[index]]

    square_results = adam(
        "adam_square",
        pick_square,
        table,
        numbers,
        (student_square, first_square, second_square),
        (1, shard_rows, D),
        lambda j: (j, 0, 0),
        3,
        pieces(3, lambda j: (0, 0)) + pieces(0, lambda j: (0, 4)) + pieces(1, lambda j: (0, 4)),
    )
    qkv_results = adam(
        "adam_qkv",
        pick_joint,
        table,
        numbers,
        (student_qkv, first_qkv, second_qkv),
        (shard_rows, 3 * half),
        lambda j: (0, j),
        2,
        pieces(2, lambda j: (0, 0), 3 * half),
    )
    expand_results = adam(
        "adam_expand",
        pick_expand,
        table,
        numbers,
        (student_expand, first_expand, second_expand),
        (shard_rows, 4 * half),
        lambda j: (0, j),
        2,
        pieces(0, lambda j: (0, 0), 4 * half),
    )
    if 4 * shard_rows == half:
        contract_pieces = pieces(1, lambda j: (0, 0), 4 * half)
    else:
        contract_pieces = []
        for item in pairs[1]:
            item = item[:, : 4 * half].reshape(shard_rows, half // shard_rows, 4 * shard_rows)
            item = item.swapaxes(0, 1).reshape(half, 4 * shard_rows).T
            contract_pieces.append((item, item.shape, lambda j: (0, 0)))
    contract_results = adam(
        "adam_contract",
        pick_contract,
        table,
        numbers,
        (student_contract, first_contract, second_contract),
        (4 * shard_rows, half),
        lambda j: (0, j),
        2,
        contract_pieces,
    )
    vector_results = adam_update(
        student_vectors, first_vectors, second_vectors, vector_grad * factor, rate_vector, 0.0
    )
    return (
        loss_sum,
        masked_count,
        grad_norm,
        *square_results,
        *qkv_results,
        *expand_results,
        *contract_results,
        *vector_results,
    )


def solution(mesh):
    return jax.shard_map(
        on_device,
        mesh=mesh,
        in_specs=(
            P(("batch", "mlp"), None, None),
            P(("batch", "mlp"), None),
            P(None, "batch", None),
            P("batch", None),
            P("batch", None),
            P("batch", None),
            P(None, "batch"),
            P(None, "batch", None),
            P("batch", None),
            P("batch", None),
            P("batch", None),
            P(None, "batch"),
            P(None, "batch", None),
            P("batch", None),
            P("batch", None),
            P("batch", None),
            P(None, "batch"),
            P(),
            P(),
            P(None, "mlp"),
            P("mlp", None),
            P(),
        ),
        out_specs=(
            P(),
            P(),
            P(),
            P(None, "batch", None),
            P(None, "batch", None),
            P(None, "batch", None),
            P("batch", None),
            P("batch", None),
            P("batch", None),
            P("batch", None),
            P("batch", None),
            P("batch", None),
            P("batch", None),
            P("batch", None),
            P("batch", None),
            P(None, "batch"),
            P(None, "batch"),
            P(None, "batch"),
        ),
        check_vma=False,
    )
```

```python
import functools

import jax
import jax.numpy as jnp
from jax import lax
from jax.experimental import pallas as pl
from jax.experimental.pallas import tpu as pltpu
from jax.sharding import PartitionSpec as P

D = 768
HEAD_DIM = 64
PAIR = 2 * HEAD_DIM
UNROLL = 3
STEP = 10


norm_eps = 1e-06
inst_eps = 1e-05
clip_bound = 0.001
rate_matrix = 0.05
rate_vector = 0.5
decay_matrix = 0.05
beta_first = 0.9
beta_second = 0.999
adam_eps = 1e-08
f32 = jnp.float32
bf16 = jnp.bfloat16


def mm(left, right):
    return lax.dot_general(left, right, (((1,), (0,)), ((), ())), preferred_element_type=f32)


def mm_nt(left, right):
    return lax.dot_general(left, right, (((1,), (1,)), ((), ())), preferred_element_type=f32)


def mm_tn(left, right):
    return lax.dot_general(left, right, (((0,), (0,)), ((), ())), preferred_element_type=f32)


def normed_rows(values):
    centred = values - jnp.mean(values, axis=-1, keepdims=True)
    variance = jnp.mean(centred * centred, axis=-1, keepdims=True)
    scale = lax.rsqrt(variance + norm_eps)
    return centred * scale, scale


def norm_back(xhat, scale, gain, grads):
    scaled = grads * gain
    mean_one = jnp.mean(scaled, axis=-1, keepdims=True)
    mean_two = jnp.mean(scaled * xhat, axis=-1, keepdims=True)
    back = scale * (scaled - mean_one - xhat * mean_two)
    return back, total_rows(grads * xhat), total_rows(grads)


def piece_copies(table_ref, semaphores, first, pieces):
    core, own_y = table_ref[0], table_ref[1]
    copies = []
    for ref, (side, unit, height, row, near), lanes, target, offset in pieces:
        width = lanes[1] - lanes[0]
        column = (core if near else 1 - core) * (target.shape[1] // 2) + offset
        column = pl.multiple_of(column, 128)
        base = (0, own_y * height, (1 - own_y) * height)[side]
        for block in range(ref.shape[0]):
            place = 0 if unit == 0 else pl.multiple_of(table_ref[row + block] * unit + base, 16)
            copies.append(
                pltpu.make_async_copy(
                    ref.at[block, :, pl.ds(lanes[0], width)],
                    target.at[pl.ds(place, height), pl.ds(column, width)],
                    semaphores.at[first + len(copies)],
                )
            )
    return copies


def total_rows(values):
    return jnp.sum(values, axis=0, keepdims=True)


def head_masks(rows):
    lane = lax.broadcasted_iota(jnp.int32, (rows, PAIR), 1)
    return lane < HEAD_DIM


def stacked(values, low):
    zero = jnp.zeros_like(values)
    return jnp.concatenate([jnp.where(low, values, zero), jnp.where(low, zero, values)], axis=0)


def pair_probs(stack, keys, real_rows):
    scores = mm_nt(stack, keys)
    column = lax.broadcasted_iota(jnp.int32, scores.shape, 1)
    scores = jnp.where(column < real_rows, scores, -1e30)
    shifted = jnp.exp(scores - jnp.max(scores, axis=-1, keepdims=True))
    return shifted * (1.0 / jnp.sum(shifted, axis=-1, keepdims=True))


def attend_block(is_student, real_rows, pad_rows, x_ref, marks_ref, weights, vec_ref, outs, waits):
    w0_ref, wj_ref, w1_ref = weights
    start_ref, mid_ref, joint_ref, act_ref = outs
    at = (lambda student, teacher: student if is_student else teacher)
    vec = lambda row: vec_ref[row : row + 1, :]
    block = x_ref.shape[0]
    if is_student:
        waits[0]()
    start = mm(x_ref[...], w0_ref[...]) + vec(0)
    if is_student:
        start = jnp.where(marks_ref[:, :1] > 0, vec(1), start)
    start_ref[...] = start
    xhat, _ = normed_rows(start)
    normed = (xhat * vec(at(2, 1)) + vec(at(3, 2))).astype(bf16)
    if is_student:
        act_ref[:, D : 2 * D] = normed
        act_ref[:, 2 * D :] = x_ref[...]
    biases = (vec(at(4, 3)), None, vec(at(5, 4)))
    if is_student:
        waits[1]()
    for part in range(3):
        cols = slice(part * D, (part + 1) * D)
        mixed = mm(normed, wj_ref[:, cols])
        if biases[part] is not None:
            mixed = mixed + biases[part]
        joint_ref[:, cols] = mixed.astype(bf16)
    low = head_masks(pad_rows)

    def one_pair(step, carry):
        image = step // (D // PAIR)
        col = pl.multiple_of((step % (D // PAIR)) * PAIR, PAIR)
        rows = pl.ds(pl.multiple_of(image * pad_rows, 16), pad_rows)
        queries = joint_ref[rows, pl.ds(col, PAIR)] * HEAD_DIM ** (-0.5)
        keys = joint_ref[rows, pl.ds(col + D, PAIR)]
        values = joint_ref[rows, pl.ds(col + 2 * D, PAIR)]
        probs = pair_probs(stacked(queries.astype(bf16), low), keys, real_rows).astype(bf16)
        mixed = mm(probs, values)
        act_ref[rows, pl.ds(col, PAIR)] = jnp.where(
            low, mixed[:pad_rows], mixed[pad_rows:]
        ).astype(bf16)
        return carry

    lax.fori_loop(0, (block // pad_rows) * (D // PAIR), one_pair, 0, unroll=2 * UNROLL)
    attended = act_ref[:, :D]
    if is_student:
        waits[2]()
    mid_ref[...] = start_ref[...] + mm(attended, w1_ref[...]) + vec(at(6, 5))


def clear_at_first(*refs):
    @pl.when(pl.program_id(0) == 0)
    def _():
        for ref in refs:
            ref[...] = jnp.zeros_like(ref)


def place_at_first(table_ref, semaphores, *groups):
    all_copies, count = [], 0
    for pieces in groups:
        all_copies.append(piece_copies(table_ref, semaphores, count, pieces))
        count += len(all_copies[-1])

    @pl.when(pl.program_id(0) == 0)
    def _():
        for copies in all_copies:
            for copy in copies:
                copy.start()

    def wait_for(copies):
        @pl.when(pl.program_id(0) == 0)
        def _():
            for copy in copies:
                copy.wait()

    return [functools.partial(wait_for, copies) for copies in all_copies]


def attend_teacher_kernel(real_rows, pad_rows, *refs):
    x_ref, w0_ref, wj_ref, w1_ref, vec_ref = refs[:5]
    mid_ref, joint_ref, att_ref = refs[-3:]
    attend_block(
        False,
        real_rows,
        pad_rows,
        x_ref,
        None,
        (w0_ref, wj_ref, w1_ref),
        vec_ref,
        (mid_ref, mid_ref, joint_ref, att_ref),
        None,
    )


def attend_student_kernel(real_rows, pad_rows, metas, joint_metas, *refs):
    (table_ref, x_ref, marks_ref, vec_ref) = refs[:4]
    count = len(metas)
    piece_refs, joint_refs = refs[4 : 4 + count], refs[4 + count : 4 + 2 * count]
    (start_ref, mid_ref, joint_ref, act_ref) = refs[4 + 2 * count : 8 + 2 * count]
    (w0_ref, w1_ref, wj_ref, semaphores) = refs[8 + 2 * count :]
    joint_pieces = section(piece_refs, metas, SQUARE_LANES[2], wj_ref)
    joint_pieces += section(joint_refs, joint_metas, (0, D), wj_ref, D // 2)
    waits = place_at_first(
        table_ref,
        semaphores,
        section(piece_refs, metas, SQUARE_LANES[0], w0_ref),
        joint_pieces,
        section(piece_refs, metas, SQUARE_LANES[1], w1_ref),
    )
    attend_block(
        True,
        real_rows,
        pad_rows,
        x_ref,
        marks_ref,
        (w0_ref, wj_ref, w1_ref),
        vec_ref,
        (start_ref, mid_ref, joint_ref, act_ref),
        waits,
    )


def gelu_half(values):
    return 0.5 * (1.0 + lax.erf(values * 0.7071067811865476))


def teacher_ffn_kernel(real_rows, pad_rows, is_last, *refs):
    mid_ref, bias_ref, vec_ref = refs[:3]
    parts = bias_ref.shape[0]
    rest = refs[3 + parts :]
    mid = mid_ref[...]
    xhat, _ = normed_rows(mid)
    normed = (xhat * vec_ref[6:7, :] + vec_ref[7:8, :]).astype(bf16)
    total = rest[0][...] if is_last else None
    for part, both_ref in enumerate(refs[3 : 3 + parts]):
        pre = mm(normed, both_ref[:, :D]) + bias_ref[part : part + 1, :]
        hidden = (pre * gelu_half(pre)).astype(bf16)
        piece = mm(hidden, both_ref[:, D:])
        total = piece if total is None else total + piece
    out_ref = rest[-1]
    if not is_last:
        out_ref[...] = total
        return
    total = total + vec_ref[12:13, :]
    valid = lax.broadcasted_iota(jnp.int32, (pad_rows, D), 0) < real_rows
    for image in range(mid_ref.shape[0] // pad_rows):
        rows = slice(image * pad_rows, (image + 1) * pad_rows)
        result = None
        for values in (mid[rows], total[rows]):
            mean = total_rows(jnp.where(valid, values, 0.0)) / real_rows
            centred = values - mean
            variance = total_rows(jnp.where(valid, centred * centred, 0.0)) / real_rows
            normal = centred * lax.rsqrt(variance + inst_eps)
            result = normal if result is None else result + normal
        out_ref[rows, :] = 0.5 * result


def student_ffn_kernel(expand_metas, contract_metas, *refs):
    (table_ref, scale_ref, mid_ref, target_ref, marks_ref, vec_ref) = refs[:6]
    counts = (len(expand_metas), len(contract_metas))
    expand_refs, contract_refs = refs[6 : 6 + counts[0]], refs[6 + counts[0] : 6 + sum(counts)]
    (keep_ref, one_ref, two_ref, dmid_ref, sum_ref) = refs[6 + sum(counts) : 11 + sum(counts)]
    (we_ref, wc_ref, wh_ref, slope_ref, half_ref, semaphores) = refs[11 + sum(counts) :]
    clear_at_first(sum_ref)
    expand_wait, contract_wait, head_wait = place_at_first(
        table_ref,
        semaphores,
        section(expand_refs, expand_metas, (0, 2 * D), we_ref),
        section(contract_refs, contract_metas, (0, D // 2), wc_ref),
        section(expand_refs, expand_metas, (2 * D, 5 * D // 2), wh_ref),
    )
    core = table_ref[0]

    def add(row, values):
        sum_ref[pl.ds(row, 1), :] += values

    def add_grad(row, grads):
        add(row, total_rows(grads.astype(f32)))

    def halves(keep_cols, send_ref, send_cols, grads):
        half_ref[...] = grads
        width = D // 2
        keep_ref[:, keep_cols : keep_cols + width] = half_ref[
            :, pl.ds(pl.multiple_of(core * width, 128), width)
        ]
        send_ref[:, send_cols : send_cols + width] = half_ref[
            :, pl.ds(pl.multiple_of((1 - core) * width, 128), width)
        ]

    vec = lambda row: vec_ref[row : row + 1, :]
    mid = mid_ref[...]
    xhat2, scale2 = normed_rows(mid)
    n2 = (xhat2 * vec(7) + vec(8)).astype(bf16)
    one_ref[:, :D] = n2
    total = None
    expand_wait()
    for part in range(4):
        cols = slice(part * D, (part + 1) * D)
        pre = mm(n2, we_ref[:, cols]) + vec(9 + part)
        half = gelu_half(pre)
        slope_ref[:, cols] = half + pre * (jnp.exp(-0.5 * pre * pre) * 0.3989422804014327)
        hidden = (pre * half).astype(bf16)
        two_ref[:, (part + 1) * D : (part + 2) * D] = hidden
        if part == 0:
            contract_wait()
        piece = mm(hidden, wc_ref[cols, :])
        total = piece if total is None else total + piece
    final = mid + total + vec(13)
    xhat3, scale3 = normed_rows(final)
    n3 = (xhat3 * vec(14) + vec(15)).astype(bf16)
    two_ref[:, :D] = n3
    head_wait()
    error = marks_ref[:, :1] * (mm(n3, wh_ref[...]) + vec(16) - target_ref[...])
    add(0, total_rows(error * error))
    dpred = (error * scale_ref[0]).astype(bf16)
    halves(2 * D, two_ref, 11 * D // 2, dpred)
    add_grad(1, dpred)
    dfinal, gain3, shift3 = norm_back(xhat3, scale3, vec(14), mm_nt(dpred, wh_ref[...]))
    add(2, gain3)
    add(3, shift3)
    dbranch = dfinal.astype(bf16)
    halves(2 * D + D // 2, two_ref, 5 * D, dbranch)
    add_grad(4, dbranch)
    dn2 = None
    for side in range(2):
        for part in range(2):
            chunk = 2 * (core ^ side) + part
            cols = pl.ds(pl.multiple_of(chunk * D, 128), D)
            dpre = (mm_nt(dbranch, wc_ref[cols, :]) * slope_ref[:, cols]).astype(bf16)
            if side == 0:
                keep_ref[:, part * D : (part + 1) * D] = dpre
            else:
                one_ref[:, (1 + part) * D : (2 + part) * D] = dpre
            add_grad(5 + chunk, dpre)
            piece = mm_nt(dpre, we_ref[:, cols])
            dn2 = piece if dn2 is None else dn2 + piece
    dmid, gain2, shift2 = norm_back(xhat2, scale2, vec(7), dn2)
    add(9, gain2)
    add(10, shift2)
    dmid = dfinal + dmid
    dmid_ref[...] = dmid
    datt = dmid.astype(bf16)
    halves(3 * D, one_ref, 3 * D, datt)
    add(11, total_rows(datt.astype(f32)))


def attend_back_kernel(real_rows, pad_rows, metas, joint_metas, *refs):
    (table_ref, dmid_ref, joint_ref, start_ref, marks_ref, vec_ref) = refs[:6]
    count = len(metas)
    piece_refs, joint_refs = refs[6 : 6 + count], refs[6 + count : 6 + 2 * count]
    (keep_ref, send_ref, sum_ref) = refs[6 + 2 * count : 9 + 2 * count]
    (w1_ref, wj_ref, grad_ref, djoint_ref, half_ref, semaphores) = refs[9 + 2 * count :]
    clear_at_first(sum_ref)
    joint_pieces = section(piece_refs, metas, SQUARE_LANES[2], wj_ref)
    joint_pieces += section(joint_refs, joint_metas, (0, D), wj_ref, D // 2)
    out_wait, joint_wait = place_at_first(
        table_ref, semaphores, section(piece_refs, metas, SQUARE_LANES[1], w1_ref), joint_pieces
    )
    out_wait()
    core = table_ref[0]

    def add(row, values):
        sum_ref[row : row + 1, :] += values

    def halves(column, source_ref, width):
        keep_ref[:, column : column + width] = source_ref[
            :, pl.ds(pl.multiple_of(core * width, 128), width)
        ]
        send_ref[:, column : column + width] = source_ref[
            :, pl.ds(pl.multiple_of((1 - core) * width, 128), width)
        ]

    vec = lambda row: vec_ref[row : row + 1, :]
    block = dmid_ref.shape[0]
    datt = dmid_ref[...].astype(bf16)
    grad_ref[...] = mm_nt(datt, w1_ref[...]).astype(bf16)
    low = head_masks(pad_rows)

    def one_pair(step, carry):
        image = step // (D // PAIR)
        col = pl.multiple_of((step % (D // PAIR)) * PAIR, PAIR)
        rows = pl.ds(pl.multiple_of(image * pad_rows, 16), pad_rows)
        queries = joint_ref[rows, pl.ds(col, PAIR)] * HEAD_DIM ** (-0.5)
        keys = joint_ref[rows, pl.ds(col + D, PAIR)]
        values = joint_ref[rows, pl.ds(col + 2 * D, PAIR)]
        stack = stacked(queries.astype(bf16), low)
        dstack = stacked(grad_ref[rows, pl.ds(col, PAIR)], low)
        probs = pair_probs(stack, keys, real_rows)
        dprobs = mm_nt(dstack, values)
        dvalues = mm_tn(probs.astype(bf16), dstack)
        weighted = probs * dprobs
        dscores = (weighted - probs * jnp.sum(weighted, axis=-1, keepdims=True)).astype(bf16)
        both = mm(dscores, keys) * HEAD_DIM ** (-0.5)
        dqueries = jnp.where(low, both[:pad_rows], both[pad_rows:])
        dkeys = mm_tn(dscores, stack)
        djoint_ref[rows, pl.ds(col, PAIR)] = dqueries.astype(bf16)
        djoint_ref[rows, pl.ds(col + D, PAIR)] = dkeys.astype(bf16)
        djoint_ref[rows, pl.ds(col + 2 * D, PAIR)] = dvalues.astype(bf16)
        return carry

    lax.fori_loop(0, (block // pad_rows) * (D // PAIR), one_pair, 0, unroll=UNROLL)
    halves(0, djoint_ref, 3 * D // 2)
    joint_wait()
    dnormed = None
    for part in range(3):
        cols = slice(part * D, (part + 1) * D)
        grads = djoint_ref[:, cols]
        if part != 1:
            add(part // 2, total_rows(grads.astype(f32)))
        piece = mm_nt(grads, wj_ref[:, cols])
        dnormed = piece if dnormed is None else dnormed + piece
    xhat, scale = normed_rows(start_ref[...])
    dstart, gain, shift = norm_back(xhat, scale, vec(2), dnormed)
    add(2, gain)
    add(3, shift)
    dstart = dstart + dmid_ref[...]
    masked = marks_ref[:, :1] > 0
    add(4, total_rows(jnp.where(masked, dstart, 0.0)))
    dembed = jnp.where(masked, 0.0, dstart).astype(bf16)
    half_ref[...] = dembed
    halves(3 * D // 2, half_ref, D // 2)
    add(5, total_rows(dembed.astype(f32)))


def relative_places(members, y_first):
    count = members.bit_length() - 1
    rels = [sum(((p >> (count - 1 - bit)) & 1) << bit for bit in range(count)) for p in range(members)]
    if y_first:
        return [(rel, side) for side in range(2) for rel in rels]
    return [(rel, None) for rel in rels]


def column_exponents(top):
    return jnp.floor(14.0 - jnp.log(jnp.clip(top, 1e-30, 1e30)) * 1.4426950408889634)


def store_halves(keep_ref, sent_ref, top_ref, table_ref, plain_ref, members, y_first):
    top = jnp.max(jnp.abs(plain_ref[...]), axis=0, keepdims=True)
    top_ref[...] = jnp.broadcast_to(top, top_ref.shape)
    exponent = column_exponents(top)
    factor = jnp.exp2(exponent)
    places = relative_places(members, y_first)
    rows = plain_ref.shape[0] // members
    height = rows // 2 if y_first else rows
    for index, (rel, side) in enumerate(places):
        first = (table_ref[2] ^ rel) * rows
        if y_first:
            first = first + (table_ref[1] ^ side) * height
        block = plain_ref[pl.ds(pl.multiple_of(first, 16), height), :]
        if index < len(places) // 2:
            keep_ref[index * height : (index + 1) * height, :] = block
        else:
            here = (index - len(places) // 2) * height
            sent_ref[here : here + height, :] = block * factor
    half_rows = keep_ref.shape[0]
    sent_ref[half_rows:, :] = jnp.broadcast_to(exponent, (16, exponent.shape[1]))


def weight_grad_kernel(members, y_first, relative, steps_of, *refs):
    table_ref = refs[0]
    sides = refs[1 : 1 + 2 * len(steps_of)]
    b_ref, b_peer_ref = refs[1 + 2 * len(steps_of) : 3 + 2 * len(steps_of)]
    outs, plain_ref = refs[3 + 2 * len(steps_of) : -1], refs[-1]
    step = pl.program_id(0)
    for index, steps in enumerate(steps_of):
        is_side = step == steps[0]
        for other in steps[1:]:
            is_side = is_side | (step == other)

        @pl.when(is_side)
        def _(index=index):
            plain_ref[...] = mm_tn(sides[2 * index][...], b_ref[...]) + mm_tn(
                sides[2 * index + 1][...], b_peer_ref[...]
            )

    if relative:
        store_halves(*outs, table_ref, plain_ref, members, y_first)
    else:
        outs[0][...] = plain_ref[...]


def contract_grad_kernel(members, relative, *refs):
    (table_ref, d_ref, d_peer_ref, h_ref, h_peer_ref) = refs[:5]
    (n_ref, n_peer_ref, b_ref, b_peer_ref) = refs[5:9]
    outs, plain_ref = refs[9:-1], refs[-1]
    step = pl.program_id(0)
    half = D // 2
    shard = D // members

    @pl.when(step < pl.num_programs(0) - 1)
    def _():
        result = mm_tn(d_ref[...], h_ref[...]) + mm_tn(d_peer_ref[...], h_peer_ref[...])
        if relative:
            count = result.shape[1] // (4 * shard)
            for member in range(count):
                here = pl.ds(pl.multiple_of((step * count + member) * shard, 16), shard)
                for part in range(half // shard):
                    plain_ref[here, part * half : (part + 1) * half] = result[
                        part * shard : (part + 1) * shard, member * half : (member + 1) * half
                    ]
        else:
            outs[0][...] = result

    @pl.when(step == pl.num_programs(0) - 1)
    def _():
        result = mm_tn(n_ref[...], b_ref[...]) + mm_tn(n_peer_ref[...], b_peer_ref[...])
        if relative:
            plain_ref[:, 2 * D :] = result
            store_halves(*outs, table_ref, plain_ref, members, True)
        else:
            outs[1][...] = result


def adam_kernel(pick, *refs):
    table_ref, numbers_ref = refs[:2]
    master_ref, first_ref, second_ref = refs[2:5]
    sums, outs = refs[5:-3], refs[-3:]
    grads = pick(pl.program_id(0), table_ref[0], numbers_ref, sums)
    results = adam_update(
        master_ref[...], first_ref[...], second_ref[...], grads, rate_matrix, decay_matrix
    )
    for out_ref, result in zip(outs, results):
        out_ref[...] = result


SQUARE_LANES = tuple((i * D // 2, (i + 1) * D // 2) for i in range(3))


def section(refs, metas, lanes, target, offset=0):
    return [(ref, meta, lanes, target, offset) for ref, meta in zip(refs, metas)]


def blocks_of(group):
    return sum(array.shape[0] for array in group[0])


def whole_spec(shape):
    return pl.BlockSpec(shape, lambda *_: (0,) * len(shape), pipeline_mode=pl.Buffered(1))


def row_spec(block, width):
    return pl.BlockSpec((block, width), lambda i, *_: (i, 0))


COSTS = {'adam_square': 3, 'adam_qkv': 3, 'adam_expand': 3, 'adam_contract': 3, 'attend_teacher': 13, 'attend_student': 0.01, 'teacher_ffn': 0.01, 'student_ffn': 35, 'attend_back': 36, 'grad_expand': 15, 'grad_contract': 13, 'grad_joint': 7, 'grad_embed': 7}
smem_spec = pl.BlockSpec(memory_space=pltpu.SMEM)
any_spec = pl.BlockSpec(memory_space=pl.ANY)


def call(kernel, name, grid, ins, outs, scratch, flops, moved, prefetch=0, aliases={}):
    return pl.pallas_call(
        kernel,
        grid_spec=pltpu.PrefetchScalarGridSpec(
            num_scalar_prefetch=prefetch,
            grid=grid,
            in_specs=[spec for _, spec in ins[prefetch:]],
            out_specs=[spec for _, spec in outs],
            scratch_shapes=scratch,
        ),
        out_shape=[jax.ShapeDtypeStruct(*item) for item, _ in outs],
        input_output_aliases=aliases,
        compiler_params=pltpu.CompilerParams(vmem_limit_bytes=60 << 20),
        cost_estimate=pl.CostEstimate(
            flops=int(COSTS[name] * 1.15e9), transcendentals=0, bytes_accessed=1
        ),
        name=name,
    )(*[item for item, _ in ins])


def attend_teacher(real_rows, pad_rows, images, first, before, x, square, wj, vectors):
    rows, block = x.shape[0], images * pad_rows
    wj, vectors = ((item, whole_spec(item.shape)) for item in (wj, vectors))
    w0, w1 = ((square, pl.BlockSpec((None, D, D), lambda i, *_, at=at: (at, 0, 0))) for at in range(2))
    here = pl.BlockSpec((block, D), lambda i, *_: (first, 0))
    return call(
        functools.partial(attend_teacher_kernel, real_rows, pad_rows),
        "attend_teacher",
        (1,),
        [(x, here), w0, wj, w1, vectors] + ([] if before is None else [(before, any_spec)]),
        [(((rows, D), f32), here)],
        [pltpu.VMEM((block, 3 * D), bf16), pltpu.VMEM((block, D), bf16)],
        14 * rows * D * D,
        20e6,
        aliases={} if before is None else {5: 0},
    )[0]


def attend_student(real_rows, pad_rows, images, table, x, marks, vectors, square, joint):
    rows, block = x.shape[0], images * pad_rows
    arrays, metas = square[0] + joint[0], (square[1], joint[1])
    outs = [(D, f32), (D, f32), (3 * D, bf16), (3 * D, bf16)]
    return call(
        functools.partial(attend_student_kernel, real_rows, pad_rows, *metas),
        "attend_student",
        (rows // block,),
        [
            (table, smem_spec),
            (x, row_spec(block, D)),
            (marks, row_spec(block, 128)),
            (vectors, whole_spec(vectors.shape)),
        ]
        + [(array, any_spec) for array in arrays],
        [(((rows, width), kind), row_spec(block, width)) for width, kind in outs],
        [
            pltpu.VMEM((D, D), bf16),
            pltpu.VMEM((D, D), bf16),
            pltpu.VMEM((D, 3 * D), bf16),
            pltpu.SemaphoreType.DMA((3 * blocks_of(square) + blocks_of(joint),)),
        ],
        14 * rows * D * D,
        25e6,
    )


def teacher_ffn(real_rows, pad_rows, images, mid, weights, biases, vectors, sums):
    rows, block = mid.shape[0], images * pad_rows
    items = [biases, vectors, *weights]
    wholes = [(item, whole_spec(item.shape)) for item in items]
    last = [] if sums is None else [(sums, row_spec(block, D))]
    return call(
        functools.partial(teacher_ffn_kernel, real_rows, pad_rows, sums is not None),
        "teacher_ffn",
        (rows // block,),
        [(mid, row_spec(block, D))] + wholes + last,
        [(((rows, D), f32), row_spec(block, D))],
        [],
        16 * rows * D * D,
        15e6,
    )[0]


def student_ffn(pad_rows, images, table, scale, mid, targets, marks, vectors, expand, contract):
    rows, block = mid.shape[0], images * pad_rows
    outs = [(7 * D // 2, bf16), (7 * D // 2, bf16), (6 * D, bf16), (D, f32)]
    return call(
        functools.partial(student_ffn_kernel, expand[1], contract[1]),
        "student_ffn",
        (rows // block,),
        [
            (table, smem_spec),
            (scale, smem_spec),
            (mid, row_spec(block, D)),
            (targets, row_spec(block, D)),
            (marks, row_spec(block, 128)),
            (vectors, whole_spec(vectors.shape)),
        ]
        + [(array, any_spec) for array in (*expand[0], *contract[0])],
        [(((rows, width), kind), row_spec(block, width)) for width, kind in outs]
        + [(((16, D), f32), whole_spec((16, D)))],
        [
            pltpu.VMEM((D, 4 * D), bf16),
            pltpu.VMEM((4 * D, D), bf16),
            pltpu.VMEM((D, D), bf16),
            pltpu.VMEM((block, 4 * D), f32),
            pltpu.VMEM((block, D), bf16),
            pltpu.SemaphoreType.DMA((2 * blocks_of(expand) + blocks_of(contract),)),
        ],
        36 * rows * D * D,
        40e6,
    )


def attend_back(
    real_rows, pad_rows, images, table, dmid, joint, start, marks, vectors, square, qkv
):
    rows, block = dmid.shape[0], images * pad_rows
    arrays, metas = square[0] + qkv[0], (square[1], qkv[1])
    return call(
        functools.partial(attend_back_kernel, real_rows, pad_rows, *metas),
        "attend_back",
        (rows // block,),
        [
            (table, smem_spec),
            (dmid, row_spec(block, D)),
            (joint, row_spec(block, 3 * D)),
            (start, row_spec(block, D)),
            (marks, row_spec(block, 128)),
            (vectors, whole_spec(vectors.shape)),
        ]
        + [(array, any_spec) for array in arrays],
        [(((rows, 2 * D), bf16), row_spec(block, 2 * D))] * 2
        + [(((16, D), f32), whole_spec((16, D)))],
        [
            pltpu.VMEM((D, D), bf16),
            pltpu.VMEM((D, 3 * D), bf16),
            pltpu.VMEM((block, D), bf16),
            pltpu.VMEM((block, 3 * D), bf16),
            pltpu.VMEM((block, D), bf16),
            pltpu.SemaphoreType.DMA((2 * blocks_of(square) + blocks_of(qkv),)),
        ],
        20 * rows * D * D,
        25e6,
    )


def split_blocks(grads, members, y_first, place, own_y):
    top = jnp.max(jnp.abs(grads), axis=0, keepdims=True)
    rows = grads.shape[0] // members
    rels = jnp.array([rel for rel, _ in relative_places(members, False)])
    blocks = jnp.take(grads.reshape(members, rows, -1), rels ^ place, axis=0)
    if y_first:
        blocks = blocks.reshape(members, 2, rows // 2, -1)
        blocks = jnp.take(blocks, jnp.arange(2) ^ own_y, axis=1).swapaxes(0, 1)
    blocks = blocks.reshape(grads.shape)
    keep, sent = jnp.split(blocks, 2)
    exponent = column_exponents(top)
    tail = jnp.broadcast_to(exponent, (16, exponent.shape[1]))
    return keep, jnp.concatenate([sent * power_of_two(exponent), tail], 0), top


def half_outs(width, columns, index):
    heights = (D // 2, D // 2 + 16, 8)
    return [(((height, columns), f32), pl.BlockSpec((height, width), index)) for height in heights]


def weight_grad(name, table, members, y_first, steps, sides, own_b, peer_b):
    rows = own_b[0].shape[0]
    wide = D // 2
    relative = (D // members) % 32 == 0
    ins = [(table, None)]
    for own, peer, index, _ in sides:
        spec = pl.BlockSpec((rows, D), lambda j, _, index=index: (0, index(j)))
        ins += [(own, spec), (peer, spec)]
    for item, index in (own_b, peer_b):
        ins.append((item, pl.BlockSpec((rows, wide), lambda j, _, index=index: (0, index(j)))))
    if relative:
        outs = half_outs(wide, steps * wide, lambda j, _: (0, j))
    else:
        outs = [(((D, steps * wide), f32), pl.BlockSpec((D, wide), lambda j, _: (0, j)))]
    results = call(
        functools.partial(
            weight_grad_kernel, members, y_first, relative, tuple(side[3] for side in sides)
        ),
        name,
        (steps,),
        ins,
        outs,
        [pltpu.VMEM((D, wide), f32)],
        4 * rows * D * wide * steps,
        4 * D * wide * steps + 4 * rows * (D + wide * steps),
        prefetch=1,
    )
    if relative:
        return results
    return split_blocks(results[0], members, y_first, table[2], table[1])


def contract_grad(table, members, keep, two, two_peer):
    rows = two.shape[0]
    wide = D // 2
    shard = D // members
    relative = shard % 32 == 0
    steps = 4
    column = lambda item, index: (item, pl.BlockSpec((rows, wide), lambda i, _: (0, index)))
    moving = lambda item: (
        item,
        pl.BlockSpec((rows, D), lambda i, _: (0, 1 + jnp.minimum(i, steps - 1))),
    )
    left = pl.BlockSpec((rows, D), lambda i, _: (0, 0))
    if relative:
        assert 4 * shard == wide
        outs = half_outs(5 * wide, 5 * wide, lambda i, _: (0, 0))
        plain = (D, 5 * wide)
    else:
        outs = [
            (((wide, 4 * D), f32), pl.BlockSpec((wide, D), lambda i, _: (0, jnp.minimum(i, steps - 1)))),
            (((D, wide), f32), pl.BlockSpec((D, wide), lambda i, _: (0, 0))),
        ]
        plain = (8, 128)
    results = call(
        functools.partial(contract_grad_kernel, members, relative),
        "grad_contract",
        (steps + 1,),
        [(table, None), column(keep, 5), column(two_peer, 10), moving(two), moving(two_peer)]
        + [(two, left), (two_peer, left), column(keep, 4), column(two_peer, 11)],
        outs,
        [pltpu.VMEM(plain, f32)],
        16 * rows * D * wide,
        16 * D * wide + 16 * rows * D,
        prefetch=1,
    )
    if relative:
        return results
    blocks = results[0].reshape(wide // shard, shard, members, 4 * shard)
    blocks = blocks.transpose(2, 1, 0, 3).reshape(D, -1)
    whole = jnp.concatenate([blocks, results[1]], 1)
    return split_blocks(whole, members, True, table[2], table[1])


def adam(name, pick, table, numbers, masters, block, index, steps, sums):
    spec = pl.BlockSpec(block, lambda j, *_: index(j))
    ins = [(table, smem_spec), (numbers, smem_spec)] + [(item, spec) for item in masters]
    ins += [(item, pl.BlockSpec(shape, lambda j, *_, at=at: at(j))) for item, shape, at in sums]
    size = masters[0].size
    return call(
        functools.partial(adam_kernel, pick),
        name,
        (steps,),
        ins,
        [((masters[0].shape, f32), spec)] * 3,
        [],
        10 * size,
        32 * size,
    )


def after(value, *others):
    return lax.optimization_barrier((value, *others))[0]


def swap(values, bit):
    total = lax.axis_size("batch") * lax.axis_size("mlp")
    return lax.ppermute(values, ("batch", "mlp"), [(i, i ^ bit) for i in range(total)])


def batch_swap(values, bit):
    return swap(values, lax.axis_size("mlp") << bit)


def bit_of(axis, bit):
    return (lax.axis_index(axis) >> bit) & 1


def all_sum(values, bits):
    for bit in bits:
        values = values + swap(values, 1 << bit)
    return values


def pairs_sum(values, bits):
    while bits:
        one, bits = 1 << bits[0], bits[1:]
        if not bits:
            return values + swap(values, one)
        two, bits = 1 << bits[0], bits[1:]
        values = (values + swap(values, one)) + (swap(values, two) + swap(values, one | two))
    return values


def half_of(values, which, axis):
    width = values.shape[axis] // 2
    return lax.dynamic_slice_in_dim(values, which * width, width, axis)


def in_order(first, second, bit_value, axis):
    return jnp.where(
        bit_value == 0,
        jnp.concatenate([first, second], axis),
        jnp.concatenate([second, first], axis),
    )


def natural_rows(blocks, order):
    count = len(order)
    full = blocks.reshape((2,) * count + blocks.shape[1:])
    for place in range(count):
        flip = bit_of("batch", order[count - 1 - place])
        full = jnp.where(flip == 0, full, jnp.flip(full, place))
    source = [count - 1 - order.index(bit) for bit in reversed(range(count))]
    full = full.transpose(source + [count, count + 1])
    return full.reshape(1, -1, full.shape[-1])


def blocks_group(held, last, order, row):
    members = 1 << len(order)
    height = held.shape[1]
    if height % 16 != 0:
        return whole_group(natural_rows(jnp.concatenate([held, last], 0), order), row)
    entries = [
        lax.axis_index("batch") ^ sum(((p >> j) & 1) << bit for j, bit in enumerate(order))
        for p in range(members)
    ]
    arrays = [held, last, swap(held, 1), swap(last, 1)]
    metas = [
        (0, height, height, row + part * (members // 2), near)
        for near in (True, False)
        for part in (0, 1)
    ]
    return (arrays, tuple(metas)), entries


def sides_group(own, peer, other, members, row):
    height = own.shape[0] // members
    own, peer, other = (item.reshape(members, height, -1) for item in (own, peer, other))
    if height % 16 != 0:
        both = in_order(own[:, None], other[:, None], bit_of("mlp", 1), 1)
        return whole_group(both.reshape(1, 2 * members * height, -1), row)[0]
    arrays = [own, other, peer, swap(other, 1)]
    metas = [(side, 2 * height, height, row, near) for near in (True, False) for side in (1, 2)]
    return arrays, tuple(metas)


def whole_group(near, row):
    metas = tuple((0, 0, near.shape[1], row, side) for side in (True, False))
    return ([near, swap(near, 1)], metas), []


def power_of_two(exponent):
    size = jnp.abs(exponent).astype(jnp.int32)
    result = jnp.ones_like(exponent)
    for bit in range(7):
        factor = jnp.where(exponent > 0, 2.0 ** (1 << bit) if bit < 7 else 1.0, 2.0 ** -(1 << bit))
        result = jnp.where((size >> bit) & 1 == 1, result * factor, result)
    return result


def low_half(values):
    return lax.reduce_precision(values, 5, 10).astype(jnp.float16)


def low_half(values):
    return lax.reduce_precision(values, 5, 10).astype(jnp.float16)


def packed(values, exponent):
    tail = jnp.broadcast_to(exponent, (16, exponent.shape[1]))
    return low_half(jnp.concatenate([values * jnp.exp2(exponent), tail], 0))


class Reduction:
    def __init__(self, blocks, order, y_first):
        self.keep, sent, _ = blocks
        self.exponent = sent[-1:]
        self.hops = (["y"] if y_first else []) + list(order) + ["last"]
        self.y_first = y_first
        self.sent = low_half(sent)
        self.other = None

    def fetch(self):
        if self.other is None:
            at_y = self.hops[0] in ("y", "last")
            self.other = swap(self.sent, 2) if at_y else batch_swap(self.sent, self.hops[0])
        return self.other

    def receive(self, *gates):
        other = after(self.fetch(), *gates)
        self.other = None
        bit = self.hops.pop(0)
        rows = other.shape[0] - 16
        exponent = other[-1:].astype(f32)
        if bit == "last":
            own = self.sent[:rows].astype(f32) * power_of_two(-self.sent[-1:].astype(f32))
            other = other[:rows].astype(f32) * power_of_two(-exponent)
            if self.y_first:
                self.sums = in_order(own, other, bit_of("mlp", 1), 0)
            else:
                self.sums = own + other
            return self
        factor = jnp.exp2(-exponent)
        self.exponent = jnp.minimum(self.exponent, exponent) - 1.0
        half = rows // 2 if len(self.hops) > 1 else 0
        sums = self.keep[half:] + other[half:rows].astype(f32) * factor
        self.sent = packed(sums, self.exponent)
        if half:
            self.keep = self.keep[:half] + other[:half].astype(f32) * factor
        return self


def adam_update(master, first, second, gradient, step_rate, weight_decay):
    moment = beta_first * first + (1.0 - beta_first) * gradient
    variance = beta_second * second + (1.0 - beta_second) * gradient * gradient
    corrected = moment / (1.0 - beta_first**STEP)
    scaled = variance / (1.0 - beta_second**STEP)
    updated = master - step_rate * (
        corrected / (jnp.sqrt(scaled) + adam_eps) + weight_decay * master
    )
    return (moment, variance, updated)


def on_device(
    patches,
    mask,
    student_square,
    student_qkv,
    student_expand,
    student_contract,
    student_vectors,
    first_square,
    first_qkv,
    first_expand,
    first_contract,
    first_vectors,
    second_square,
    second_qkv,
    second_expand,
    second_contract,
    second_vectors,
    teacher_square,
    teacher_qkv,
    teacher_expand,
    teacher_contract,
    teacher_vectors,
):
    members = lax.axis_size("batch")
    count = members.bit_length() - 1
    mlp_bits = lax.axis_size("mlp").bit_length() - 1
    near = list(range(count))
    far = near[::-1]
    batch_bits = range(mlp_bits, mlp_bits + count)
    shard_rows = D // members
    core, own_y = bit_of("mlp", 0), bit_of("mlp", 1)
    place = lax.axis_index("batch")
    group, real_rows = mask.shape
    pad_rows = -(-real_rows // 16) * 16
    half = D // 2

    pad = ((0, 0), (0, pad_rows - real_rows))
    x = jnp.pad(patches, pad + ((0, 0),)).reshape(-1, D)
    marks = jnp.pad(mask.astype(f32), pad).reshape(-1)
    wide_marks = jnp.broadcast_to(marks[:, None], (marks.shape[0], 128))

    square_held = jnp.concatenate(
        [half_of(student_square[i], core, 1) for i in range(2)]
        + [lax.dynamic_slice_in_dim(student_qkv, core * 3 * half, half, 1)],
        1,
    ).astype(bf16)[None]
    qkv_held = lax.dynamic_slice_in_dim(student_qkv, core * 3 * half + half, D, 1)
    qkv_held = qkv_held.astype(bf16)[None]
    expand_held = jnp.concatenate(
        [half_of(half_of(item, core, 1), own_y, 0) for item in (student_expand, student_square[2])],
        1,
    )
    expand_own = lax.all_gather(expand_held.astype(bf16), "batch", axis=0, tiled=True)
    contract_near = lax.all_gather(
        half_of(student_contract, core, 1).astype(bf16), "batch", axis=0, tiled=True
    )
    low_vectors = lax.reduce_precision(student_vectors, 8, 7)
    small = lax.dynamic_update_slice(
        jnp.zeros((low_vectors.shape[0], D), f32), low_vectors, (0, place * shard_rows)
    )
    small = jnp.concatenate([small, jnp.full((1, D), jnp.sum(marks))], 0)

    images = min(group, 2)
    sizes = (real_rows, pad_rows, images)
    teacher_weights = (teacher_square, teacher_qkv, teacher_vectors)
    own = lax.axis_index("mlp")
    biases = jnp.concatenate(
        [lax.dynamic_slice_in_dim(teacher_vectors, 8 + (own ^ part), 1, 0) for part in range(4)]
    )
    tmid, runs, tsum, done = None, 0, None, ()
    square_order, qkv_order = far, near[:1] + far[:-1]
    for hop in range(count):
        sends = lax.optimization_barrier((square_held, qkv_held, small, *done))[:3]
        square_held, qkv_held, small = sends
        square_last = batch_swap(square_held, square_order[hop])
        qkv_last = batch_swap(qkv_held, qkv_order[hop])
        small_last = batch_swap(small, near[hop])
        if runs < group // images:
            tmid = attend_teacher(*sizes, runs, tmid, after(x, *sends), *teacher_weights)
            runs += 1
            done = (tmid,)
            if runs == 1:
                teacher_own = jnp.concatenate([after(teacher_expand, tmid), teacher_contract], 1)
                teacher_y = swap(teacher_own, 2)
                teacher_core = swap(teacher_own, 1)
        elif tsum is None:
            tsum = teacher_ffn(
                *sizes,
                after(tmid, *sends, expand_own),
                (teacher_own, teacher_core),
                biases[:2],
                teacher_vectors,
                None,
            )
            done = (tsum,)
        if hop + 1 < count:
            square_held = jnp.concatenate([square_held, square_last], 0)
            qkv_held = jnp.concatenate([qkv_held, qkv_last], 0)
        small = small + after(small_last, *done)
    vectors = small[:-1]
    square_held, qkv_held, square_last, qkv_last = lax.optimization_barrier(
        (square_held, qkv_held, square_last, qkv_last, *done, teacher_y, small)
    )[:4]
    square, square_rows = blocks_group(square_held, square_last, square_order, 3)
    qkv, qkv_rows = blocks_group(qkv_held, qkv_last, qkv_order, 3 + len(square_rows))
    entries = [core, own_y, place] + square_rows + qkv_rows + list(range(members))
    table = jnp.stack([jnp.asarray(entry, jnp.int32) for entry in entries])

    marked = all_sum(after(small, square_last, qkv_last)[-1:, :128], [0])
    teacher_far = swap(after(teacher_y, square_last, qkv_last), 1)
    masked_count = all_sum(marked, range(1, mlp_bits))
    expand_y = swap(after(expand_own, square_last, qkv_last), 2)
    targets = teacher_ffn(
        *sizes,
        after(tmid, marked, expand_own),
        (teacher_y, teacher_far),
        biases[2:],
        teacher_vectors,
        tsum,
    )
    start, mid, joint, act = attend_student(
        *sizes, table, after(x, targets), wide_marks, vectors, square, qkv
    )
    mid, expand_y, expand_peer = lax.optimization_barrier((mid, expand_y, swap(expand_own, 1)))
    masked_count = masked_count[0, 0]
    row = 3 + len(square_rows + qkv_rows)
    expand = sides_group(expand_own, expand_peer, expand_y, members, row)
    contract, _ = whole_group(after(contract_near, mid)[None], 0)
    act_peer = swap(after(act, mid), 1)
    scale = (2.0 / (masked_count * D)).reshape(1)
    keep, one, two, dmid, ffn_sums = student_ffn(
        pad_rows, images, table, scale, mid, targets, wide_marks, vectors, expand, contract
    )
    one_peer = swap(after(one, act_peer), 1)
    two_peer = swap(after(two, one_peer), 1)

    blocks = weight_grad(
        "grad_expand",
        table,
        members,
        False,
        5,
        [
            (one, one_peer, lambda j: 0, (0, 1, 2, 3)),
            (act, act_peer, lambda j: 0, (4,)),
        ],
        (keep, lambda j: jnp.where(j == 4, 6, j)),
        (one_peer, lambda j: jnp.where(j == 4, 6, j + 2)),
    )
    to_expand = Reduction(blocks, near, False)
    blocks = contract_grad(table, members, keep, two, after(two_peer, to_expand.sent))
    to_contract = Reduction(blocks, near, True)
    keep3, send3, att_sums = attend_back(
        *sizes,
        table,
        after(dmid, to_contract.sent),
        joint,
        start,
        wide_marks,
        vectors,
        square,
        qkv,
    )
    send3_peer = swap(send3, 1)
    to_expand.receive(att_sums)
    to_contract.receive()

    total = jnp.concatenate([ffn_sums[:12], att_sums[:6]], 0)
    total_bits = list(range(mlp_bits + count))

    def total_hop(*gates):
        nonlocal total
        if total_bits:
            total = after(total, *gates)
            total = total + swap(total, 1 << total_bits.pop(0))

    total_hop(to_expand.sent, to_contract.sent)
    blocks = weight_grad(
        "grad_joint",
        table,
        members,
        False,
        3,
        [(act, act_peer, lambda j: 1, (0, 1, 2))],
        (keep3, lambda j: j),
        (after(send3_peer, to_expand.sent, to_contract.sent), lambda j: j),
    )
    to_first = Reduction(blocks, near, False)
    to_expand.receive(to_first.sent)
    to_contract.receive(to_first.sent)
    total_hop(to_first.sent)
    blocks = weight_grad(
        "grad_embed",
        table,
        members,
        True,
        1,
        [(act, act_peer, lambda j: 2, (0,))],
        (keep3, lambda j: j + 3),
        (after(send3_peer, to_first.sent, to_expand.sent, to_contract.sent), lambda j: j + 3),
    )
    keep_rows, sent_rows, top = blocks
    sent_rows = after(sent_rows, to_first.fetch())
    to_second = Reduction((keep_rows, sent_rows, top), near, True)
    others = to_expand.fetch(), to_contract.fetch()
    to_first.receive(to_second.sent)
    to_second.receive(*others)
    gates = (to_second.sent, to_first.sent)
    to_expand.receive(*gates)
    to_contract.receive(*gates)
    moving = [to_first, to_second, to_contract, to_expand]
    while moving:
        total_hop(*gates)
        for item in list(moving):
            item.receive(*gates)
            if not item.hops:
                moving.remove(item)
        gates = (moving[0].sent,) if moving else ()
    while total_bits:
        total_hop()
    ffn_total, att_total = total[:12], total[12:]

    own_sums = [item.sums for item in (to_expand, to_contract, to_first, to_second)]
    vector_total = jnp.concatenate(
        [
            att_total[5:6],
            att_total[4:5],
            att_total[2:4],
            att_total[0:2],
            ffn_total[11:12],
            ffn_total[9:11],
            ffn_total[5:9],
            ffn_total[4:5],
            ffn_total[2:4],
            ffn_total[1:2],
        ]
    )
    loss_sum = jnp.sum(ffn_total[0])
    vector_grad = lax.dynamic_slice_in_dim(vector_total, place * shard_rows, shard_rows, 1)
    squares = 0.5 * jnp.sum(vector_grad * vector_grad)
    for member in own_sums:
        squares = squares + jnp.sum(member * member)
    squares = pairs_sum(jnp.full((1, 128), squares), [0, *batch_bits])
    grad_norm = jnp.sqrt(squares[0, 0])
    factor = clip_bound / jnp.maximum(grad_norm, clip_bound)

    pairs = [(item, swap(item, 1)) for item in own_sums]
    numbers = factor.reshape(1)

    def picked(is_own, own_ref, peer_ref):
        return jnp.where(is_own, own_ref[...], peer_ref[...])

    def pick_square(step, core_of, numbers_ref, refs):
        sides = []
        for near in (True, False):
            parts = [refs[2 * i + (0 if near else 1)][...] for i in range(3)]
            side = jnp.where(step == 0, parts[0], jnp.where(step == 1, parts[1], parts[2]))
            sides.append(side)
        left = jnp.where(core_of == 0, sides[0], sides[1])
        right = jnp.where(core_of == 0, sides[1], sides[0])
        return (jnp.concatenate([left, right], 1) * numbers_ref[0])[None]

    def pick_joint(step, core_of, numbers_ref, refs):
        return picked(step == core_of, *refs) * numbers_ref[0]

    def pick_expand(step, core_of, numbers_ref, refs):
        return picked(step == core_of, *refs) * numbers_ref[0]

    def pick_contract(step, core_of, numbers_ref, refs):
        grads = picked(step == core_of, *refs)
        if grads.shape[0] != 4 * shard_rows:
            parts = half // shard_rows
            grads = [grads[:, i * 4 * shard_rows : (i + 1) * 4 * shard_rows] for i in range(parts)]
            grads = jnp.concatenate(grads, 0).T
        return grads * numbers_ref[0]

    def pieces(index, at, width=half):
        return [(item, (shard_rows, width), at) for item in pairs[index]]

    square_results = adam(
        "adam_square",
        pick_square,
        table,
        numbers,
        (student_square, first_square, second_square),
        (1, shard_rows, D),
        lambda j: (j, 0, 0),
        3,
        pieces(3, lambda j: (0, 0)) + pieces(0, lambda j: (0, 4)) + pieces(1, lambda j: (0, 4)),
    )
    qkv_results = adam(
        "adam_qkv",
        pick_joint,
        table,
        numbers,
        (student_qkv, first_qkv, second_qkv),
        (shard_rows, 3 * half),
        lambda j: (0, j),
        2,
        pieces(2, lambda j: (0, 0), 3 * half),
    )
    expand_results = adam(
        "adam_expand",
        pick_expand,
        table,
        numbers,
        (student_expand, first_expand, second_expand),
        (shard_rows, 4 * half),
        lambda j: (0, j),
        2,
        pieces(0, lambda j: (0, 0), 4 * half),
    )
    if 4 * shard_rows == half:
        contract_pieces = pieces(1, lambda j: (0, 0), 4 * half)
    else:
        contract_pieces = []
        for item in pairs[1]:
            item = item[:, : 4 * half].reshape(shard_rows, half // shard_rows, 4 * shard_rows)
            item = item.swapaxes(0, 1).reshape(half, 4 * shard_rows).T
            contract_pieces.append((item, item.shape, lambda j: (0, 0)))
    contract_results = adam(
        "adam_contract",
        pick_contract,
        table,
        numbers,
        (student_contract, first_contract, second_contract),
        (4 * shard_rows, half),
        lambda j: (0, j),
        2,
        contract_pieces,
    )
    vector_results = adam_update(
        student_vectors, first_vectors, second_vectors, vector_grad * factor, rate_vector, 0.0
    )
    return (
        loss_sum,
        masked_count,
        grad_norm,
        *square_results,
        *qkv_results,
        *expand_results,
        *contract_results,
        *vector_results,
    )


def solution(mesh):
    return jax.shard_map(
        on_device,
        mesh=mesh,
        in_specs=(
            P(("batch", "mlp"), None, None),
            P(("batch", "mlp"), None),
            P(None, "batch", None),
            P("batch", None),
            P("batch", None),
            P("batch", None),
            P(None, "batch"),
            P(None, "batch", None),
            P("batch", None),
            P("batch", None),
            P("batch", None),
            P(None, "batch"),
            P(None, "batch", None),
            P("batch", None),
            P("batch", None),
            P("batch", None),
            P(None, "batch"),
            P(),
            P(),
            P(None, "mlp"),
            P("mlp", None),
            P(),
        ),
        out_specs=(
            P(),
            P(),
            P(),
            P(None, "batch", None),
            P(None, "batch", None),
            P(None, "batch", None),
            P("batch", None),
            P("batch", None),
            P("batch", None),
            P("batch", None),
            P("batch", None),
            P("batch", None),
            P("batch", None),
            P("batch", None),
            P("batch", None),
            P(None, "batch"),
            P(None, "batch"),
            P(None, "batch"),
        ),
        check_vma=False,
    )
```

```python
import functools

import jax
import jax.numpy as jnp
from jax import lax
from jax.experimental import pallas as pl
from jax.experimental.pallas import tpu as pltpu
from jax.sharding import PartitionSpec as P

D = 768
HEAD_DIM = 64
PAIR = 2 * HEAD_DIM
UNROLL = 3
STEP = 10


norm_eps = 1e-06
inst_eps = 1e-05
clip_bound = 0.001
rate_matrix = 0.05
rate_vector = 0.5
decay_matrix = 0.05
beta_first = 0.9
beta_second = 0.999
adam_eps = 1e-08
f32 = jnp.float32
bf16 = jnp.bfloat16


def mm(left, right):
    return lax.dot_general(left, right, (((1,), (0,)), ((), ())), preferred_element_type=f32)


def mm_nt(left, right):
    return lax.dot_general(left, right, (((1,), (1,)), ((), ())), preferred_element_type=f32)


def mm_tn(left, right):
    return lax.dot_general(left, right, (((0,), (0,)), ((), ())), preferred_element_type=f32)


def normed_rows(values):
    centred = values - jnp.mean(values, axis=-1, keepdims=True)
    variance = jnp.mean(centred * centred, axis=-1, keepdims=True)
    scale = lax.rsqrt(variance + norm_eps)
    return centred * scale, scale


def norm_back(xhat, scale, gain, grads):
    scaled = grads * gain
    mean_one = jnp.mean(scaled, axis=-1, keepdims=True)
    mean_two = jnp.mean(scaled * xhat, axis=-1, keepdims=True)
    back = scale * (scaled - mean_one - xhat * mean_two)
    return back, total_rows(grads * xhat), total_rows(grads)


def piece_copies(table_ref, semaphores, first, pieces):
    core, own_y = table_ref[0], table_ref[1]
    copies = []
    for ref, (side, unit, height, row, near), lanes, target, offset in pieces:
        width = lanes[1] - lanes[0]
        column = (core if near else 1 - core) * (target.shape[1] // 2) + offset
        column = pl.multiple_of(column, 128)
        base = (0, own_y * height, (1 - own_y) * height)[side]
        for block in range(ref.shape[0]):
            place = 0 if unit == 0 else pl.multiple_of(table_ref[row + block] * unit + base, 16)
            copies.append(
                pltpu.make_async_copy(
                    ref.at[block, :, pl.ds(lanes[0], width)],
                    target.at[pl.ds(place, height), pl.ds(column, width)],
                    semaphores.at[first + len(copies)],
                )
            )
    return copies


def total_rows(values):
    return jnp.sum(values, axis=0, keepdims=True)


def head_masks(rows):
    lane = lax.broadcasted_iota(jnp.int32, (rows, PAIR), 1)
    return lane < HEAD_DIM


def stacked(values, low):
    zero = jnp.zeros_like(values)
    return jnp.concatenate([jnp.where(low, values, zero), jnp.where(low, zero, values)], axis=0)


def pair_probs(stack, keys, real_rows):
    scores = mm_nt(stack, keys)
    column = lax.broadcasted_iota(jnp.int32, scores.shape, 1)
    scores = jnp.where(column < real_rows, scores, -1e30)
    shifted = jnp.exp(scores - jnp.max(scores, axis=-1, keepdims=True))
    return shifted * (1.0 / jnp.sum(shifted, axis=-1, keepdims=True))


def attend_block(is_student, real_rows, pad_rows, x_ref, marks_ref, weights, vec_ref, outs, waits):
    w0_ref, wj_ref, w1_ref = weights
    start_ref, mid_ref, joint_ref, act_ref = outs
    at = (lambda student, teacher: student if is_student else teacher)
    vec = lambda row: vec_ref[row : row + 1, :]
    block = x_ref.shape[0]
    if is_student:
        waits[0]()
    start = mm(x_ref[...], w0_ref[...]) + vec(0)
    if is_student:
        start = jnp.where(marks_ref[:, :1] > 0, vec(1), start)
    start_ref[...] = start
    xhat, _ = normed_rows(start)
    normed = (xhat * vec(at(2, 1)) + vec(at(3, 2))).astype(bf16)
    if is_student:
        act_ref[:, D : 2 * D] = normed
        act_ref[:, 2 * D :] = x_ref[...]
    biases = (vec(at(4, 3)), None, vec(at(5, 4)))
    if is_student:
        waits[1]()
    for part in range(3):
        cols = slice(part * D, (part + 1) * D)
        mixed = mm(normed, wj_ref[:, cols])
        if biases[part] is not None:
            mixed = mixed + biases[part]
        joint_ref[:, cols] = mixed.astype(bf16)
    low = head_masks(pad_rows)

    def one_pair(step, carry):
        image = step // (D // PAIR)
        col = pl.multiple_of((step % (D // PAIR)) * PAIR, PAIR)
        rows = pl.ds(pl.multiple_of(image * pad_rows, 16), pad_rows)
        queries = joint_ref[rows, pl.ds(col, PAIR)] * HEAD_DIM ** (-0.5)
        keys = joint_ref[rows, pl.ds(col + D, PAIR)]
        values = joint_ref[rows, pl.ds(col + 2 * D, PAIR)]
        probs = pair_probs(stacked(queries.astype(bf16), low), keys, real_rows).astype(bf16)
        mixed = mm(probs, values)
        act_ref[rows, pl.ds(col, PAIR)] = jnp.where(
            low, mixed[:pad_rows], mixed[pad_rows:]
        ).astype(bf16)
        return carry

    lax.fori_loop(0, (block // pad_rows) * (D // PAIR), one_pair, 0, unroll=2 * UNROLL)
    attended = act_ref[:, :D]
    if is_student:
        waits[2]()
    mid_ref[...] = start_ref[...] + mm(attended, w1_ref[...]) + vec(at(6, 5))


def clear_at_first(*refs):
    @pl.when(pl.program_id(0) == 0)
    def _():
        for ref in refs:
            ref[...] = jnp.zeros_like(ref)


def place_at_first(table_ref, semaphores, *groups):
    all_copies, count = [], 0
    for pieces in groups:
        all_copies.append(piece_copies(table_ref, semaphores, count, pieces))
        count += len(all_copies[-1])

    @pl.when(pl.program_id(0) == 0)
    def _():
        for copies in all_copies:
            for copy in copies:
                copy.start()

    def wait_for(copies):
        @pl.when(pl.program_id(0) == 0)
        def _():
            for copy in copies:
                copy.wait()

    return [functools.partial(wait_for, copies) for copies in all_copies]


def attend_teacher_kernel(real_rows, pad_rows, *refs):
    x_ref, w0_ref, wj_ref, w1_ref, vec_ref = refs[:5]
    mid_ref, joint_ref, att_ref = refs[-3:]
    attend_block(
        False,
        real_rows,
        pad_rows,
        x_ref,
        None,
        (w0_ref, wj_ref, w1_ref),
        vec_ref,
        (mid_ref, mid_ref, joint_ref, att_ref),
        None,
    )


def attend_student_kernel(real_rows, pad_rows, metas, joint_metas, *refs):
    (table_ref, x_ref, marks_ref, vec_ref) = refs[:4]
    count = len(metas)
    piece_refs, joint_refs = refs[4 : 4 + count], refs[4 + count : 4 + 2 * count]
    (start_ref, mid_ref, joint_ref, act_ref) = refs[4 + 2 * count : 8 + 2 * count]
    (w0_ref, w1_ref, wj_ref, semaphores) = refs[8 + 2 * count :]
    joint_pieces = section(piece_refs, metas, SQUARE_LANES[2], wj_ref)
    joint_pieces += section(joint_refs, joint_metas, (0, D), wj_ref, D // 2)
    waits = place_at_first(
        table_ref,
        semaphores,
        section(piece_refs, metas, SQUARE_LANES[0], w0_ref),
        joint_pieces,
        section(piece_refs, metas, SQUARE_LANES[1], w1_ref),
    )
    attend_block(
        True,
        real_rows,
        pad_rows,
        x_ref,
        marks_ref,
        (w0_ref, wj_ref, w1_ref),
        vec_ref,
        (start_ref, mid_ref, joint_ref, act_ref),
        waits,
    )


def gelu_half(values):
    return 0.5 * (1.0 + lax.erf(values * 0.7071067811865476))


def teacher_ffn_kernel(real_rows, pad_rows, is_last, *refs):
    mid_ref, bias_ref, vec_ref = refs[:3]
    parts = bias_ref.shape[0]
    rest = refs[3 + parts :]
    mid = mid_ref[...]
    xhat, _ = normed_rows(mid)
    normed = (xhat * vec_ref[6:7, :] + vec_ref[7:8, :]).astype(bf16)
    total = rest[0][...] if is_last else None
    for part, both_ref in enumerate(refs[3 : 3 + parts]):
        pre = mm(normed, both_ref[:, :D]) + bias_ref[part : part + 1, :]
        hidden = (pre * gelu_half(pre)).astype(bf16)
        piece = mm(hidden, both_ref[:, D:])
        total = piece if total is None else total + piece
    out_ref = rest[-1]
    if not is_last:
        out_ref[...] = total
        return
    total = total + vec_ref[12:13, :]
    valid = lax.broadcasted_iota(jnp.int32, (pad_rows, D), 0) < real_rows
    for image in range(mid_ref.shape[0] // pad_rows):
        rows = slice(image * pad_rows, (image + 1) * pad_rows)
        result = None
        for values in (mid[rows], total[rows]):
            mean = total_rows(jnp.where(valid, values, 0.0)) / real_rows
            centred = values - mean
            variance = total_rows(jnp.where(valid, centred * centred, 0.0)) / real_rows
            normal = centred * lax.rsqrt(variance + inst_eps)
            result = normal if result is None else result + normal
        out_ref[rows, :] = 0.5 * result


def student_ffn_kernel(expand_metas, contract_metas, *refs):
    (table_ref, scale_ref, mid_ref, target_ref, marks_ref, vec_ref) = refs[:6]
    counts = (len(expand_metas), len(contract_metas))
    expand_refs, contract_refs = refs[6 : 6 + counts[0]], refs[6 + counts[0] : 6 + sum(counts)]
    (keep_ref, one_ref, two_ref, dmid_ref, sum_ref) = refs[6 + sum(counts) : 11 + sum(counts)]
    (we_ref, wc_ref, wh_ref, slope_ref, half_ref, semaphores) = refs[11 + sum(counts) :]
    clear_at_first(sum_ref)
    expand_wait, contract_wait, head_wait = place_at_first(
        table_ref,
        semaphores,
        section(expand_refs, expand_metas, (0, 2 * D), we_ref),
        section(contract_refs, contract_metas, (0, D // 2), wc_ref),
        section(expand_refs, expand_metas, (2 * D, 5 * D // 2), wh_ref),
    )
    core = table_ref[0]

    def add(row, values):
        sum_ref[pl.ds(row, 1), :] += values

    def add_grad(row, grads):
        add(row, total_rows(grads.astype(f32)))

    def halves(keep_cols, send_ref, send_cols, grads):
        half_ref[...] = grads
        width = D // 2
        keep_ref[:, keep_cols : keep_cols + width] = half_ref[
            :, pl.ds(pl.multiple_of(core * width, 128), width)
        ]
        send_ref[:, send_cols : send_cols + width] = half_ref[
            :, pl.ds(pl.multiple_of((1 - core) * width, 128), width)
        ]

    vec = lambda row: vec_ref[row : row + 1, :]
    mid = mid_ref[...]
    xhat2, scale2 = normed_rows(mid)
    n2 = (xhat2 * vec(7) + vec(8)).astype(bf16)
    one_ref[:, :D] = n2
    total = None
    expand_wait()
    for part in range(4):
        cols = slice(part * D, (part + 1) * D)
        pre = mm(n2, we_ref[:, cols]) + vec(9 + part)
        half = gelu_half(pre)
        slope_ref[:, cols] = half + pre * (jnp.exp(-0.5 * pre * pre) * 0.3989422804014327)
        hidden = (pre * half).astype(bf16)
        two_ref[:, (part + 1) * D : (part + 2) * D] = hidden
        if part == 0:
            contract_wait()
        piece = mm(hidden, wc_ref[cols, :])
        total = piece if total is None else total + piece
    final = mid + total + vec(13)
    xhat3, scale3 = normed_rows(final)
    n3 = (xhat3 * vec(14) + vec(15)).astype(bf16)
    two_ref[:, :D] = n3
    head_wait()
    error = marks_ref[:, :1] * (mm(n3, wh_ref[...]) + vec(16) - target_ref[...])
    add(0, total_rows(error * error))
    dpred = (error * scale_ref[0]).astype(bf16)
    halves(2 * D, two_ref, 11 * D // 2, dpred)
    add_grad(1, dpred)
    dfinal, gain3, shift3 = norm_back(xhat3, scale3, vec(14), mm_nt(dpred, wh_ref[...]))
    add(2, gain3)
    add(3, shift3)
    dbranch = dfinal.astype(bf16)
    halves(2 * D + D // 2, two_ref, 5 * D, dbranch)
    add_grad(4, dbranch)
    dn2 = None
    for side in range(2):
        for part in range(2):
            chunk = 2 * (core ^ side) + part
            cols = pl.ds(pl.multiple_of(chunk * D, 128), D)
            dpre = (mm_nt(dbranch, wc_ref[cols, :]) * slope_ref[:, cols]).astype(bf16)
            if side == 0:
                keep_ref[:, part * D : (part + 1) * D] = dpre
            else:
                one_ref[:, (1 + part) * D : (2 + part) * D] = dpre
            add_grad(5 + chunk, dpre)
            piece = mm_nt(dpre, we_ref[:, cols])
            dn2 = piece if dn2 is None else dn2 + piece
    dmid, gain2, shift2 = norm_back(xhat2, scale2, vec(7), dn2)
    add(9, gain2)
    add(10, shift2)
    dmid = dfinal + dmid
    dmid_ref[...] = dmid
    datt = dmid.astype(bf16)
    halves(3 * D, one_ref, 3 * D, datt)
    add(11, total_rows(datt.astype(f32)))


def attend_back_kernel(real_rows, pad_rows, metas, joint_metas, *refs):
    (table_ref, dmid_ref, joint_ref, start_ref, marks_ref, vec_ref) = refs[:6]
    count = len(metas)
    piece_refs, joint_refs = refs[6 : 6 + count], refs[6 + count : 6 + 2 * count]
    (keep_ref, send_ref, sum_ref) = refs[6 + 2 * count : 9 + 2 * count]
    (w1_ref, wj_ref, grad_ref, djoint_ref, half_ref, semaphores) = refs[9 + 2 * count :]
    clear_at_first(sum_ref)
    joint_pieces = section(piece_refs, metas, SQUARE_LANES[2], wj_ref)
    joint_pieces += section(joint_refs, joint_metas, (0, D), wj_ref, D // 2)
    out_wait, joint_wait = place_at_first(
        table_ref, semaphores, section(piece_refs, metas, SQUARE_LANES[1], w1_ref), joint_pieces
    )
    out_wait()
    core = table_ref[0]

    def add(row, values):
        sum_ref[row : row + 1, :] += values

    def halves(column, source_ref, width):
        keep_ref[:, column : column + width] = source_ref[
            :, pl.ds(pl.multiple_of(core * width, 128), width)
        ]
        send_ref[:, column : column + width] = source_ref[
            :, pl.ds(pl.multiple_of((1 - core) * width, 128), width)
        ]

    vec = lambda row: vec_ref[row : row + 1, :]
    block = dmid_ref.shape[0]
    datt = dmid_ref[...].astype(bf16)
    grad_ref[...] = mm_nt(datt, w1_ref[...]).astype(bf16)
    low = head_masks(pad_rows)

    def one_pair(step, carry):
        image = step // (D // PAIR)
        col = pl.multiple_of((step % (D // PAIR)) * PAIR, PAIR)
        rows = pl.ds(pl.multiple_of(image * pad_rows, 16), pad_rows)
        queries = joint_ref[rows, pl.ds(col, PAIR)] * HEAD_DIM ** (-0.5)
        keys = joint_ref[rows, pl.ds(col + D, PAIR)]
        values = joint_ref[rows, pl.ds(col + 2 * D, PAIR)]
        stack = stacked(queries.astype(bf16), low)
        dstack = stacked(grad_ref[rows, pl.ds(col, PAIR)], low)
        probs = pair_probs(stack, keys, real_rows)
        dprobs = mm_nt(dstack, values)
        dvalues = mm_tn(probs.astype(bf16), dstack)
        weighted = probs * dprobs
        dscores = (weighted - probs * jnp.sum(weighted, axis=-1, keepdims=True)).astype(bf16)
        both = mm(dscores, keys) * HEAD_DIM ** (-0.5)
        dqueries = jnp.where(low, both[:pad_rows], both[pad_rows:])
        dkeys = mm_tn(dscores, stack)
        djoint_ref[rows, pl.ds(col, PAIR)] = dqueries.astype(bf16)
        djoint_ref[rows, pl.ds(col + D, PAIR)] = dkeys.astype(bf16)
        djoint_ref[rows, pl.ds(col + 2 * D, PAIR)] = dvalues.astype(bf16)
        return carry

    lax.fori_loop(0, (block // pad_rows) * (D // PAIR), one_pair, 0, unroll=2 * UNROLL)
    halves(0, djoint_ref, 3 * D // 2)
    joint_wait()
    dnormed = None
    for part in range(3):
        cols = slice(part * D, (part + 1) * D)
        grads = djoint_ref[:, cols]
        if part != 1:
            add(part // 2, total_rows(grads.astype(f32)))
        piece = mm_nt(grads, wj_ref[:, cols])
        dnormed = piece if dnormed is None else dnormed + piece
    xhat, scale = normed_rows(start_ref[...])
    dstart, gain, shift = norm_back(xhat, scale, vec(2), dnormed)
    add(2, gain)
    add(3, shift)
    dstart = dstart + dmid_ref[...]
    masked = marks_ref[:, :1] > 0
    add(4, total_rows(jnp.where(masked, dstart, 0.0)))
    dembed = jnp.where(masked, 0.0, dstart).astype(bf16)
    half_ref[...] = dembed
    halves(3 * D // 2, half_ref, D // 2)
    add(5, total_rows(dembed.astype(f32)))


def relative_places(members, y_first):
    count = members.bit_length() - 1
    rels = [sum(((p >> (count - 1 - bit)) & 1) << bit for bit in range(count)) for p in range(members)]
    if y_first:
        return [(rel, side) for side in range(2) for rel in rels]
    return [(rel, None) for rel in rels]


def column_exponents(top):
    return jnp.floor(14.0 - jnp.log(jnp.clip(top, 1e-30, 1e30)) * 1.4426950408889634)


def store_halves(keep_ref, sent_ref, top_ref, table_ref, plain_ref, members, y_first):
    top = jnp.max(jnp.abs(plain_ref[...]), axis=0, keepdims=True)
    top_ref[...] = jnp.broadcast_to(top, top_ref.shape)
    exponent = column_exponents(top)
    factor = jnp.exp2(exponent)
    places = relative_places(members, y_first)
    rows = plain_ref.shape[0] // members
    height = rows // 2 if y_first else rows
    for index, (rel, side) in enumerate(places):
        first = (table_ref[2] ^ rel) * rows
        if y_first:
            first = first + (table_ref[1] ^ side) * height
        block = plain_ref[pl.ds(pl.multiple_of(first, 16), height), :]
        if index < len(places) // 2:
            keep_ref[index * height : (index + 1) * height, :] = block
        else:
            here = (index - len(places) // 2) * height
            sent_ref[here : here + height, :] = block * factor
    half_rows = keep_ref.shape[0]
    sent_ref[half_rows:, :] = jnp.broadcast_to(exponent, (16, exponent.shape[1]))


def weight_grad_kernel(members, y_first, relative, steps_of, *refs):
    table_ref = refs[0]
    sides = refs[1 : 1 + 2 * len(steps_of)]
    b_ref, b_peer_ref = refs[1 + 2 * len(steps_of) : 3 + 2 * len(steps_of)]
    outs, plain_ref = refs[3 + 2 * len(steps_of) : -1], refs[-1]
    step = pl.program_id(0)
    for index, steps in enumerate(steps_of):
        is_side = step == steps[0]
        for other in steps[1:]:
            is_side = is_side | (step == other)

        @pl.when(is_side)
        def _(index=index):
            plain_ref[...] = mm_tn(sides[2 * index][...], b_ref[...]) + mm_tn(
                sides[2 * index + 1][...], b_peer_ref[...]
            )

    if relative:
        store_halves(*outs, table_ref, plain_ref, members, y_first)
    else:
        outs[0][...] = plain_ref[...]


def contract_grad_kernel(members, relative, *refs):
    (table_ref, d_ref, d_peer_ref, h_ref, h_peer_ref) = refs[:5]
    (n_ref, n_peer_ref, b_ref, b_peer_ref) = refs[5:9]
    outs, plain_ref = refs[9:-1], refs[-1]
    step = pl.program_id(0)
    half = D // 2
    shard = D // members

    @pl.when(step < pl.num_programs(0) - 1)
    def _():
        result = mm_tn(d_ref[...], h_ref[...]) + mm_tn(d_peer_ref[...], h_peer_ref[...])
        if relative:
            count = result.shape[1] // (4 * shard)
            for member in range(count):
                here = pl.ds(pl.multiple_of((step * count + member) * shard, 16), shard)
                for part in range(half // shard):
                    plain_ref[here, part * half : (part + 1) * half] = result[
                        part * shard : (part + 1) * shard, member * half : (member + 1) * half
                    ]
        else:
            outs[0][...] = result

    @pl.when(step == pl.num_programs(0) - 1)
    def _():
        result = mm_tn(n_ref[...], b_ref[...]) + mm_tn(n_peer_ref[...], b_peer_ref[...])
        if relative:
            plain_ref[:, 2 * D :] = result
            store_halves(*outs, table_ref, plain_ref, members, True)
        else:
            outs[1][...] = result


def adam_kernel(pick, *refs):
    table_ref, numbers_ref = refs[:2]
    master_ref, first_ref, second_ref = refs[2:5]
    sums, outs = refs[5:-3], refs[-3:]
    grads = pick(pl.program_id(0), table_ref[0], numbers_ref, sums)
    results = adam_update(
        master_ref[...], first_ref[...], second_ref[...], grads, rate_matrix, decay_matrix
    )
    for out_ref, result in zip(outs, results):
        out_ref[...] = result


SQUARE_LANES = tuple((i * D // 2, (i + 1) * D // 2) for i in range(3))


def section(refs, metas, lanes, target, offset=0):
    return [(ref, meta, lanes, target, offset) for ref, meta in zip(refs, metas)]


def blocks_of(group):
    return sum(array.shape[0] for array in group[0])


def whole_spec(shape):
    return pl.BlockSpec(shape, lambda *_: (0,) * len(shape), pipeline_mode=pl.Buffered(1))


def row_spec(block, width):
    return pl.BlockSpec((block, width), lambda i, *_: (i, 0))


COSTS = {'adam_square': 3, 'adam_qkv': 3, 'adam_expand': 3, 'adam_contract': 3, 'attend_teacher': 13, 'attend_student': 0.01, 'teacher_ffn': 0.01, 'student_ffn': 35, 'attend_back': 36, 'grad_expand': 15, 'grad_contract': 13, 'grad_joint': 7, 'grad_embed': 7}
smem_spec = pl.BlockSpec(memory_space=pltpu.SMEM)
any_spec = pl.BlockSpec(memory_space=pl.ANY)


def call(kernel, name, grid, ins, outs, scratch, flops, moved, prefetch=0, aliases={}):
    return pl.pallas_call(
        kernel,
        grid_spec=pltpu.PrefetchScalarGridSpec(
            num_scalar_prefetch=prefetch,
            grid=grid,
            in_specs=[spec for _, spec in ins[prefetch:]],
            out_specs=[spec for _, spec in outs],
            scratch_shapes=scratch,
        ),
        out_shape=[jax.ShapeDtypeStruct(*item) for item, _ in outs],
        input_output_aliases=aliases,
        compiler_params=pltpu.CompilerParams(vmem_limit_bytes=60 << 20),
        cost_estimate=pl.CostEstimate(
            flops=int(COSTS[name] * 1.15e9), transcendentals=0, bytes_accessed=1
        ),
        name=name,
    )(*[item for item, _ in ins])


def attend_teacher(real_rows, pad_rows, images, first, before, x, square, wj, vectors):
    rows, block = x.shape[0], images * pad_rows
    wj, vectors = ((item, whole_spec(item.shape)) for item in (wj, vectors))
    w0, w1 = ((square, pl.BlockSpec((None, D, D), lambda i, *_, at=at: (at, 0, 0))) for at in range(2))
    here = pl.BlockSpec((block, D), lambda i, *_: (first, 0))
    return call(
        functools.partial(attend_teacher_kernel, real_rows, pad_rows),
        "attend_teacher",
        (1,),
        [(x, here), w0, wj, w1, vectors] + ([] if before is None else [(before, any_spec)]),
        [(((rows, D), f32), here)],
        [pltpu.VMEM((block, 3 * D), bf16), pltpu.VMEM((block, D), bf16)],
        14 * rows * D * D,
        20e6,
        aliases={} if before is None else {5: 0},
    )[0]


def attend_student(real_rows, pad_rows, images, table, x, marks, vectors, square, joint):
    rows, block = x.shape[0], images * pad_rows
    arrays, metas = square[0] + joint[0], (square[1], joint[1])
    outs = [(D, f32), (D, f32), (3 * D, bf16), (3 * D, bf16)]
    return call(
        functools.partial(attend_student_kernel, real_rows, pad_rows, *metas),
        "attend_student",
        (rows // block,),
        [
            (table, smem_spec),
            (x, row_spec(block, D)),
            (marks, row_spec(block, 128)),
            (vectors, whole_spec(vectors.shape)),
        ]
        + [(array, any_spec) for array in arrays],
        [(((rows, width), kind), row_spec(block, width)) for width, kind in outs],
        [
            pltpu.VMEM((D, D), bf16),
            pltpu.VMEM((D, D), bf16),
            pltpu.VMEM((D, 3 * D), bf16),
            pltpu.SemaphoreType.DMA((3 * blocks_of(square) + blocks_of(joint),)),
        ],
        14 * rows * D * D,
        25e6,
    )


def teacher_ffn(real_rows, pad_rows, images, mid, weights, biases, vectors, sums):
    rows, block = mid.shape[0], images * pad_rows
    items = [biases, vectors, *weights]
    wholes = [(item, whole_spec(item.shape)) for item in items]
    last = [] if sums is None else [(sums, row_spec(block, D))]
    return call(
        functools.partial(teacher_ffn_kernel, real_rows, pad_rows, sums is not None),
        "teacher_ffn",
        (rows // block,),
        [(mid, row_spec(block, D))] + wholes + last,
        [(((rows, D), f32), row_spec(block, D))],
        [],
        16 * rows * D * D,
        15e6,
    )[0]


def student_ffn(pad_rows, images, table, scale, mid, targets, marks, vectors, expand, contract):
    rows, block = mid.shape[0], images * pad_rows
    outs = [(7 * D // 2, bf16), (7 * D // 2, bf16), (6 * D, bf16), (D, f32)]
    return call(
        functools.partial(student_ffn_kernel, expand[1], contract[1]),
        "student_ffn",
        (rows // block,),
        [
            (table, smem_spec),
            (scale, smem_spec),
            (mid, row_spec(block, D)),
            (targets, row_spec(block, D)),
            (marks, row_spec(block, 128)),
            (vectors, whole_spec(vectors.shape)),
        ]
        + [(array, any_spec) for array in (*expand[0], *contract[0])],
        [(((rows, width), kind), row_spec(block, width)) for width, kind in outs]
        + [(((16, D), f32), whole_spec((16, D)))],
        [
            pltpu.VMEM((D, 4 * D), bf16),
            pltpu.VMEM((4 * D, D), bf16),
            pltpu.VMEM((D, D), bf16),
            pltpu.VMEM((block, 4 * D), f32),
            pltpu.VMEM((block, D), bf16),
            pltpu.SemaphoreType.DMA((2 * blocks_of(expand) + blocks_of(contract),)),
        ],
        36 * rows * D * D,
        40e6,
    )


def attend_back(
    real_rows, pad_rows, images, table, dmid, joint, start, marks, vectors, square, qkv
):
    rows, block = dmid.shape[0], images * pad_rows
    arrays, metas = square[0] + qkv[0], (square[1], qkv[1])
    return call(
        functools.partial(attend_back_kernel, real_rows, pad_rows, *metas),
        "attend_back",
        (rows // block,),
        [
            (table, smem_spec),
            (dmid, row_spec(block, D)),
            (joint, row_spec(block, 3 * D)),
            (start, row_spec(block, D)),
            (marks, row_spec(block, 128)),
            (vectors, whole_spec(vectors.shape)),
        ]
        + [(array, any_spec) for array in arrays],
        [(((rows, 2 * D), bf16), row_spec(block, 2 * D))] * 2
        + [(((16, D), f32), whole_spec((16, D)))],
        [
            pltpu.VMEM((D, D), bf16),
            pltpu.VMEM((D, 3 * D), bf16),
            pltpu.VMEM((block, D), bf16),
            pltpu.VMEM((block, 3 * D), bf16),
            pltpu.VMEM((block, D), bf16),
            pltpu.SemaphoreType.DMA((2 * blocks_of(square) + blocks_of(qkv),)),
        ],
        20 * rows * D * D,
        25e6,
    )


def split_blocks(grads, members, y_first, place, own_y):
    top = jnp.max(jnp.abs(grads), axis=0, keepdims=True)
    rows = grads.shape[0] // members
    rels = jnp.array([rel for rel, _ in relative_places(members, False)])
    blocks = jnp.take(grads.reshape(members, rows, -1), rels ^ place, axis=0)
    if y_first:
        blocks = blocks.reshape(members, 2, rows // 2, -1)
        blocks = jnp.take(blocks, jnp.arange(2) ^ own_y, axis=1).swapaxes(0, 1)
    blocks = blocks.reshape(grads.shape)
    keep, sent = jnp.split(blocks, 2)
    exponent = column_exponents(top)
    tail = jnp.broadcast_to(exponent, (16, exponent.shape[1]))
    return keep, jnp.concatenate([sent * power_of_two(exponent), tail], 0), top


def half_outs(width, columns, index):
    heights = (D // 2, D // 2 + 16, 8)
    return [(((height, columns), f32), pl.BlockSpec((height, width), index)) for height in heights]


def weight_grad(name, table, members, y_first, steps, sides, own_b, peer_b):
    rows = own_b[0].shape[0]
    wide = D // 2
    relative = (D // members) % 32 == 0
    ins = [(table, None)]
    for own, peer, index, _ in sides:
        spec = pl.BlockSpec((rows, D), lambda j, _, index=index: (0, index(j)))
        ins += [(own, spec), (peer, spec)]
    for item, index in (own_b, peer_b):
        ins.append((item, pl.BlockSpec((rows, wide), lambda j, _, index=index: (0, index(j)))))
    if relative:
        outs = half_outs(wide, steps * wide, lambda j, _: (0, j))
    else:
        outs = [(((D, steps * wide), f32), pl.BlockSpec((D, wide), lambda j, _: (0, j)))]
    results = call(
        functools.partial(
            weight_grad_kernel, members, y_first, relative, tuple(side[3] for side in sides)
        ),
        name,
        (steps,),
        ins,
        outs,
        [pltpu.VMEM((D, wide), f32)],
        4 * rows * D * wide * steps,
        4 * D * wide * steps + 4 * rows * (D + wide * steps),
        prefetch=1,
    )
    if relative:
        return results
    return split_blocks(results[0], members, y_first, table[2], table[1])


def contract_grad(table, members, keep, two, two_peer):
    rows = two.shape[0]
    wide = D // 2
    shard = D // members
    relative = shard % 32 == 0
    steps = 4
    column = lambda item, index: (item, pl.BlockSpec((rows, wide), lambda i, _: (0, index)))
    moving = lambda item: (
        item,
        pl.BlockSpec((rows, D), lambda i, _: (0, 1 + jnp.minimum(i, steps - 1))),
    )
    left = pl.BlockSpec((rows, D), lambda i, _: (0, 0))
    if relative:
        assert 4 * shard == wide
        outs = half_outs(5 * wide, 5 * wide, lambda i, _: (0, 0))
        plain = (D, 5 * wide)
    else:
        outs = [
            (((wide, 4 * D), f32), pl.BlockSpec((wide, D), lambda i, _: (0, jnp.minimum(i, steps - 1)))),
            (((D, wide), f32), pl.BlockSpec((D, wide), lambda i, _: (0, 0))),
        ]
        plain = (8, 128)
    results = call(
        functools.partial(contract_grad_kernel, members, relative),
        "grad_contract",
        (steps + 1,),
        [(table, None), column(keep, 5), column(two_peer, 10), moving(two), moving(two_peer)]
        + [(two, left), (two_peer, left), column(keep, 4), column(two_peer, 11)],
        outs,
        [pltpu.VMEM(plain, f32)],
        16 * rows * D * wide,
        16 * D * wide + 16 * rows * D,
        prefetch=1,
    )
    if relative:
        return results
    blocks = results[0].reshape(wide // shard, shard, members, 4 * shard)
    blocks = blocks.transpose(2, 1, 0, 3).reshape(D, -1)
    whole = jnp.concatenate([blocks, results[1]], 1)
    return split_blocks(whole, members, True, table[2], table[1])


def adam(name, pick, table, numbers, masters, block, index, steps, sums):
    spec = pl.BlockSpec(block, lambda j, *_: index(j))
    ins = [(table, smem_spec), (numbers, smem_spec)] + [(item, spec) for item in masters]
    ins += [(item, pl.BlockSpec(shape, lambda j, *_, at=at: at(j))) for item, shape, at in sums]
    size = masters[0].size
    return call(
        functools.partial(adam_kernel, pick),
        name,
        (steps,),
        ins,
        [((masters[0].shape, f32), spec)] * 3,
        [],
        10 * size,
        32 * size,
    )


def after(value, *others):
    return lax.optimization_barrier((value, *others))[0]


def swap(values, bit):
    total = lax.axis_size("batch") * lax.axis_size("mlp")
    return lax.ppermute(values, ("batch", "mlp"), [(i, i ^ bit) for i in range(total)])


def batch_swap(values, bit):
    return swap(values, lax.axis_size("mlp") << bit)


def bit_of(axis, bit):
    return (lax.axis_index(axis) >> bit) & 1


def all_sum(values, bits):
    for bit in bits:
        values = values + swap(values, 1 << bit)
    return values


def pairs_sum(values, bits):
    while bits:
        one, bits = 1 << bits[0], bits[1:]
        if not bits:
            return values + swap(values, one)
        two, bits = 1 << bits[0], bits[1:]
        values = (values + swap(values, one)) + (swap(values, two) + swap(values, one | two))
    return values


def half_of(values, which, axis):
    width = values.shape[axis] // 2
    return lax.dynamic_slice_in_dim(values, which * width, width, axis)


def in_order(first, second, bit_value, axis):
    return jnp.where(
        bit_value == 0,
        jnp.concatenate([first, second], axis),
        jnp.concatenate([second, first], axis),
    )


def natural_rows(blocks, order):
    count = len(order)
    full = blocks.reshape((2,) * count + blocks.shape[1:])
    for place in range(count):
        flip = bit_of("batch", order[count - 1 - place])
        full = jnp.where(flip == 0, full, jnp.flip(full, place))
    source = [count - 1 - order.index(bit) for bit in reversed(range(count))]
    full = full.transpose(source + [count, count + 1])
    return full.reshape(1, -1, full.shape[-1])


def blocks_group(held, last, order, row):
    members = 1 << len(order)
    height = held.shape[1]
    if height % 16 != 0:
        return whole_group(natural_rows(jnp.concatenate([held, last], 0), order), row)
    entries = [
        lax.axis_index("batch") ^ sum(((p >> j) & 1) << bit for j, bit in enumerate(order))
        for p in range(members)
    ]
    arrays = [held, last, swap(held, 1), swap(last, 1)]
    metas = [
        (0, height, height, row + part * (members // 2), near)
        for near in (True, False)
        for part in (0, 1)
    ]
    return (arrays, tuple(metas)), entries


def sides_group(own, peer, other, members, row):
    height = own.shape[0] // members
    own, peer, other = (item.reshape(members, height, -1) for item in (own, peer, other))
    if height % 16 != 0:
        both = in_order(own[:, None], other[:, None], bit_of("mlp", 1), 1)
        return whole_group(both.reshape(1, 2 * members * height, -1), row)[0]
    arrays = [own, other, peer, swap(other, 1)]
    metas = [(side, 2 * height, height, row, near) for near in (True, False) for side in (1, 2)]
    return arrays, tuple(metas)


def whole_group(near, row):
    metas = tuple((0, 0, near.shape[1], row, side) for side in (True, False))
    return ([near, swap(near, 1)], metas), []


def power_of_two(exponent):
    size = jnp.abs(exponent).astype(jnp.int32)
    result = jnp.ones_like(exponent)
    for bit in range(7):
        factor = jnp.where(exponent > 0, 2.0 ** (1 << bit) if bit < 7 else 1.0, 2.0 ** -(1 << bit))
        result = jnp.where((size >> bit) & 1 == 1, result * factor, result)
    return result


def low_half(values):
    return lax.reduce_precision(values, 5, 10).astype(jnp.float16)


def low_half(values):
    return lax.reduce_precision(values, 5, 10).astype(jnp.float16)


def packed(values, exponent):
    tail = jnp.broadcast_to(exponent, (16, exponent.shape[1]))
    return low_half(jnp.concatenate([values * jnp.exp2(exponent), tail], 0))


class Reduction:
    def __init__(self, blocks, order, y_first):
        self.keep, sent, _ = blocks
        self.exponent = sent[-1:]
        self.hops = (["y"] if y_first else []) + list(order) + ["last"]
        self.y_first = y_first
        self.sent = low_half(sent)
        self.other = None

    def fetch(self):
        if self.other is None:
            at_y = self.hops[0] in ("y", "last")
            self.other = swap(self.sent, 2) if at_y else batch_swap(self.sent, self.hops[0])
        return self.other

    def receive(self, *gates):
        other = after(self.fetch(), *gates)
        self.other = None
        bit = self.hops.pop(0)
        rows = other.shape[0] - 16
        exponent = other[-1:].astype(f32)
        if bit == "last":
            own = self.sent[:rows].astype(f32) * power_of_two(-self.sent[-1:].astype(f32))
            other = other[:rows].astype(f32) * power_of_two(-exponent)
            if self.y_first:
                self.sums = in_order(own, other, bit_of("mlp", 1), 0)
            else:
                self.sums = own + other
            return self
        factor = jnp.exp2(-exponent)
        self.exponent = jnp.minimum(self.exponent, exponent) - 1.0
        half = rows // 2 if len(self.hops) > 1 else 0
        sums = self.keep[half:] + other[half:rows].astype(f32) * factor
        self.sent = packed(sums, self.exponent)
        if half:
            self.keep = self.keep[:half] + other[:half].astype(f32) * factor
        return self


def adam_update(master, first, second, gradient, step_rate, weight_decay):
    moment = beta_first * first + (1.0 - beta_first) * gradient
    variance = beta_second * second + (1.0 - beta_second) * gradient * gradient
    corrected = moment / (1.0 - beta_first**STEP)
    scaled = variance / (1.0 - beta_second**STEP)
    updated = master - step_rate * (
        corrected / (jnp.sqrt(scaled) + adam_eps) + weight_decay * master
    )
    return (moment, variance, updated)


def on_device(
    patches,
    mask,
    student_square,
    student_qkv,
    student_expand,
    student_contract,
    student_vectors,
    first_square,
    first_qkv,
    first_expand,
    first_contract,
    first_vectors,
    second_square,
    second_qkv,
    second_expand,
    second_contract,
    second_vectors,
    teacher_square,
    teacher_qkv,
    teacher_expand,
    teacher_contract,
    teacher_vectors,
):
    members = lax.axis_size("batch")
    count = members.bit_length() - 1
    mlp_bits = lax.axis_size("mlp").bit_length() - 1
    near = list(range(count))
    far = near[::-1]
    batch_bits = range(mlp_bits, mlp_bits + count)
    shard_rows = D // members
    core, own_y = bit_of("mlp", 0), bit_of("mlp", 1)
    place = lax.axis_index("batch")
    group, real_rows = mask.shape
    pad_rows = -(-real_rows // 16) * 16
    half = D // 2

    pad = ((0, 0), (0, pad_rows - real_rows))
    x = jnp.pad(patches, pad + ((0, 0),)).reshape(-1, D)
    marks = jnp.pad(mask.astype(f32), pad).reshape(-1)
    wide_marks = jnp.broadcast_to(marks[:, None], (marks.shape[0], 128))

    square_held = jnp.concatenate(
        [half_of(student_square[i], core, 1) for i in range(2)]
        + [lax.dynamic_slice_in_dim(student_qkv, core * 3 * half, half, 1)],
        1,
    ).astype(bf16)[None]
    qkv_held = lax.dynamic_slice_in_dim(student_qkv, core * 3 * half + half, D, 1)
    qkv_held = qkv_held.astype(bf16)[None]
    expand_held = jnp.concatenate(
        [half_of(half_of(item, core, 1), own_y, 0) for item in (student_expand, student_square[2])],
        1,
    )
    expand_own = lax.all_gather(expand_held.astype(bf16), "batch", axis=0, tiled=True)
    contract_near = lax.all_gather(
        half_of(student_contract, core, 1).astype(bf16), "batch", axis=0, tiled=True
    )
    low_vectors = lax.reduce_precision(student_vectors, 8, 7)
    small = lax.dynamic_update_slice(
        jnp.zeros((low_vectors.shape[0], D), f32), low_vectors, (0, place * shard_rows)
    )
    small = jnp.concatenate([small, jnp.full((1, D), jnp.sum(marks))], 0)

    images = min(group, 2)
    sizes = (real_rows, pad_rows, images)
    teacher_weights = (teacher_square, teacher_qkv, teacher_vectors)
    own = lax.axis_index("mlp")
    biases = jnp.concatenate(
        [lax.dynamic_slice_in_dim(teacher_vectors, 8 + (own ^ part), 1, 0) for part in range(4)]
    )
    tmid, runs, tsum, done = None, 0, None, ()
    square_order, qkv_order = far, near[:1] + far[:-1]
    for hop in range(count):
        sends = lax.optimization_barrier((square_held, qkv_held, small, *done))[:3]
        square_held, qkv_held, small = sends
        square_last = batch_swap(square_held, square_order[hop])
        qkv_last = batch_swap(qkv_held, qkv_order[hop])
        small_last = batch_swap(small, near[hop])
        if runs < group // images:
            tmid = attend_teacher(*sizes, runs, tmid, after(x, *sends), *teacher_weights)
            runs += 1
            done = (tmid,)
            if runs == 1:
                teacher_own = jnp.concatenate([after(teacher_expand, tmid), teacher_contract], 1)
                teacher_y = swap(teacher_own, 2)
                teacher_core = swap(teacher_own, 1)
        elif tsum is None:
            tsum = teacher_ffn(
                *sizes,
                after(tmid, *sends, expand_own),
                (teacher_own, teacher_core),
                biases[:2],
                teacher_vectors,
                None,
            )
            done = (tsum,)
        if hop + 1 < count:
            square_held = jnp.concatenate([square_held, square_last], 0)
            qkv_held = jnp.concatenate([qkv_held, qkv_last], 0)
        small = small + after(small_last, *done)
    vectors = small[:-1]
    square_held, qkv_held, square_last, qkv_last = lax.optimization_barrier(
        (square_held, qkv_held, square_last, qkv_last, *done, teacher_y, small)
    )[:4]
    square, square_rows = blocks_group(square_held, square_last, square_order, 3)
    qkv, qkv_rows = blocks_group(qkv_held, qkv_last, qkv_order, 3 + len(square_rows))
    entries = [core, own_y, place] + square_rows + qkv_rows + list(range(members))
    table = jnp.stack([jnp.asarray(entry, jnp.int32) for entry in entries])

    marked = all_sum(after(small, square_last, qkv_last)[-1:, :128], [0])
    teacher_far = swap(after(teacher_y, square_last, qkv_last), 1)
    masked_count = all_sum(marked, range(1, mlp_bits))
    expand_y = swap(after(expand_own, square_last, qkv_last), 2)
    targets = teacher_ffn(
        *sizes,
        after(tmid, marked, expand_own),
        (teacher_y, teacher_far),
        biases[2:],
        teacher_vectors,
        tsum,
    )
    start, mid, joint, act = attend_student(
        *sizes, table, after(x, targets), wide_marks, vectors, square, qkv
    )
    mid, expand_y, expand_peer = lax.optimization_barrier((mid, expand_y, swap(expand_own, 1)))
    masked_count = masked_count[0, 0]
    row = 3 + len(square_rows + qkv_rows)
    expand = sides_group(expand_own, expand_peer, expand_y, members, row)
    contract, _ = whole_group(after(contract_near, mid)[None], 0)
    act_peer = swap(after(act, mid), 1)
    scale = (2.0 / (masked_count * D)).reshape(1)
    keep, one, two, dmid, ffn_sums = student_ffn(
        pad_rows, images, table, scale, mid, targets, wide_marks, vectors, expand, contract
    )
    one_peer = swap(after(one, act_peer), 1)
    two_peer = swap(after(two, one_peer), 1)

    blocks = weight_grad(
        "grad_expand",
        table,
        members,
        False,
        5,
        [
            (one, one_peer, lambda j: 0, (0, 1, 2, 3)),
            (act, act_peer, lambda j: 0, (4,)),
        ],
        (keep, lambda j: jnp.where(j == 4, 6, j)),
        (one_peer, lambda j: jnp.where(j == 4, 6, j + 2)),
    )
    to_expand = Reduction(blocks, near, False)
    blocks = contract_grad(table, members, keep, two, after(two_peer, to_expand.sent))
    to_contract = Reduction(blocks, near, True)
    keep3, send3, att_sums = attend_back(
        *sizes,
        table,
        after(dmid, to_contract.sent),
        joint,
        start,
        wide_marks,
        vectors,
        square,
        qkv,
    )
    send3_peer = swap(send3, 1)
    to_expand.receive(att_sums)
    to_contract.receive()

    total = jnp.concatenate([ffn_sums[:12], att_sums[:6]], 0)
    total_bits = list(range(mlp_bits + count))

    def total_hop(*gates):
        nonlocal total
        if total_bits:
            total = after(total, *gates)
            total = total + swap(total, 1 << total_bits.pop(0))

    total_hop(to_expand.sent, to_contract.sent)
    blocks = weight_grad(
        "grad_joint",
        table,
        members,
        False,
        3,
        [(act, act_peer, lambda j: 1, (0, 1, 2))],
        (keep3, lambda j: j),
        (after(send3_peer, to_expand.sent, to_contract.sent), lambda j: j),
    )
    to_first = Reduction(blocks, near, False)
    to_expand.receive(to_first.sent)
    to_contract.receive(to_first.sent)
    total_hop(to_first.sent)
    blocks = weight_grad(
        "grad_embed",
        table,
        members,
        True,
        1,
        [(act, act_peer, lambda j: 2, (0,))],
        (keep3, lambda j: j + 3),
        (after(send3_peer, to_first.sent, to_expand.sent, to_contract.sent), lambda j: j + 3),
    )
    keep_rows, sent_rows, top = blocks
    sent_rows = after(sent_rows, to_first.fetch())
    to_second = Reduction((keep_rows, sent_rows, top), near, True)
    others = to_expand.fetch(), to_contract.fetch()
    to_first.receive(to_second.sent)
    to_second.receive(*others)
    gates = (to_second.sent, to_first.sent)
    to_contract.receive(*gates)
    to_expand.receive(*gates)
    moving = [to_first, to_contract, to_second, to_expand]
    while moving:
        total_hop(*gates)
        for item in list(moving):
            item.receive(*gates)
            if not item.hops:
                moving.remove(item)
        gates = (moving[0].sent,) if moving else ()
    while total_bits:
        total_hop()
    ffn_total, att_total = total[:12], total[12:]

    own_sums = [item.sums for item in (to_expand, to_contract, to_first, to_second)]
    vector_total = jnp.concatenate(
        [
            att_total[5:6],
            att_total[4:5],
            att_total[2:4],
            att_total[0:2],
            ffn_total[11:12],
            ffn_total[9:11],
            ffn_total[5:9],
            ffn_total[4:5],
            ffn_total[2:4],
            ffn_total[1:2],
        ]
    )
    loss_sum = jnp.sum(ffn_total[0])
    vector_grad = lax.dynamic_slice_in_dim(vector_total, place * shard_rows, shard_rows, 1)
    squares = 0.5 * jnp.sum(vector_grad * vector_grad)
    for member in own_sums:
        squares = squares + jnp.sum(member * member)
    squares = pairs_sum(jnp.full((1, 128), squares), [0, *batch_bits])
    grad_norm = jnp.sqrt(squares[0, 0])
    factor = clip_bound / jnp.maximum(grad_norm, clip_bound)

    pairs = [(item, swap(item, 1)) for item in own_sums]
    numbers = factor.reshape(1)

    def picked(is_own, own_ref, peer_ref):
        return jnp.where(is_own, own_ref[...], peer_ref[...])

    def pick_square(step, core_of, numbers_ref, refs):
        sides = []
        for near in (True, False):
            parts = [refs[2 * i + (0 if near else 1)][...] for i in range(3)]
            side = jnp.where(step == 0, parts[0], jnp.where(step == 1, parts[1], parts[2]))
            sides.append(side)
        left = jnp.where(core_of == 0, sides[0], sides[1])
        right = jnp.where(core_of == 0, sides[1], sides[0])
        return (jnp.concatenate([left, right], 1) * numbers_ref[0])[None]

    def pick_joint(step, core_of, numbers_ref, refs):
        return picked(step == core_of, *refs) * numbers_ref[0]

    def pick_expand(step, core_of, numbers_ref, refs):
        return picked(step == core_of, *refs) * numbers_ref[0]

    def pick_contract(step, core_of, numbers_ref, refs):
        grads = picked(step == core_of, *refs)
        if grads.shape[0] != 4 * shard_rows:
            parts = half // shard_rows
            grads = [grads[:, i * 4 * shard_rows : (i + 1) * 4 * shard_rows] for i in range(parts)]
            grads = jnp.concatenate(grads, 0).T
        return grads * numbers_ref[0]

    def pieces(index, at, width=half):
        return [(item, (shard_rows, width), at) for item in pairs[index]]

    square_results = adam(
        "adam_square",
        pick_square,
        table,
        numbers,
        (student_square, first_square, second_square),
        (1, shard_rows, D),
        lambda j: (j, 0, 0),
        3,
        pieces(3, lambda j: (0, 0)) + pieces(0, lambda j: (0, 4)) + pieces(1, lambda j: (0, 4)),
    )
    qkv_results = adam(
        "adam_qkv",
        pick_joint,
        table,
        numbers,
        (student_qkv, first_qkv, second_qkv),
        (shard_rows, 3 * half),
        lambda j: (0, j),
        2,
        pieces(2, lambda j: (0, 0), 3 * half),
    )
    expand_results = adam(
        "adam_expand",
        pick_expand,
        table,
        numbers,
        (student_expand, first_expand, second_expand),
        (shard_rows, 4 * half),
        lambda j: (0, j),
        2,
        pieces(0, lambda j: (0, 0), 4 * half),
    )
    if 4 * shard_rows == half:
        contract_pieces = pieces(1, lambda j: (0, 0), 4 * half)
    else:
        contract_pieces = []
        for item in pairs[1]:
            item = item[:, : 4 * half].reshape(shard_rows, half // shard_rows, 4 * shard_rows)
            item = item.swapaxes(0, 1).reshape(half, 4 * shard_rows).T
            contract_pieces.append((item, item.shape, lambda j: (0, 0)))
    contract_results = adam(
        "adam_contract",
        pick_contract,
        table,
        numbers,
        (student_contract, first_contract, second_contract),
        (4 * shard_rows, half),
        lambda j: (0, j),
        2,
        contract_pieces,
    )
    vector_results = adam_update(
        student_vectors, first_vectors, second_vectors, vector_grad * factor, rate_vector, 0.0
    )
    return (
        loss_sum,
        masked_count,
        grad_norm,
        *square_results,
        *qkv_results,
        *expand_results,
        *contract_results,
        *vector_results,
    )


def solution(mesh):
    return jax.shard_map(
        on_device,
        mesh=mesh,
        in_specs=(
            P(("batch", "mlp"), None, None),
            P(("batch", "mlp"), None),
            P(None, "batch", None),
            P("batch", None),
            P("batch", None),
            P("batch", None),
            P(None, "batch"),
            P(None, "batch", None),
            P("batch", None),
            P("batch", None),
            P("batch", None),
            P(None, "batch"),
            P(None, "batch", None),
            P("batch", None),
            P("batch", None),
            P("batch", None),
            P(None, "batch"),
            P(),
            P(),
            P(None, "mlp"),
            P("mlp", None),
            P(),
        ),
        out_specs=(
            P(),
            P(),
            P(),
            P(None, "batch", None),
            P(None, "batch", None),
            P(None, "batch", None),
            P("batch", None),
            P("batch", None),
            P("batch", None),
            P("batch", None),
            P("batch", None),
            P("batch", None),
            P("batch", None),
            P("batch", None),
            P("batch", None),
            P(None, "batch"),
            P(None, "batch"),
            P(None, "batch"),
        ),
        check_vma=False,
    )
```
